32 devices in a mesh: lat: 16 (over z, y, x), field: 2 (over core).
Axes of the slice: x: 2, y: 2, z: 4, core: 2. Of those that a mesh axis runs over, the one named last changes fastest.
Arguments:
- precip: float32 [4, 512, 1024], P('field', 'lat'), as said below
Outputs:
- barycenter: float32 [512, 1024], P('lat')
- scaling_logs: float32 [4, 512, 1024], P('field', 'lat')
Inputs may be any that keep to these rules, and one draw needn't show every extreme that they name: `precip`: Nonnegative; each cell is dry (zero) or wet independently of the others.
All inputs are finite; a program needn't handle non-finite values.
Results may differ from the reference program's by a relative error of at most 0.0012.
Values sent between devices are 32-bit elements; how exact they have to be, the bound alone decides.
No kernel may reach another device: no remote copies, remote signals or barrier semaphores. Data moves between devices by JAX's collectives and lax.ppermute only.
A program may use at most 128 MiB of HBM per device.

```python
import jax
import jax.numpy as jnp
from jax import lax

NLAT = 512
DEG = 512
NLON = 1024
FIELD_TOTAL = 4
ITERS = 2


def draw_precip(key, part):
    key_wet, key_amount = jax.random.split(key, 2)
    full_shape = (FIELD_TOTAL, NLAT, NLON)
    wet_cells = jax.random.uniform(key_wet, full_shape) < 0.7
    polar_angle = jnp.pi * (jnp.arange(NLAT, dtype=jnp.float32) + 0.5) / NLAT
    band_factor = 0.3 + 1.7 * jnp.sin(polar_angle) ** 2
    amount = jnp.exp(0.8 * jax.random.normal(key_amount, full_shape))
    return jnp.where(wet_cells, amount * band_factor[None, :, None], 0.0).astype(jnp.float32)


def setup_inputs(seed: int = 0) -> dict:
    seeds = jax.random.split(jax.random.key(seed), 2)
    precip = draw_precip(jax.random.fold_in(seeds[1], 71), 0)
    return {"precip": precip}


heat_rate = 2.0
floor_value = 0.1

def colatitudes(lat_total):
    index_rows = jnp.arange(lat_total, dtype=jnp.float32)
    return jnp.pi * (index_rows + 0.5) / lat_total

def quad_weights(lat_total, lon_total):
    polar_angle = colatitudes(lat_total)
    return jnp.sin(polar_angle) * (jnp.pi / lat_total) * (2.0 * jnp.pi / lon_total)

def heat_factors(degrees):
    level = jnp.arange(degrees, dtype=jnp.float32)
    return jnp.exp(-heat_rate * level * (level + 1.0) / (degrees * (degrees - 1.0)))

def legendre_north(orders, lat_total, degrees):
    half_rows = lat_total // 2
    polar_angle = colatitudes(lat_total)[:half_rows]
    cosine = jnp.cos(polar_angle)
    log_sine = jnp.log(jnp.sin(polar_angle))
    order_value = orders.astype(jnp.float32)
    step_count = jnp.arange(1, degrees + 1, dtype=jnp.float32)
    log_ratios = jnp.log((2.0 * step_count - 1.0) / (2.0 * step_count))
    within = step_count[None, :] <= order_value[:, None]
    partial_log = lax.optimization_barrier(jnp.sum(jnp.where(within, log_ratios[None, :], 0.0), axis=1))
    log_start = 0.5 * jnp.log((2.0 * order_value + 1.0) / (4.0 * jnp.pi)) + 0.5 * partial_log
    start_log = log_start[:, None] + order_value[:, None] * log_sine[None, :]
    span_size = min(32, degrees)

    def advance(state, block_start):
        prev_one, prev_two, log_scale = state
        collected = []
        for offset in range(span_size):
            degree = (block_start + offset).astype(jnp.float32)
            safe_diff = jnp.maximum(degree * degree - order_value * order_value, 1.0)
            first_factor = jnp.sqrt((4.0 * degree * degree - 1.0) / safe_diff)
            numerator = (2.0 * degree + 1.0) * (degree + order_value - 1.0) * (degree - order_value - 1.0)
            denominator = jnp.maximum((2.0 * degree - 3.0) * safe_diff, 1.0)
            second_factor = jnp.sqrt(jnp.maximum(numerator, 0.0) / denominator)
            recurred = first_factor[:, None] * cosine[None, :] * prev_one - second_factor[:, None] * prev_two
            current = jnp.where((degree > order_value)[:, None], recurred, jnp.where((degree == order_value)[:, None], jnp.ones_like(recurred), jnp.zeros_like(recurred)))
            collected.append(current * jnp.exp(log_scale))
            prev_two = prev_one
            prev_one = current
            if (offset + 1) % 8 == 0:
                magnitude = jnp.maximum(jnp.abs(prev_one), jnp.abs(prev_two))
                safe_size = jnp.where(magnitude > 0.0, magnitude, jnp.ones_like(magnitude))
                prev_one = prev_one / safe_size
                prev_two = prev_two / safe_size
                log_scale = log_scale + jnp.log(safe_size)
        return ((prev_one, prev_two, log_scale), jnp.stack(collected))
    empty_state = jnp.zeros((orders.shape[0], half_rows), jnp.float32)
    block_starts = jnp.arange(0, degrees, span_size, dtype=jnp.int32)
    final_state, stacked = lax.scan(advance, (empty_state, empty_state, start_log), block_starts)
    legendre = stacked.reshape(degrees, orders.shape[0], half_rows)
    return jnp.transpose(legendre, (1, 2, 0))

def mirror_table(north_table, orders):
    degrees = north_table.shape[2]
    level = jnp.arange(degrees, dtype=jnp.int32)
    parity_sign = jnp.where((level[None, :] + orders[:, None]) % 2 == 0, 1.0, -1.0)
    south_table = jnp.flip(north_table, axis=1) * parity_sign[:, None, :]
    return jnp.concatenate([north_table, south_table], axis=1)

def fourier_tables(lon_total, degrees, groups):
    per_group = degrees // groups
    column = jnp.arange(2 * degrees, dtype=jnp.int32)
    group_index = column // (2 * per_group)
    within_group = column % (2 * per_group)
    part_index = within_group // per_group
    order_index = group_index * per_group + within_group % per_group
    points = jnp.arange(lon_total, dtype=jnp.int32)
    phase = (points[:, None] * order_index[None, :] % lon_total).astype(jnp.float32) * (2.0 * jnp.pi / lon_total)
    forward = jnp.where(part_index[None, :] == 0, jnp.cos(phase), -jnp.sin(phase))
    doubled = jnp.where(order_index == 0, 1.0, 2.0)
    backward = jnp.transpose(forward) * doubled[:, None]
    return (forward, backward)

def kernel_apply_step(fields):
    count_fields = fields.shape[0]
    forward, backward = fourier_tables(NLON, DEG, 1)
    weights = quad_weights(NLAT, NLON)
    heat_factor = heat_factors(DEG)
    spectra = jnp.einsum('fjk,kc->fjc', fields, forward, precision=lax.Precision.HIGHEST)
    span_size = min(32, DEG)
    block_count = DEG // span_size
    spectra = spectra.reshape(count_fields, NLAT, 2, block_count, span_size)
    split_blocks = jnp.transpose(spectra, (3, 0, 1, 2, 4))

    def one_block(packed):
        piece, block_index = packed
        orders = block_index * span_size + jnp.arange(span_size, dtype=jnp.int32)
        full_table = mirror_table(legendre_north(orders, NLAT, DEG), orders)
        weighted = piece * weights[None, :, None, None]
        coefficients = jnp.einsum('mjl,fjpm->mfpl', full_table, weighted, precision=lax.Precision.HIGHEST)
        coefficients = coefficients * heat_factor[None, None, None, :]
        return jnp.einsum('mjl,mfpl->fjpm', full_table, coefficients, precision=lax.Precision.HIGHEST)
    filtered = lax.map(one_block, (split_blocks, jnp.arange(block_count, dtype=jnp.int32)))
    filtered = jnp.transpose(filtered, (1, 2, 3, 0, 4)).reshape(count_fields, NLAT, 2 * DEG)
    return jnp.einsum('fjc,ck->fjk', filtered, backward, precision=lax.Precision.HIGHEST)

def reference(precip):
    weights = quad_weights(NLAT, NLON)
    masses = lax.optimization_barrier(jnp.sum(precip * weights[None, :, None], axis=(1, 2))) / (4.0 * jnp.pi)
    scaled = precip / masses[:, None, None]
    ratio_field = scaled
    scaling_logs = jnp.zeros(precip.shape, jnp.float32)
    log_barycenter = jnp.zeros(precip.shape[1:], jnp.float32)
    for sweep in range(ITERS):
        smoothed = kernel_apply_step(ratio_field)
        clamped_values = jnp.log(jnp.maximum(smoothed, floor_value))
        log_barycenter = lax.optimization_barrier(jnp.sum(scaling_logs + clamped_values, axis=0)) / FIELD_TOTAL
        scaling_logs = log_barycenter[None] - clamped_values
        if sweep + 1 < ITERS:
            blurred_scale = kernel_apply_step(jnp.exp(scaling_logs))
            ratio_field = scaled / jnp.maximum(blurred_scale, floor_value)
    return (jnp.exp(log_barycenter), scaling_logs)
```

```python
import math

import jax
import jax.numpy as jnp
import ml_dtypes
import numpy as np
from jax import lax
from jax.experimental import pallas as pl
from jax.experimental.pallas import tpu as pltpu
from jax.sharding import PartitionSpec as P

ITERS = 2


heat_rate = 2.0
floor_value = 0.1


def colatitudes(lat_total):
    index_rows = jnp.arange(lat_total, dtype=jnp.float32)
    return jnp.pi * (index_rows + 0.5) / lat_total


def quad_weights(lat_total, lon_total):
    polar_angle = colatitudes(lat_total)
    return jnp.sin(polar_angle) * (jnp.pi / lat_total) * (2.0 * jnp.pi / lon_total)


def heat_factors(degrees):
    level = jnp.arange(degrees, dtype=jnp.float32)
    return jnp.exp(-heat_rate * level * (level + 1.0) / (degrees * (degrees - 1.0)))


def legendre_north(orders, lat_total, degrees):
    half_rows = lat_total // 2
    polar_angle = colatitudes(lat_total)[:half_rows]
    cosine = jnp.cos(polar_angle)
    log_sine = jnp.log(jnp.sin(polar_angle))
    order_value = orders.astype(jnp.float32)
    step_count = jnp.arange(1, degrees + 1, dtype=jnp.float32)
    log_ratios = jnp.log((2.0 * step_count - 1.0) / (2.0 * step_count))
    within = step_count[None, :] <= order_value[:, None]
    partial_log = jnp.sum(jnp.where(within, log_ratios[None, :], 0.0), axis=1)
    log_start = 0.5 * jnp.log((2.0 * order_value + 1.0) / (4.0 * jnp.pi)) + 0.5 * partial_log
    start_log = log_start[:, None] + order_value[:, None] * log_sine[None, :]
    span_size = min(32, degrees)

    def advance(state, block_start):
        prev_one, prev_two, log_scale = state
        collected = []
        for offset in range(span_size):
            degree = (block_start + offset).astype(jnp.float32)
            safe_diff = jnp.maximum(degree * degree - order_value * order_value, 1.0)
            first_factor = jnp.sqrt((4.0 * degree * degree - 1.0) / safe_diff)
            numerator = (
                (2.0 * degree + 1.0) * (degree + order_value - 1.0) * (degree - order_value - 1.0)
            )
            denominator = jnp.maximum((2.0 * degree - 3.0) * safe_diff, 1.0)
            second_factor = jnp.sqrt(jnp.maximum(numerator, 0.0) / denominator)
            recurred = (
                first_factor[:, None] * cosine[None, :] * prev_one
                - second_factor[:, None] * prev_two
            )
            current = jnp.where(
                (degree > order_value)[:, None],
                recurred,
                jnp.where(
                    (degree == order_value)[:, None],
                    jnp.ones_like(recurred),
                    jnp.zeros_like(recurred),
                ),
            )
            collected.append(current * jnp.exp(log_scale))
            prev_two = prev_one
            prev_one = current
            if (offset + 1) % 8 == 0:
                magnitude = jnp.maximum(jnp.abs(prev_one), jnp.abs(prev_two))
                safe_size = jnp.where(magnitude > 0.0, magnitude, jnp.ones_like(magnitude))
                prev_one = prev_one / safe_size
                prev_two = prev_two / safe_size
                log_scale = log_scale + jnp.log(safe_size)
        return ((prev_one, prev_two, log_scale), jnp.stack(collected))

    empty_state = jnp.zeros((orders.shape[0], half_rows), jnp.float32)
    block_starts = jnp.arange(0, degrees, span_size, dtype=jnp.int32)
    final_state, stacked = lax.scan(advance, (empty_state, empty_state, start_log), block_starts)
    legendre = stacked.reshape(degrees, orders.shape[0], half_rows)
    return jnp.transpose(legendre, (1, 2, 0))


def fourier_tables(lon_total, degrees, groups):
    per_group = degrees // groups
    column = jnp.arange(2 * degrees, dtype=jnp.int32)
    group_index = column // (2 * per_group)
    within_group = column % (2 * per_group)
    part_index = within_group // per_group
    order_index = group_index * per_group + within_group % per_group
    points = jnp.arange(lon_total, dtype=jnp.int32)
    phase = (points[:, None] * order_index[None, :] % lon_total).astype(jnp.float32) * (
        2.0 * jnp.pi / lon_total
    )
    forward = jnp.where(part_index[None, :] == 0, jnp.cos(phase), -jnp.sin(phase))
    doubled = jnp.where(order_index == 0, 1.0, 2.0)
    backward = jnp.transpose(forward) * doubled[:, None]
    return (forward, backward)


def on_device_plain(precip):
    groups = lax.axis_size("lat")
    lat_index = lax.axis_index("lat")
    local_fields, lat_rows, lon_total = precip.shape
    lat_total = lat_rows * groups
    degrees = lon_total // 2
    orders_here = degrees // groups
    half_rows = lat_total // 2
    count_fields = local_fields * lax.axis_size("field")
    weights_all = quad_weights(lat_total, lon_total)
    local_weights = lax.dynamic_slice_in_dim(weights_all, lat_index * lat_rows, lat_rows)
    forward, backward = fourier_tables(lon_total, degrees, groups)
    heat_factor = heat_factors(degrees)
    orders = lat_index * orders_here + jnp.arange(orders_here, dtype=jnp.int32)
    north_table = legendre_north(orders, lat_total, degrees)
    paired = north_table.reshape(orders_here, half_rows, degrees // 2, 2)
    parity = (orders % 2 == 0)[:, None, None]
    even_table = jnp.where(parity, paired[..., 0], paired[..., 1])
    odd_table = jnp.where(parity, paired[..., 1], paired[..., 0])
    heat_paired = heat_factor.reshape(degrees // 2, 2)
    heat_even = jnp.where(parity[:, :, 0], heat_paired[None, :, 0], heat_paired[None, :, 1])
    heat_odd = jnp.where(parity[:, :, 0], heat_paired[None, :, 1], heat_paired[None, :, 0])
    weights_north = weights_all[:half_rows]

    def legendre_pass(spread):
        count_here = spread.shape[0]
        shaped = spread.reshape(count_here, lat_total, 2, orders_here)
        north_part = shaped[:, :half_rows]
        south_part = jnp.flip(shaped[:, half_rows:], axis=1)
        even_input = (north_part + south_part) * weights_north[None, :, None, None]
        odd_input = (north_part - south_part) * weights_north[None, :, None, None]
        even_coef = jnp.einsum(
            "mjk,fjpm->mfpk", even_table, even_input, precision=lax.Precision.HIGHEST
        )
        odd_coef = jnp.einsum(
            "mjk,fjpm->mfpk", odd_table, odd_input, precision=lax.Precision.HIGHEST
        )
        even_coef = even_coef * heat_even[:, None, None, :]
        odd_coef = odd_coef * heat_odd[:, None, None, :]
        even_sum = jnp.einsum(
            "mjk,mfpk->fjpm", even_table, even_coef, precision=lax.Precision.HIGHEST
        )
        odd_sum = jnp.einsum("mjk,mfpk->fjpm", odd_table, odd_coef, precision=lax.Precision.HIGHEST)
        result = jnp.concatenate([even_sum + odd_sum, jnp.flip(even_sum - odd_sum, axis=1)], axis=1)
        return result.reshape(count_here, lat_total, 2 * orders_here)

    def kernel_apply_step(fields):
        spectra = jnp.einsum("fjk,kc->fjc", fields, forward, precision=lax.Precision.HIGHEST)

        def one_member(carry, member_spectra):
            spread = lax.all_to_all(member_spectra, "lat", split_axis=1, concat_axis=0, tiled=True)
            filtered = legendre_pass(spread[None])
            returned = lax.all_to_all(filtered[0], "lat", split_axis=0, concat_axis=1, tiled=True)
            return (carry, returned)

        unused, gathered = lax.scan(one_member, jnp.zeros((), jnp.float32), spectra)
        return jnp.einsum("fjc,ck->fjk", gathered, backward, precision=lax.Precision.HIGHEST)

    partial_value = jnp.sum(precip * local_weights[None, :, None], axis=(1, 2))
    masses = lax.psum(partial_value, "lat") / (4.0 * jnp.pi)
    scaling_logs = jnp.zeros(precip.shape, jnp.float32)
    log_barycenter = jnp.zeros(precip.shape[1:], jnp.float32)
    scaled = precip / masses[:, None, None]
    ratio_field = scaled
    for sweep in range(ITERS):
        smoothed = kernel_apply_step(ratio_field)
        clamped_values = jnp.log(jnp.maximum(smoothed, floor_value))
        added_total = lax.psum(jnp.sum(scaling_logs + clamped_values, axis=0), "field")
        log_barycenter = added_total / count_fields
        scaling_logs = log_barycenter[None] - clamped_values
        if sweep + 1 < ITERS:
            blurred_scale = kernel_apply_step(jnp.exp(scaling_logs))
            ratio_field = scaled / jnp.maximum(blurred_scale, floor_value)
    return (jnp.exp(log_barycenter), scaling_logs)


QUART = 4


def split_pair(value):
    high = value.astype(jnp.bfloat16)
    low = (value - high.astype(jnp.float32)).astype(jnp.bfloat16)
    return high, low


def pair_rows(value):
    high, low = split_pair(value)
    return jnp.concatenate([high, low], axis=0)


def dot_nt(left, right):
    return lax.dot_general(left, right, (((1,), (1,)), ((), ())), preferred_element_type=jnp.float32)


def dot_nn(left, right):
    return lax.dot_general(left, right, (((1,), (0,)), ((), ())), preferred_element_type=jnp.float32)


def wave_tables(lon_total, devices, slots):
    span = lon_total // QUART
    residue = np.arange(QUART)[:, None, None]
    order = residue + QUART * np.arange(devices // QUART)[None, :, None]
    order = (order + devices * np.arange(slots)[None, None, :]).reshape(QUART, -1)
    phase = (order[:, :, None] * np.arange(span)[None, None, :] % lon_total) * (2.0 * np.pi / lon_total)
    table = np.concatenate([np.cos(phase), np.sin(phase)], axis=1).astype(np.float32)
    high = table.astype(ml_dtypes.bfloat16)
    low = (table - high.astype(np.float32)).astype(ml_dtypes.bfloat16)
    return high, low


def forward_waves(field, high_ref, low_ref, out_ref):
    span = field.shape[1] // QUART
    rows = field.shape[0]
    lanes = 2 * rows
    part = [field[:, q * span : (q + 1) * span] for q in range(QUART)]
    sum_even, sum_odd = part[0] + part[2], part[1] + part[3]
    diff_even, diff_odd = part[0] - part[2], part[1] - part[3]
    stack_even = pair_rows(jnp.concatenate([sum_even + sum_odd, sum_even - sum_odd], axis=0))
    stack_odd = pair_rows(jnp.concatenate([diff_even, diff_odd], axis=0))
    orders = high_ref.shape[1] // 2
    first = lax.broadcasted_iota(jnp.int32, (orders, lanes), 1) < rows
    for residue in range(QUART):
        stack = stack_odd if residue % 2 else stack_even
        found = dot_nt(high_ref[residue], stack) + dot_nt(low_ref[residue], stack)
        found = found[:, :lanes] + found[:, lanes:]
        cosine, sine = found[:orders], found[orders:]
        if residue == 0:
            packed = jnp.where(first, cosine, -pltpu.roll(sine, rows, 1))
        elif residue == 2:
            packed = jnp.where(first, pltpu.roll(cosine, rows, 1), -sine)
        elif residue == 1:
            packed = jnp.where(first, cosine, -cosine) - pltpu.roll(sine, rows, 1)
        else:
            turned = pltpu.roll(sine, rows, 1)
            packed = cosine + jnp.where(first, turned, -turned)
        out_ref[:, residue] = packed.reshape(out_ref.shape[0], out_ref.shape[2], lanes)


def inverse_waves(spec_ref, high_ref, low_ref):
    outer, _, slots, lanes = spec_ref.shape
    rows = lanes // 2
    real = [None] * QUART
    cross = {}
    spare = None
    for residue in range(QUART):
        turned = jnp.transpose(spec_ref[:, residue].reshape(outer * slots, lanes))
        cosine, sine = turned[:rows], turned[rows:]
        if residue == 0:
            spare = sine[:, 0:1]
        left = jnp.concatenate([cosine, -sine], axis=1)
        if residue % 2:
            left = jnp.concatenate([left, jnp.concatenate([sine, cosine], axis=1)], axis=0)
        count = left.shape[0]
        left = pair_rows(left)
        found = dot_nn(left, high_ref[residue]) + dot_nn(left, low_ref[residue])
        found = found[:count] + found[count:]
        real[residue] = found[:rows]
        if residue % 2:
            cross[residue] = found[rows:]
    plus, minus = real[0] + real[2], real[0] - real[2]
    both, gap = real[1] + real[3], cross[1] - cross[3]
    return jnp.concatenate([plus + both, minus - gap, plus - both, minus + gap], axis=1), spare


def copy_flipped(src_ref, dst_ref, south, lat_rows):
    rows = src_ref.shape[0]
    for row in range(rows):
        base, offset = row - row % lat_rows, row % lat_rows
        target = base + jnp.where(south, lat_rows - 1 - offset, offset)
        dst_ref[pl.ds(target, 1), :] = src_ref[row : row + 1, :]


def first_body(lat_rows, dev_ref, field_ref, high_ref, low_ref, flipped_ref, out_ref):
    copy_flipped(field_ref, flipped_ref, dev_ref[1] > 0, lat_rows)
    forward_waves(flipped_ref[...], high_ref, low_ref, out_ref)


def member_sum(value, lat_rows):
    total = value[:lat_rows]
    for member in range(1, value.shape[0] // lat_rows):
        total = total + value[member * lat_rows : (member + 1) * lat_rows]
    return total


def mass_body(lat_rows, spec_ref, field_ref, high_ref, low_ref, clamp_ref, sum_ref, scaled_ref):
    blurred, total = inverse_waves(spec_ref, high_ref, low_ref)
    inverse = (4.0 * math.pi) / total
    scaled_ref[...] = field_ref[...] * inverse
    clamped = jnp.log(jnp.maximum(blurred * inverse, floor_value))
    clamp_ref[...] = clamped
    sum_ref[...] = member_sum(clamped, lat_rows)


def center_body(count, lat_rows, clamp_ref, sum_ref, other_ref, high_ref, low_ref, logs_ref, out_ref):
    center = (sum_ref[...] + other_ref[...]) / count
    members = clamp_ref.shape[0] // lat_rows
    logs = jnp.concatenate([center] * members, axis=0) - clamp_ref[...]
    logs_ref[...] = logs
    forward_waves(jnp.exp(logs), high_ref, low_ref, out_ref)


def ratio_body(spec_ref, scaled_ref, high_ref, low_ref, out_ref):
    blurred, _ = inverse_waves(spec_ref, high_ref, low_ref)
    forward_waves(scaled_ref[...] / jnp.maximum(blurred, floor_value), high_ref, low_ref, out_ref)


def last_body(lat_rows, dev_ref, spec_ref, logs_ref, high_ref, low_ref, clamp_ref, sum_ref, clamp_tmp, sum_tmp):
    blurred, _ = inverse_waves(spec_ref, high_ref, low_ref)
    clamped = jnp.log(jnp.maximum(blurred, floor_value))
    clamp_tmp[...] = clamped
    sum_tmp[...] = member_sum(logs_ref[...] + clamped, lat_rows)
    copy_flipped(clamp_tmp, clamp_ref, dev_ref[1] > 0, lat_rows)
    copy_flipped(sum_tmp, sum_ref, dev_ref[1] > 0, lat_rows)


def table_rows(degrees, devices, slot):
    return (degrees - devices * slot) // 2


def table_offset(degrees, devices, slot, parity):
    start = sum(2 * table_rows(degrees, devices, s) for s in range(slot))
    return start + parity * table_rows(degrees, devices, slot)


def legendre_body(degrees, devices, slots, dev_ref, place_ref, start_ref, high_ref, low_ref,
                  first_coef, second_coef, left_half, right_half):
    half = (left_half, right_half)
    lanes = 128
    device = dev_ref[0]
    order = lax.broadcasted_iota(jnp.int32, (slots, degrees), 0) * devices + device
    level = lax.broadcasted_iota(jnp.int32, (slots, degrees), 1)
    above = level > order
    order, level = order.astype(jnp.float32), level.astype(jnp.float32)
    diff = jnp.maximum(level * level - order * order, 1.0)
    first_coef[...] = jnp.where(above, jnp.sqrt((4.0 * level * level - 1.0) / diff), 0.0)
    numer = (2.0 * level + 1.0) * (level + order - 1.0) * (level - order - 1.0)
    denom = jnp.maximum((2.0 * level - 3.0) * diff, 1.0)
    second_coef[...] = jnp.where(above, jnp.sqrt(jnp.maximum(numer, 0.0) / denom), 0.0)

    lane = lax.broadcasted_iota(jnp.int32, (slots, lanes), 1)
    start = jnp.sum(jnp.where(lane == device, start_ref[...], 0.0), axis=1, keepdims=True)
    sub = lax.broadcasted_iota(jnp.int32, (8, lanes), 0)
    tiles = slots // 8
    cosine = [jnp.broadcast_to(place_ref[0:1, h * lanes : (h + 1) * lanes], (8, lanes)) for h in range(2)]
    log_sine = [jnp.broadcast_to(place_ref[1:2, h * lanes : (h + 1) * lanes], (8, lanes)) for h in range(2)]
    order_tile = [(sub + 8 * t) * devices + device for t in range(tiles)]
    zero = jnp.zeros((8, lanes), jnp.float32)
    span_log = 60.0 * math.log(2.0)

    def fresh(tile):
        state = []
        for h in range(2):
            scale_log = start[8 * tile : 8 * tile + 8] + order_tile[tile].astype(jnp.float32) * log_sine[h]
            state.append((zero, zero, scale_log, jnp.exp(scale_log)))
        return state

    def chunk(index, states):
        active = len(states)
        base = pl.multiple_of(index * lanes, lanes)
        first = [first_coef[8 * t : 8 * t + 8, pl.ds(base, lanes)] for t in range(active)]
        second = [second_coef[8 * t : 8 * t + 8, pl.ds(base, lanes)] for t in range(active)]
        states = [list(s) for s in states]
        for k in range(lanes):
            degree = base + k
            for t in range(active):
                a = jnp.broadcast_to(first[t][:, k : k + 1], (8, lanes))
                b = jnp.broadcast_to(second[t][:, k : k + 1], (8, lanes))
                begin = jnp.where(order_tile[t] == degree, 1.0, 0.0)
                for h in range(2):
                    one, two, scale_log, scale = states[t][h]
                    now = (a * cosine[h]) * one + (begin - b * two)
                    half[h][pl.ds(degree * slots + 8 * t, 8), :] = now * scale
                    two, one = one, now
                    if (k + 1) % 8 == 0:
                        large = jnp.maximum(jnp.abs(one), jnp.abs(two)) > 2.0**30
                        factor = jnp.where(large, 2.0**-60, 1.0)
                        one, two = one * factor, two * factor
                        scale_log = scale_log + jnp.where(large, span_log, 0.0)
                        scale = jnp.exp(scale_log)
                    states[t][h] = (one, two, scale_log, scale)
        return states

    states = []
    chunks = degrees // lanes
    for index in range(chunks):
        while len(states) < tiles and 8 * len(states) * devices < (index + 1) * lanes:
            states.append(fresh(len(states)))
        states = chunk(index, states)

    for slot in range(slots):
        count = table_rows(degrees, devices, slot)
        for parity in range(2):
            offset = table_offset(degrees, devices, slot, parity)
            begin = (devices * slot + parity) * slots + slot
            for h in range(2):
                high, low = split_pair(half[h][pl.ds(begin, count, stride=2 * slots), :])
                high_ref[offset : offset + count, h * lanes : (h + 1) * lanes] = high
                low_ref[offset : offset + count, h * lanes : (h + 1) * lanes] = low


def sphere_body(degrees, devices, slots, lat_groups, lat_rows, members, with_mass, dev_ref, spec_ref, high_ref,
                low_ref, weight_ref, heat_ref, out_ref, even_in0, even_in1, odd_in0, odd_in1,
                north0, north1, south0, south1):
    device = dev_ref[0]
    sign = jnp.where(device % 2 == 0, 1.0, -1.0)
    fields = devices // lat_groups
    half_groups = lat_groups // 2
    per_field = 2 * members
    columns = fields * per_field
    group_lanes = 128 // lat_rows
    for field in range(fields):
        for h in range(2):
            even, odd = [], []
            for q in range(group_lanes):
                lat = h * group_lanes + q
                north = spec_ref[lat * fields + field]
                south = spec_ref[(lat_groups - 1 - lat) * fields + field] * sign
                even.append(north + south)
                odd.append(north - south)
            for c in range(per_field):
                row = (field * per_field + c) * slots
                cut = slice(c * lat_rows, (c + 1) * lat_rows)
                (even_in0, even_in1)[h][row : row + slots, :] = jnp.concatenate([e[:, cut] for e in even], axis=1)
                (odd_in0, odd_in1)[h][row : row + slots, :] = jnp.concatenate([o[:, cut] for o in odd], axis=1)

    for slot in range(slots):
        picked = pl.ds(slot, columns, stride=slots)
        gain = 2.0 if slot else jnp.where(device == 0, 1.0, 2.0)
        weights = weight_ref[...] * gain
        found = []
        for parity, pair in enumerate(((even_in0, even_in1), (odd_in0, odd_in1))):
            values = jnp.concatenate([pair[0][picked, :], pair[1][picked, :]], axis=1) * weights
            if with_mass and slot == 0 and parity == 0:
                mass = jnp.sum(values, axis=1, keepdims=True)
            count = table_rows(degrees, devices, slot)
            offset = table_offset(degrees, devices, slot, parity)
            high, low = high_ref[offset : offset + count, :], low_ref[offset : offset + count, :]
            packed = pair_rows(values)
            coef = dot_nt(packed, high) + dot_nt(packed, low)
            level = degrees // 2 - count
            coef = (coef[:columns] + coef[columns:]) * heat_ref[parity : parity + 1, level:]
            packed = pair_rows(coef)
            back = dot_nn(packed, high) + dot_nn(packed, low)
            found.append(back[:columns] + back[columns:])
        north, south = found[0] + found[1], (found[0] - found[1]) * sign
        if with_mass and slot == 0:
            spread = jnp.broadcast_to(mass, north.shape)
            spread = pltpu.roll(spread, members, 0)
            which = lax.broadcasted_iota(jnp.int32, north.shape, 0) % per_field
            spare = (which >= members) & (device == 0)
            north, south = jnp.where(spare, spread, north), jnp.where(spare, spread, south)
        north0[picked, :], north1[picked, :] = north[:, :128], north[:, 128:]
        south0[picked, :], south1[picked, :] = south[:, :128], south[:, 128:]

    for field in range(fields):
        for lat in range(half_groups):
            h, q = lat // group_lanes, lat % group_lanes
            cut = slice(q * lat_rows, (q + 1) * lat_rows)
            rows = [(field * per_field + c) * slots for c in range(per_field)]
            north = [(north0, north1)[h][row : row + slots, cut] for row in rows]
            south = [(south0, south1)[h][row : row + slots, cut] for row in rows]
            out_ref[lat * fields + field] = jnp.concatenate(north, axis=1)
            out_ref[(lat_groups - 1 - lat) * fields + field] = jnp.concatenate(south, axis=1)


def on_device_packed(precip):
    lat_groups, fields = lax.axis_size("lat"), lax.axis_size("field")
    devices = lat_groups * fields
    members, lat_rows, lon_total = precip.shape
    lat_total, degrees = lat_rows * lat_groups, lon_total // 2
    slots = degrees // devices
    rows = members * lat_rows
    lat_index = lax.axis_index("lat")
    device = lat_index * fields + lax.axis_index("field")
    south = (lat_index >= lat_groups // 2).astype(jnp.int32)
    dev = jnp.stack([device.astype(jnp.int32), south])

    polar = np.pi * (np.arange(lat_total // 2) + 0.5) / lat_total
    weights = (np.sin(polar) * (np.pi / lat_total) * (2.0 * np.pi / lon_total)).astype(np.float32)[None]
    place = np.stack([np.cos(polar), np.log(np.sin(polar))]).astype(np.float32)
    level = np.arange(degrees)
    heat = np.exp(-heat_rate * level * (level + 1.0) / (degrees * (degrees - 1.0)))
    heat = heat.reshape(degrees // 2, 2).T.astype(np.float32)
    step = np.arange(1, degrees)
    starts = np.concatenate([[0.0], np.cumsum(np.log((2.0 * step - 1.0) / (2.0 * step)))])
    starts = 0.5 * np.log((2.0 * level + 1.0) / (4.0 * np.pi)) + 0.5 * starts
    starts = np.pad(starts.reshape(slots, devices), ((0, 0), (0, 128 - devices))).astype(np.float32)
    wave_high, wave_low = (jnp.asarray(t) for t in wave_tables(lon_total, devices, slots))

    vmem = pl.BlockSpec(memory_space=pltpu.VMEM)
    smem = pl.BlockSpec(memory_space=pltpu.SMEM)
    outer = devices // QUART
    spec_shape = jax.ShapeDtypeStruct((outer, QUART, slots, 2 * rows), jnp.float32)
    grid_shape = jax.ShapeDtypeStruct((rows, lon_total), jnp.float32)
    sum_shape = jax.ShapeDtypeStruct((lat_rows, lon_total), jnp.float32)
    table_total = table_offset(degrees, devices, slots, 0)
    table_shape = jax.ShapeDtypeStruct((table_total, lat_total // 2), jnp.bfloat16)

    def call(body, shapes, *operands, scratch=(), cost=None, name=None):
        return pl.pallas_call(
            body,
            out_shape=shapes,
            in_specs=[smem if o is dev else vmem for o in operands],
            out_specs=jax.tree.map(lambda _: vmem, shapes),
            scratch_shapes=list(scratch),
            cost_estimate=cost,
            compiler_params=pltpu.CompilerParams(vmem_limit_bytes=48 << 20),
            name=name,
        )(*operands)

    def exchange(spec):
        flat = spec.reshape(devices, slots, 2 * rows)
        return lax.all_to_all(flat, ("lat", "field"), split_axis=0, concat_axis=0, tiled=True)

    def swap(value):
        return lax.ppermute(value, "field", [(0, 1), (1, 0)])

    scratch128 = lambda count: pltpu.VMEM((count, 128), jnp.float32)

    def sphere(spec, with_mass):
        columns = fields * 2 * members

        def body(*refs):
            sphere_body(degrees, devices, slots, lat_groups, lat_rows, members, with_mass, *refs)

        shape = jax.ShapeDtypeStruct((devices, slots, 2 * rows), jnp.float32)
        done = call(
            body, shape, dev, exchange(spec), table_high, table_low, jnp.asarray(weights), jnp.asarray(heat),
            scratch=[scratch128(columns * slots)] * 8, name="sphere",
        )
        return exchange(done).reshape(spec_shape.shape)

    def bind(body, *fixed):
        return lambda *refs: body(*fixed, *refs)

    table_high, table_low = call(
        bind(legendre_body, degrees, devices, slots), (table_shape, table_shape), dev, jnp.asarray(place),
        jnp.asarray(starts),
        scratch=[pltpu.VMEM((slots, degrees), jnp.float32)] * 2 + [scratch128(degrees * slots)] * 2,
        cost=pl.CostEstimate(flops=40_000_000, bytes_accessed=16 << 20, transcendentals=0), name="legendre",
    )
    flipped, spec = call(
        bind(first_body, lat_rows), (grid_shape, spec_shape), dev, precip.reshape(rows, lon_total),
        wave_high, wave_low, name="first",
    )
    clamped, total, scaled = call(
        bind(mass_body, lat_rows), (grid_shape, sum_shape, grid_shape), sphere(spec, True), flipped,
        wave_high, wave_low, name="mass",
    )
    count = float(members * fields)
    logs, spec = call(
        bind(center_body, count, lat_rows), (grid_shape, spec_shape), clamped, total, swap(total),
        wave_high, wave_low, name="center",
    )
    spec = call(ratio_body, spec_shape, sphere(spec, False), scaled, wave_high, wave_low, name="ratio")
    clamped, total = call(
        bind(last_body, lat_rows), (grid_shape, sum_shape), dev, sphere(spec, False), logs, wave_high, wave_low,
        scratch=[pltpu.VMEM((rows, lon_total), jnp.float32), pltpu.VMEM((lat_rows, lon_total), jnp.float32)],
        name="last",
    )
    center = (total + swap(total)) / count
    return jnp.exp(center), center[None] - clamped.reshape(precip.shape)


def fits_packed(mesh, shape):
    lat_groups, fields = mesh.shape["lat"], mesh.shape["field"]
    devices = lat_groups * fields
    field_total, lat_total, lon_total = shape
    degrees = lon_total // 2
    members, lat_rows = field_total // fields, lat_total // lat_groups
    return (
        fields == 2
        and lon_total == 4 * lat_total // 2
        and lat_total == 512
        and 2 * members * lat_rows == 128
        and fields * 2 * members == 8
        and lat_groups % 2 == 0
        and devices % QUART == 0
        and degrees % (8 * devices) == 0
        and (devices // 2) % 16 == 0
        and devices <= 128
    )


def on_device(mesh, precip):
    members, lat_rows, lon_total = precip.shape
    shape = (members * mesh.shape["field"], lat_rows * mesh.shape["lat"], lon_total)
    return on_device_packed(precip) if ITERS == 2 and fits_packed(mesh, shape) else on_device_plain(precip)


def solution(mesh):
    in_specs = (P("field", "lat", None),)
    out_specs = (P("lat", None), P("field", "lat", None))
    return jax.shard_map(
        lambda precip: on_device(mesh, precip),
        mesh=mesh, in_specs=in_specs, out_specs=out_specs, check_vma=False,
    )
```

```python
import math

import jax
import jax.numpy as jnp
import ml_dtypes
import numpy as np
from jax import lax
from jax.experimental import pallas as pl
from jax.experimental.pallas import tpu as pltpu
from jax.sharding import PartitionSpec as P

ITERS = 2


heat_rate = 2.0
floor_value = 0.1


def colatitudes(lat_total):
    index_rows = jnp.arange(lat_total, dtype=jnp.float32)
    return jnp.pi * (index_rows + 0.5) / lat_total


def quad_weights(lat_total, lon_total):
    polar_angle = colatitudes(lat_total)
    return jnp.sin(polar_angle) * (jnp.pi / lat_total) * (2.0 * jnp.pi / lon_total)


def heat_factors(degrees):
    level = jnp.arange(degrees, dtype=jnp.float32)
    return jnp.exp(-heat_rate * level * (level + 1.0) / (degrees * (degrees - 1.0)))


def legendre_north(orders, lat_total, degrees):
    half_rows = lat_total // 2
    polar_angle = colatitudes(lat_total)[:half_rows]
    cosine = jnp.cos(polar_angle)
    log_sine = jnp.log(jnp.sin(polar_angle))
    order_value = orders.astype(jnp.float32)
    step_count = jnp.arange(1, degrees + 1, dtype=jnp.float32)
    log_ratios = jnp.log((2.0 * step_count - 1.0) / (2.0 * step_count))
    within = step_count[None, :] <= order_value[:, None]
    partial_log = jnp.sum(jnp.where(within, log_ratios[None, :], 0.0), axis=1)
    log_start = 0.5 * jnp.log((2.0 * order_value + 1.0) / (4.0 * jnp.pi)) + 0.5 * partial_log
    start_log = log_start[:, None] + order_value[:, None] * log_sine[None, :]
    span_size = min(32, degrees)

    def advance(state, block_start):
        prev_one, prev_two, log_scale = state
        collected = []
        for offset in range(span_size):
            degree = (block_start + offset).astype(jnp.float32)
            safe_diff = jnp.maximum(degree * degree - order_value * order_value, 1.0)
            first_factor = jnp.sqrt((4.0 * degree * degree - 1.0) / safe_diff)
            numerator = (
                (2.0 * degree + 1.0) * (degree + order_value - 1.0) * (degree - order_value - 1.0)
            )
            denominator = jnp.maximum((2.0 * degree - 3.0) * safe_diff, 1.0)
            second_factor = jnp.sqrt(jnp.maximum(numerator, 0.0) / denominator)
            recurred = (
                first_factor[:, None] * cosine[None, :] * prev_one
                - second_factor[:, None] * prev_two
            )
            current = jnp.where(
                (degree > order_value)[:, None],
                recurred,
                jnp.where(
                    (degree == order_value)[:, None],
                    jnp.ones_like(recurred),
                    jnp.zeros_like(recurred),
                ),
            )
            collected.append(current * jnp.exp(log_scale))
            prev_two = prev_one
            prev_one = current
            if (offset + 1) % 8 == 0:
                magnitude = jnp.maximum(jnp.abs(prev_one), jnp.abs(prev_two))
                safe_size = jnp.where(magnitude > 0.0, magnitude, jnp.ones_like(magnitude))
                prev_one = prev_one / safe_size
                prev_two = prev_two / safe_size
                log_scale = log_scale + jnp.log(safe_size)
        return ((prev_one, prev_two, log_scale), jnp.stack(collected))

    empty_state = jnp.zeros((orders.shape[0], half_rows), jnp.float32)
    block_starts = jnp.arange(0, degrees, span_size, dtype=jnp.int32)
    final_state, stacked = lax.scan(advance, (empty_state, empty_state, start_log), block_starts)
    legendre = stacked.reshape(degrees, orders.shape[0], half_rows)
    return jnp.transpose(legendre, (1, 2, 0))


def fourier_tables(lon_total, degrees, groups):
    per_group = degrees // groups
    column = jnp.arange(2 * degrees, dtype=jnp.int32)
    group_index = column // (2 * per_group)
    within_group = column % (2 * per_group)
    part_index = within_group // per_group
    order_index = group_index * per_group + within_group % per_group
    points = jnp.arange(lon_total, dtype=jnp.int32)
    phase = (points[:, None] * order_index[None, :] % lon_total).astype(jnp.float32) * (
        2.0 * jnp.pi / lon_total
    )
    forward = jnp.where(part_index[None, :] == 0, jnp.cos(phase), -jnp.sin(phase))
    doubled = jnp.where(order_index == 0, 1.0, 2.0)
    backward = jnp.transpose(forward) * doubled[:, None]
    return (forward, backward)


def on_device_plain(precip):
    groups = lax.axis_size("lat")
    lat_index = lax.axis_index("lat")
    local_fields, lat_rows, lon_total = precip.shape
    lat_total = lat_rows * groups
    degrees = lon_total // 2
    orders_here = degrees // groups
    half_rows = lat_total // 2
    count_fields = local_fields * lax.axis_size("field")
    weights_all = quad_weights(lat_total, lon_total)
    local_weights = lax.dynamic_slice_in_dim(weights_all, lat_index * lat_rows, lat_rows)
    forward, backward = fourier_tables(lon_total, degrees, groups)
    heat_factor = heat_factors(degrees)
    orders = lat_index * orders_here + jnp.arange(orders_here, dtype=jnp.int32)
    north_table = legendre_north(orders, lat_total, degrees)
    paired = north_table.reshape(orders_here, half_rows, degrees // 2, 2)
    parity = (orders % 2 == 0)[:, None, None]
    even_table = jnp.where(parity, paired[..., 0], paired[..., 1])
    odd_table = jnp.where(parity, paired[..., 1], paired[..., 0])
    heat_paired = heat_factor.reshape(degrees // 2, 2)
    heat_even = jnp.where(parity[:, :, 0], heat_paired[None, :, 0], heat_paired[None, :, 1])
    heat_odd = jnp.where(parity[:, :, 0], heat_paired[None, :, 1], heat_paired[None, :, 0])
    weights_north = weights_all[:half_rows]

    def legendre_pass(spread):
        count_here = spread.shape[0]
        shaped = spread.reshape(count_here, lat_total, 2, orders_here)
        north_part = shaped[:, :half_rows]
        south_part = jnp.flip(shaped[:, half_rows:], axis=1)
        even_input = (north_part + south_part) * weights_north[None, :, None, None]
        odd_input = (north_part - south_part) * weights_north[None, :, None, None]
        even_coef = jnp.einsum(
            "mjk,fjpm->mfpk", even_table, even_input, precision=lax.Precision.HIGHEST
        )
        odd_coef = jnp.einsum(
            "mjk,fjpm->mfpk", odd_table, odd_input, precision=lax.Precision.HIGHEST
        )
        even_coef = even_coef * heat_even[:, None, None, :]
        odd_coef = odd_coef * heat_odd[:, None, None, :]
        even_sum = jnp.einsum(
            "mjk,mfpk->fjpm", even_table, even_coef, precision=lax.Precision.HIGHEST
        )
        odd_sum = jnp.einsum("mjk,mfpk->fjpm", odd_table, odd_coef, precision=lax.Precision.HIGHEST)
        result = jnp.concatenate([even_sum + odd_sum, jnp.flip(even_sum - odd_sum, axis=1)], axis=1)
        return result.reshape(count_here, lat_total, 2 * orders_here)

    def kernel_apply_step(fields):
        spectra = jnp.einsum("fjk,kc->fjc", fields, forward, precision=lax.Precision.HIGHEST)

        def one_member(carry, member_spectra):
            spread = lax.all_to_all(member_spectra, "lat", split_axis=1, concat_axis=0, tiled=True)
            filtered = legendre_pass(spread[None])
            returned = lax.all_to_all(filtered[0], "lat", split_axis=0, concat_axis=1, tiled=True)
            return (carry, returned)

        unused, gathered = lax.scan(one_member, jnp.zeros((), jnp.float32), spectra)
        return jnp.einsum("fjc,ck->fjk", gathered, backward, precision=lax.Precision.HIGHEST)

    partial_value = jnp.sum(precip * local_weights[None, :, None], axis=(1, 2))
    masses = lax.psum(partial_value, "lat") / (4.0 * jnp.pi)
    scaling_logs = jnp.zeros(precip.shape, jnp.float32)
    log_barycenter = jnp.zeros(precip.shape[1:], jnp.float32)
    scaled = precip / masses[:, None, None]
    ratio_field = scaled
    for sweep in range(ITERS):
        smoothed = kernel_apply_step(ratio_field)
        clamped_values = jnp.log(jnp.maximum(smoothed, floor_value))
        added_total = lax.psum(jnp.sum(scaling_logs + clamped_values, axis=0), "field")
        log_barycenter = added_total / count_fields
        scaling_logs = log_barycenter[None] - clamped_values
        if sweep + 1 < ITERS:
            blurred_scale = kernel_apply_step(jnp.exp(scaling_logs))
            ratio_field = scaled / jnp.maximum(blurred_scale, floor_value)
    return (jnp.exp(log_barycenter), scaling_logs)


QUART = 4


def split_pair(value):
    high = value.astype(jnp.bfloat16)
    low = (value - high.astype(jnp.float32)).astype(jnp.bfloat16)
    return high, low


def pair_rows(value):
    high, low = split_pair(value)
    return jnp.concatenate([high, low], axis=0)


def dot_nt(left, right):
    return lax.dot_general(left, right, (((1,), (1,)), ((), ())), preferred_element_type=jnp.float32)


def dot_nn(left, right):
    return lax.dot_general(left, right, (((1,), (0,)), ((), ())), preferred_element_type=jnp.float32)


def wave_tables(lon_total, devices, slots):
    span = lon_total // QUART
    residue = np.arange(QUART)[:, None, None]
    order = residue + QUART * np.arange(devices // QUART)[None, :, None]
    order = (order + devices * np.arange(slots)[None, None, :]).reshape(QUART, -1)
    phase = (order[:, :, None] * np.arange(span)[None, None, :] % lon_total) * (2.0 * np.pi / lon_total)
    table = np.concatenate([np.cos(phase), np.sin(phase)], axis=1).astype(np.float32)
    high = table.astype(ml_dtypes.bfloat16)
    low = (table - high.astype(np.float32)).astype(ml_dtypes.bfloat16)
    return np.stack([high, low])


def forward_waves(field, wave_ref, out_ref, ready=None, done=None):
    span = field.shape[1] // QUART
    rows = field.shape[0]
    lanes = 2 * rows
    part = [field[:, q * span : (q + 1) * span] for q in range(QUART)]
    sum_even, sum_odd = part[0] + part[2], part[1] + part[3]
    diff_even, diff_odd = part[0] - part[2], part[1] - part[3]
    stack_even = pair_rows(jnp.concatenate([sum_even + sum_odd, sum_even - sum_odd], axis=0))
    stack_odd = pair_rows(jnp.concatenate([diff_even, diff_odd], axis=0))
    orders = wave_ref.shape[2] // 2
    first = lax.broadcasted_iota(jnp.int32, (orders, lanes), 1) < rows
    for residue in range(QUART):
        stack = stack_odd if residue % 2 else stack_even
        if ready:
            ready[residue].wait()
        found = dot_nt(wave_ref[0, residue], stack) + dot_nt(wave_ref[1, residue], stack)
        found = found[:, :lanes] + found[:, lanes:]
        cosine, sine = found[:orders], found[orders:]
        if residue == 0:
            packed = jnp.where(first, cosine, -pltpu.roll(sine, rows, 1))
        elif residue == 2:
            packed = jnp.where(first, pltpu.roll(cosine, rows, 1), -sine)
        elif residue == 1:
            packed = jnp.where(first, cosine, -cosine) - pltpu.roll(sine, rows, 1)
        else:
            turned = pltpu.roll(sine, rows, 1)
            packed = cosine + jnp.where(first, turned, -turned)
        out_ref[:, residue] = packed.reshape(out_ref.shape[0], out_ref.shape[2], lanes)
        if done:
            done[residue].start()


def inverse_waves(spec_ref, wave_ref):
    outer, _, slots, lanes = spec_ref.shape
    rows = lanes // 2
    real = [None] * QUART
    cross = {}
    spare = None
    for residue in range(QUART):
        turned = jnp.transpose(spec_ref[:, residue].reshape(outer * slots, lanes))
        cosine, sine = turned[:rows], turned[rows:]
        if residue == 0:
            spare = sine[:, 0:1]
        left = jnp.concatenate([cosine, -sine], axis=1)
        if residue % 2:
            left = jnp.concatenate([left, jnp.concatenate([sine, cosine], axis=1)], axis=0)
        count = left.shape[0]
        left = pair_rows(left)
        found = dot_nn(left, wave_ref[0, residue]) + dot_nn(left, wave_ref[1, residue])
        found = found[:count] + found[count:]
        real[residue] = found[:rows]
        if residue % 2:
            cross[residue] = found[rows:]
    plus, minus = real[0] + real[2], real[0] - real[2]
    both, gap = real[1] + real[3], cross[1] - cross[3]
    return jnp.concatenate([plus + both, minus - gap, plus - both, minus + gap], axis=1), spare


def flip_rows(value, south, lat_rows):
    lanes = 128
    rows, width = value.shape
    sub = lax.broadcasted_iota(jnp.int32, (8, lanes), 0)
    source = jnp.where(south, 7 - sub, sub)
    blocks = lat_rows // 8
    out = []
    for base in range(0, rows, lat_rows):
        for block in range(blocks):
            near = value[base + 8 * block : base + 8 * block + 8]
            far = value[base + 8 * (blocks - 1 - block) : base + 8 * (blocks - block)]
            tile = jnp.where(south, far, near)
            pieces = [
                jnp.take_along_axis(tile[:, at : at + lanes], source, axis=0) for at in range(0, width, lanes)
            ]
            out.append(jnp.concatenate(pieces, axis=1))
    return jnp.concatenate(out, axis=0)


def device_index():
    return lax.axis_index("lat") * lax.axis_size("field") + lax.axis_index("field")


def in_south():
    return lax.axis_index("lat") >= lax.axis_size("lat") // 2


def first_body(lat_rows, field_hbm, wave_hbm, flipped_hbm, out_hbm, field_ref, wave_ref, flipped_ref, out_ref, sems):
    get_field = pltpu.make_async_copy(field_hbm, field_ref, sems.at[0])
    get_wave = [
        pltpu.make_async_copy(wave_hbm.at[:, r], wave_ref.at[:, r], sems.at[1 + r]) for r in range(QUART)
    ]
    put_flipped = pltpu.make_async_copy(flipped_ref, flipped_hbm, sems.at[1 + QUART])
    put_wave = [
        pltpu.make_async_copy(out_ref.at[:, r], out_hbm.at[:, r], sems.at[2 + QUART + r]) for r in range(QUART)
    ]
    get_field.start()
    for copy in get_wave:
        copy.start()
    get_field.wait()
    flipped_ref[...] = flip_rows(field_ref[...], in_south(), lat_rows)
    put_flipped.start()
    forward_waves(flipped_ref[...], wave_ref, out_ref, get_wave, put_wave)
    put_flipped.wait()
    for copy in put_wave:
        copy.wait()


def member_sum(value, lat_rows):
    total = value[:lat_rows]
    for member in range(1, value.shape[0] // lat_rows):
        total = total + value[member * lat_rows : (member + 1) * lat_rows]
    return total


def mass_body(lat_rows, spec_ref, field_ref, wave_ref, clamp_ref, sum_ref, scaled_ref):
    blurred, total = inverse_waves(spec_ref, wave_ref)
    inverse = (4.0 * math.pi) / total
    scaled_ref[...] = field_ref[...] * inverse
    clamped = jnp.log(jnp.maximum(blurred * inverse, floor_value))
    clamp_ref[...] = clamped
    sum_ref[...] = member_sum(clamped, lat_rows)


def center_body(count, lat_rows, clamp_ref, sum_ref, other_ref, wave_ref, logs_ref, out_ref):
    center = (sum_ref[...] + other_ref[...]) / count
    members = clamp_ref.shape[0] // lat_rows
    logs = jnp.concatenate([center] * members, axis=0) - clamp_ref[...]
    logs_ref[...] = logs
    forward_waves(jnp.exp(logs), wave_ref, out_ref)


def ratio_body(spec_ref, scaled_ref, wave_ref, out_ref):
    blurred, _ = inverse_waves(spec_ref, wave_ref)
    forward_waves(scaled_ref[...] / jnp.maximum(blurred, floor_value), wave_ref, out_ref)


def last_body(lat_rows, spec_ref, logs_ref, wave_ref, clamp_ref, sum_ref):
    blurred, _ = inverse_waves(spec_ref, wave_ref)
    clamped = jnp.log(jnp.maximum(blurred, floor_value))
    clamp_ref[...] = clamped
    sum_ref[...] = member_sum(logs_ref[...] + clamped, lat_rows)


def final_body(count, lat_rows, clamp_ref, sum_ref, other_ref, center_ref, logs_ref):
    south = in_south()
    center = flip_rows((sum_ref[...] + other_ref[...]) / count, south, lat_rows)
    center_ref[...] = jnp.exp(center)
    members = clamp_ref.shape[0] // lat_rows
    logs_ref[...] = jnp.concatenate([center] * members, axis=0) - flip_rows(clamp_ref[...], south, lat_rows)


def table_rows(degrees, devices, slot):
    return (degrees - devices * slot) // 2


def table_offset(degrees, devices, slot, parity):
    start = sum(2 * table_rows(degrees, devices, s) for s in range(slot))
    return start + parity * table_rows(degrees, devices, slot)


FAR_SLOTS = 3


def table_part(degrees, devices, slot, parity, near_ref, far_ref):
    count = table_rows(degrees, devices, slot)
    offset = table_offset(degrees, devices, slot, parity)
    if slot < FAR_SLOTS:
        return far_ref, offset, count
    return near_ref, offset - table_offset(degrees, devices, FAR_SLOTS, 0), count


def legendre_body(degrees, devices, slots, fixed_hbm, near_ref, far_hbm, fixed_ref, first_coef,
                  second_coef, left_half, right_half, far_ref, sem, far_sem):
    copy = pltpu.make_async_copy(fixed_hbm, fixed_ref, sem)
    copy.start()
    half = (left_half, right_half)
    lanes = 128
    device = device_index()
    order = lax.broadcasted_iota(jnp.int32, (slots, degrees), 0) * devices + device
    level = lax.broadcasted_iota(jnp.int32, (slots, degrees), 1)
    above = level > order
    order, level = order.astype(jnp.float32), level.astype(jnp.float32)
    diff = jnp.maximum(level * level - order * order, 1.0)
    rate = 0.5 * heat_rate / (degrees * (degrees - 1.0))
    first_ratio = jnp.exp(-rate * (2.0 * level))
    second_ratio = jnp.exp(-rate * (4.0 * level - 2.0))
    first_coef[...] = jnp.where(above, jnp.sqrt((4.0 * level * level - 1.0) / diff) * first_ratio, 0.0)
    numer = (2.0 * level + 1.0) * (level + order - 1.0) * (level - order - 1.0)
    denom = jnp.maximum((2.0 * level - 3.0) * diff, 1.0)
    second_coef[...] = jnp.where(above, jnp.sqrt(jnp.maximum(numer, 0.0) / denom) * second_ratio, 0.0)
    copy.wait()

    lane = lax.broadcasted_iota(jnp.int32, (slots, lanes), 1)
    start = jnp.sum(jnp.where(lane == device, fixed_ref[0:slots, 0:lanes], 0.0), axis=1, keepdims=True)
    sub = lax.broadcasted_iota(jnp.int32, (8, lanes), 0)
    tiles = slots // 8
    cosine = [jnp.broadcast_to(fixed_ref[slots : slots + 1, h * lanes : (h + 1) * lanes], (8, lanes)) for h in range(2)]
    log_sine = [jnp.broadcast_to(fixed_ref[slots + 1 : slots + 2, h * lanes : (h + 1) * lanes], (8, lanes)) for h in range(2)]
    order_tile = [(sub + 8 * t) * devices + device for t in range(tiles)]
    zero = jnp.zeros((8, lanes), jnp.float32)
    span_log = 60.0 * math.log(2.0)

    def fresh(tile):
        state = []
        for h in range(2):
            scale_log = start[8 * tile : 8 * tile + 8] + order_tile[tile].astype(jnp.float32) * log_sine[h]
            state.append((zero, zero, scale_log, jnp.exp(scale_log)))
        return state

    def chunk(index, states):
        active = len(states)
        base = pl.multiple_of(index * lanes, lanes)
        first = [first_coef[8 * t : 8 * t + 8, pl.ds(base, lanes)] for t in range(active)]
        second = [second_coef[8 * t : 8 * t + 8, pl.ds(base, lanes)] for t in range(active)]
        states = [list(s) for s in states]
        for k in range(lanes):
            degree = base + k
            for t in range(active):
                a = jnp.broadcast_to(first[t][:, k : k + 1], (8, lanes))
                b = jnp.broadcast_to(second[t][:, k : k + 1], (8, lanes))
                begin = jnp.where(order_tile[t] == degree, 1.0, 0.0)
                for h in range(2):
                    one, two, scale_log, scale = states[t][h]
                    now = (a * cosine[h]) * one + (begin - b * two)
                    half[h][pl.ds(degree * slots + 8 * t, 8), :] = now * scale
                    two, one = one, now
                    if (k + 1) % 8 == 0:
                        large = jnp.maximum(jnp.abs(one), jnp.abs(two)) > 2.0**30
                        factor = jnp.where(large, 2.0**-60, 1.0)
                        one, two = one * factor, two * factor
                        scale_log = scale_log + jnp.where(large, span_log, 0.0)
                        scale = jnp.exp(scale_log)
                    states[t][h] = (one, two, scale_log, scale)
        return states

    states = []
    chunks = degrees // lanes
    for index in range(chunks):
        while len(states) < tiles and 8 * len(states) * devices < (index + 1) * lanes:
            states.append(fresh(len(states)))
        states = chunk(index, states)

    put_far = pltpu.make_async_copy(far_ref, far_hbm, far_sem)
    for slot in range(slots):
        for parity in range(2):
            part_ref, offset, count = table_part(degrees, devices, slot, parity, near_ref, far_ref)
            begin = (devices * slot + parity) * slots + slot
            for h in range(2):
                high, low = split_pair(half[h][pl.ds(begin, count, stride=2 * slots), :])
                part_ref[0, offset : offset + count, h * lanes : (h + 1) * lanes] = high
                part_ref[1, offset : offset + count, h * lanes : (h + 1) * lanes] = low
        if slot == FAR_SLOTS - 1:
            put_far.start()
    put_far.wait()


def gather_orders(spec_ref, sign, fields, lat_groups, lat_rows, per_field, slots, even_in, odd_in):
    group_lanes = 128 // lat_rows
    for field in range(fields):
        for h in range(2):
            even, odd = [], []
            for q in range(group_lanes):
                lat = h * group_lanes + q
                north = spec_ref[lat * fields + field]
                south = spec_ref[(lat_groups - 1 - lat) * fields + field] * sign
                even.append(north + south)
                odd.append(north - south)
            for c in range(per_field):
                row = (field * per_field + c) * slots
                cut = slice(c * lat_rows, (c + 1) * lat_rows)
                even_in[h][row : row + slots, :] = jnp.concatenate([e[:, cut] for e in even], axis=1)
                odd_in[h][row : row + slots, :] = jnp.concatenate([o[:, cut] for o in odd], axis=1)


def scatter_orders(out_ref, fields, lat_groups, lat_rows, per_field, slots, north, south):
    group_lanes = 128 // lat_rows
    for field in range(fields):
        for lat in range(lat_groups // 2):
            h, q = lat // group_lanes, lat % group_lanes
            cut = slice(q * lat_rows, (q + 1) * lat_rows)
            rows = [(field * per_field + c) * slots for c in range(per_field)]
            near = [north[h][row : row + slots, cut] for row in rows]
            far = [south[h][row : row + slots, cut] for row in rows]
            out_ref[lat * fields + field] = jnp.concatenate(near, axis=1)
            out_ref[(lat_groups - 1 - lat) * fields + field] = jnp.concatenate(far, axis=1)


def sphere_body(degrees, devices, slots, lat_groups, lat_rows, members, with_mass, spec_ref, near_ref, far_in,
                fixed_hbm, out_ref, *rest):
    far_ref, rest = (rest[0], rest[1:]) if with_mass else (far_in, rest)
    fixed_ref, coef_ref, sem, far_sem = rest[:4]
    halves = rest[4:]
    copy = pltpu.make_async_copy(fixed_hbm, fixed_ref, sem)
    copy.start()
    if with_mass:
        get_far = pltpu.make_async_copy(far_in, far_ref, far_sem)
        get_far.start()
    even_in, odd_in, north_out, south_out = halves[0:2], halves[2:4], halves[4:6], halves[6:8]
    device = device_index()
    sign = jnp.where(device % 2 == 0, 1.0, -1.0)
    fields = devices // lat_groups
    per_field = 2 * members
    columns = fields * per_field
    gather_orders(spec_ref, sign, fields, lat_groups, lat_rows, per_field, slots, even_in, odd_in)
    copy.wait()
    mass = None

    def pick(slot, parity):
        picked = pl.ds(slot, columns, stride=slots)
        gain = 2.0 if slot else jnp.where(device == 0, 1.0, 2.0)
        pair = (even_in, odd_in)[parity]
        values = jnp.concatenate([pair[0][picked, :], pair[1][picked, :]], axis=1)
        return values * (fixed_ref[slots + 2 : slots + 3, :] * gain)

    def table(slot, parity):
        part_ref, offset, count = table_part(degrees, devices, slot, parity, near_ref, far_ref)
        return part_ref[0, offset : offset + count, :], part_ref[1, offset : offset + count, :], count

    if with_mass:
        mass = jnp.sum(pick(0, 0), axis=1, keepdims=True)
    for slot in list(range(FAR_SLOTS, slots)) + list(range(FAR_SLOTS)):
        if with_mass and slot == 0:
            get_far.wait()
        for parity in range(2):
            high, low, count = table(slot, parity)
            packed = pair_rows(pick(slot, parity))
            coef = dot_nt(packed, high) + dot_nt(packed, low)
            coef_ref[2 * slot + parity, :, 0:count] = pair_rows(coef[:columns] + coef[columns:])

    for slot in range(slots):
        found = []
        for parity in range(2):
            high, low, count = table(slot, parity)
            packed = coef_ref[2 * slot + parity, :, 0:count]
            back = dot_nn(packed, high) + dot_nn(packed, low)
            found.append(back[:columns] + back[columns:])
        north, south = found[0] + found[1], (found[0] - found[1]) * sign
        if with_mass and slot == 0:
            spread = jnp.broadcast_to(mass, north.shape)
            spread = pltpu.roll(spread, members, 0)
            which = lax.broadcasted_iota(jnp.int32, north.shape, 0) % per_field
            spare = (which >= members) & (device == 0)
            north, south = jnp.where(spare, spread, north), jnp.where(spare, spread, south)
        picked = pl.ds(slot, columns, stride=slots)
        for h in range(2):
            north_out[h][picked, :] = north[:, 128 * h : 128 * h + 128]
            south_out[h][picked, :] = south[:, 128 * h : 128 * h + 128]

    scatter_orders(out_ref, fields, lat_groups, lat_rows, per_field, slots, north_out, south_out)


def on_device_packed(precip):
    lat_groups, fields = lax.axis_size("lat"), lax.axis_size("field")
    devices = lat_groups * fields
    members, lat_rows, lon_total = precip.shape
    lat_total, degrees = lat_rows * lat_groups, lon_total // 2
    slots = degrees // devices
    rows = members * lat_rows
    polar = np.pi * (np.arange(lat_total // 2) + 0.5) / lat_total
    level = np.arange(degrees)
    step = np.arange(1, degrees)
    starts = np.concatenate([[0.0], np.cumsum(np.log((2.0 * step - 1.0) / (2.0 * step)))])
    starts = 0.5 * np.log((2.0 * level + 1.0) / (4.0 * np.pi)) + 0.5 * starts
    starts = starts - 0.5 * heat_rate * level * (level + 1.0) / (degrees * (degrees - 1.0))
    fixed = np.zeros((slots + 8, lat_total // 2), np.float32)
    fixed[:slots, :devices] = starts.reshape(slots, devices)
    fixed[slots] = np.cos(polar)
    fixed[slots + 1] = np.log(np.sin(polar))
    fixed[slots + 2] = np.sin(polar) * (np.pi / lat_total) * (2.0 * np.pi / lon_total)
    fixed = jnp.asarray(fixed)
    wave = jnp.asarray(wave_tables(lon_total, devices, slots))

    vmem = pl.BlockSpec(memory_space=pltpu.VMEM)
    outer = devices // QUART
    spec_shape = jax.ShapeDtypeStruct((outer, QUART, slots, 2 * rows), jnp.float32)
    grid_shape = jax.ShapeDtypeStruct((rows, lon_total), jnp.float32)
    sum_shape = jax.ShapeDtypeStruct((lat_rows, lon_total), jnp.float32)
    far_rows = table_offset(degrees, devices, FAR_SLOTS, 0)
    near_rows = table_offset(degrees, devices, slots, 0) - far_rows
    near_shape = jax.ShapeDtypeStruct((2, near_rows, lat_total // 2), jnp.bfloat16)
    far_shape = jax.ShapeDtypeStruct((2, far_rows, lat_total // 2), jnp.bfloat16)
    flat_shape = jax.ShapeDtypeStruct((devices, slots, 2 * rows), jnp.float32)
    hbm = pl.BlockSpec(memory_space=pl.ANY)

    def call(body, shapes, *operands, name, far=(), far_out=(), scratch=(), cost=None, limit=8):
        single = not isinstance(shapes, tuple)
        outs = [hbm if index in far_out else vmem for index in range(1 if single else len(shapes))]
        return pl.pallas_call(
            body,
            out_shape=shapes,
            in_specs=[hbm if any(o is f for f in far) else vmem for o in operands],
            out_specs=outs[0] if single else outs,
            scratch_shapes=list(scratch),
            cost_estimate=cost,
            compiler_params=pltpu.CompilerParams(vmem_limit_bytes=limit << 20),
            name=name,
        )(*operands)

    def exchange(spec):
        flat = spec.reshape(devices, slots, 2 * rows)
        return lax.all_to_all(flat, ("lat", "field"), split_axis=0, concat_axis=0, tiled=True)

    def swap(value):
        return lax.ppermute(value, "field", [(0, 1), (1, 0)])

    def bind(body, *bound):
        return lambda *refs: body(*bound, *refs)

    def buffer(shape, dtype=jnp.float32):
        return pltpu.VMEM(shape, dtype)

    columns = fields * 2 * members
    signal = pltpu.SemaphoreType.DMA(())

    def sphere(spec, near, far, with_mass):
        return call(
            bind(sphere_body, degrees, devices, slots, lat_groups, lat_rows, members, with_mass),
            (flat_shape, far_shape) if with_mass else flat_shape,
            exchange(spec), near, far, fixed, far=(far, fixed) if with_mass else (fixed,), name="sphere",
            limit=58 if with_mass else 8,
            scratch=[buffer(fixed.shape), buffer((2 * slots, 2 * columns, 256), jnp.bfloat16), signal, signal]
            + [buffer((columns * slots, 128))] * 8,
        )

    def arrive(spec):
        return exchange(spec).reshape(spec_shape.shape)

    near, far = call(
        bind(legendre_body, degrees, devices, slots), (near_shape, far_shape), fixed, far=(fixed,), far_out=(1,),
        scratch=[buffer(fixed.shape)] + [buffer((slots, degrees))] * 2 + [buffer((degrees * slots, 128))] * 2
        + [buffer(far_shape.shape, jnp.bfloat16), signal, signal],
        cost=pl.CostEstimate(flops=40_000_000, bytes_accessed=16 << 20, transcendentals=0),
        name="legendre", limit=60,
    )
    field = precip.reshape(rows, lon_total)
    flipped, spec = call(
        bind(first_body, lat_rows), (grid_shape, spec_shape), field, wave, far=(field, wave), far_out=(0, 1),
        name="first", limit=63,
        scratch=[buffer((rows, lon_total)), buffer(wave.shape, jnp.bfloat16), buffer((rows, lon_total)),
                 buffer(spec_shape.shape), pltpu.SemaphoreType.DMA((2 + 2 * QUART,))],
    )
    spec, far = sphere(spec, near, far, True)
    clamped, total, scaled = call(
        bind(mass_body, lat_rows), (grid_shape, sum_shape, grid_shape), arrive(spec), flipped, wave, name="mass",
    )
    count = float(members * fields)
    logs, spec = call(
        bind(center_body, count, lat_rows), (grid_shape, spec_shape), clamped, total, swap(total), wave,
        name="center",
    )
    spec = sphere(spec, near, far, False)
    spec = call(ratio_body, spec_shape, arrive(spec), scaled, wave, name="ratio")
    spec = sphere(spec, near, far, False)
    clamped, total = call(
        bind(last_body, lat_rows), (grid_shape, sum_shape), arrive(spec), logs, wave, name="last",
    )
    barycenter, logs = call(
        bind(final_body, count, lat_rows), (sum_shape, grid_shape), clamped, total, swap(total), name="final",
    )
    return barycenter, logs.reshape(precip.shape)


def fits_packed(mesh, shape):
    lat_groups, fields = mesh.shape["lat"], mesh.shape["field"]
    devices = lat_groups * fields
    field_total, lat_total, lon_total = shape
    degrees = lon_total // 2
    members, lat_rows = field_total // fields, lat_total // lat_groups
    return (
        fields == 2
        and lon_total == 4 * lat_total // 2
        and lat_total == 512
        and 2 * members * lat_rows == 128
        and fields * 2 * members == 8
        and lat_groups % 2 == 0
        and devices % QUART == 0
        and degrees % (8 * devices) == 0
        and (devices // 2) % 16 == 0
        and devices <= 128
    )


def on_device(mesh, precip):
    members, lat_rows, lon_total = precip.shape
    shape = (members * mesh.shape["field"], lat_rows * mesh.shape["lat"], lon_total)
    return on_device_packed(precip) if ITERS == 2 and fits_packed(mesh, shape) else on_device_plain(precip)


def solution(mesh):
    in_specs = (P("field", "lat", None),)
    out_specs = (P("lat", None), P("field", "lat", None))
    return jax.shard_map(
        lambda precip: on_device(mesh, precip),
        mesh=mesh, in_specs=in_specs, out_specs=out_specs, check_vma=False,
    )
```

```python
import math

import jax
import jax.numpy as jnp
import ml_dtypes
import numpy as np
from jax import lax
from jax.experimental import pallas as pl
from jax.experimental.pallas import tpu as pltpu
from jax.sharding import PartitionSpec as P

ITERS = 2


heat_rate = 2.0
floor_value = 0.1


def colatitudes(lat_total):
    index_rows = jnp.arange(lat_total, dtype=jnp.float32)
    return jnp.pi * (index_rows + 0.5) / lat_total


def quad_weights(lat_total, lon_total):
    polar_angle = colatitudes(lat_total)
    return jnp.sin(polar_angle) * (jnp.pi / lat_total) * (2.0 * jnp.pi / lon_total)


def heat_factors(degrees):
    level = jnp.arange(degrees, dtype=jnp.float32)
    return jnp.exp(-heat_rate * level * (level + 1.0) / (degrees * (degrees - 1.0)))


def legendre_north(orders, lat_total, degrees):
    half_rows = lat_total // 2
    polar_angle = colatitudes(lat_total)[:half_rows]
    cosine = jnp.cos(polar_angle)
    log_sine = jnp.log(jnp.sin(polar_angle))
    order_value = orders.astype(jnp.float32)
    step_count = jnp.arange(1, degrees + 1, dtype=jnp.float32)
    log_ratios = jnp.log((2.0 * step_count - 1.0) / (2.0 * step_count))
    within = step_count[None, :] <= order_value[:, None]
    partial_log = jnp.sum(jnp.where(within, log_ratios[None, :], 0.0), axis=1)
    log_start = 0.5 * jnp.log((2.0 * order_value + 1.0) / (4.0 * jnp.pi)) + 0.5 * partial_log
    start_log = log_start[:, None] + order_value[:, None] * log_sine[None, :]
    span_size = min(32, degrees)

    def advance(state, block_start):
        prev_one, prev_two, log_scale = state
        collected = []
        for offset in range(span_size):
            degree = (block_start + offset).astype(jnp.float32)
            safe_diff = jnp.maximum(degree * degree - order_value * order_value, 1.0)
            first_factor = jnp.sqrt((4.0 * degree * degree - 1.0) / safe_diff)
            numerator = (
                (2.0 * degree + 1.0) * (degree + order_value - 1.0) * (degree - order_value - 1.0)
            )
            denominator = jnp.maximum((2.0 * degree - 3.0) * safe_diff, 1.0)
            second_factor = jnp.sqrt(jnp.maximum(numerator, 0.0) / denominator)
            recurred = (
                first_factor[:, None] * cosine[None, :] * prev_one
                - second_factor[:, None] * prev_two
            )
            current = jnp.where(
                (degree > order_value)[:, None],
                recurred,
                jnp.where(
                    (degree == order_value)[:, None],
                    jnp.ones_like(recurred),
                    jnp.zeros_like(recurred),
                ),
            )
            collected.append(current * jnp.exp(log_scale))
            prev_two = prev_one
            prev_one = current
            if (offset + 1) % 8 == 0:
                magnitude = jnp.maximum(jnp.abs(prev_one), jnp.abs(prev_two))
                safe_size = jnp.where(magnitude > 0.0, magnitude, jnp.ones_like(magnitude))
                prev_one = prev_one / safe_size
                prev_two = prev_two / safe_size
                log_scale = log_scale + jnp.log(safe_size)
        return ((prev_one, prev_two, log_scale), jnp.stack(collected))

    empty_state = jnp.zeros((orders.shape[0], half_rows), jnp.float32)
    block_starts = jnp.arange(0, degrees, span_size, dtype=jnp.int32)
    final_state, stacked = lax.scan(advance, (empty_state, empty_state, start_log), block_starts)
    legendre = stacked.reshape(degrees, orders.shape[0], half_rows)
    return jnp.transpose(legendre, (1, 2, 0))


def fourier_tables(lon_total, degrees, groups):
    per_group = degrees // groups
    column = jnp.arange(2 * degrees, dtype=jnp.int32)
    group_index = column // (2 * per_group)
    within_group = column % (2 * per_group)
    part_index = within_group // per_group
    order_index = group_index * per_group + within_group % per_group
    points = jnp.arange(lon_total, dtype=jnp.int32)
    phase = (points[:, None] * order_index[None, :] % lon_total).astype(jnp.float32) * (
        2.0 * jnp.pi / lon_total
    )
    forward = jnp.where(part_index[None, :] == 0, jnp.cos(phase), -jnp.sin(phase))
    doubled = jnp.where(order_index == 0, 1.0, 2.0)
    backward = jnp.transpose(forward) * doubled[:, None]
    return (forward, backward)


def on_device_plain(precip):
    groups = lax.axis_size("lat")
    lat_index = lax.axis_index("lat")
    local_fields, lat_rows, lon_total = precip.shape
    lat_total = lat_rows * groups
    degrees = lon_total // 2
    orders_here = degrees // groups
    half_rows = lat_total // 2
    count_fields = local_fields * lax.axis_size("field")
    weights_all = quad_weights(lat_total, lon_total)
    local_weights = lax.dynamic_slice_in_dim(weights_all, lat_index * lat_rows, lat_rows)
    forward, backward = fourier_tables(lon_total, degrees, groups)
    heat_factor = heat_factors(degrees)
    orders = lat_index * orders_here + jnp.arange(orders_here, dtype=jnp.int32)
    north_table = legendre_north(orders, lat_total, degrees)
    paired = north_table.reshape(orders_here, half_rows, degrees // 2, 2)
    parity = (orders % 2 == 0)[:, None, None]
    even_table = jnp.where(parity, paired[..., 0], paired[..., 1])
    odd_table = jnp.where(parity, paired[..., 1], paired[..., 0])
    heat_paired = heat_factor.reshape(degrees // 2, 2)
    heat_even = jnp.where(parity[:, :, 0], heat_paired[None, :, 0], heat_paired[None, :, 1])
    heat_odd = jnp.where(parity[:, :, 0], heat_paired[None, :, 1], heat_paired[None, :, 0])
    weights_north = weights_all[:half_rows]

    def legendre_pass(spread):
        count_here = spread.shape[0]
        shaped = spread.reshape(count_here, lat_total, 2, orders_here)
        north_part = shaped[:, :half_rows]
        south_part = jnp.flip(shaped[:, half_rows:], axis=1)
        even_input = (north_part + south_part) * weights_north[None, :, None, None]
        odd_input = (north_part - south_part) * weights_north[None, :, None, None]
        even_coef = jnp.einsum(
            "mjk,fjpm->mfpk", even_table, even_input, precision=lax.Precision.HIGHEST
        )
        odd_coef = jnp.einsum(
            "mjk,fjpm->mfpk", odd_table, odd_input, precision=lax.Precision.HIGHEST
        )
        even_coef = even_coef * heat_even[:, None, None, :]
        odd_coef = odd_coef * heat_odd[:, None, None, :]
        even_sum = jnp.einsum(
            "mjk,mfpk->fjpm", even_table, even_coef, precision=lax.Precision.HIGHEST
        )
        odd_sum = jnp.einsum("mjk,mfpk->fjpm", odd_table, odd_coef, precision=lax.Precision.HIGHEST)
        result = jnp.concatenate([even_sum + odd_sum, jnp.flip(even_sum - odd_sum, axis=1)], axis=1)
        return result.reshape(count_here, lat_total, 2 * orders_here)

    def kernel_apply_step(fields):
        spectra = jnp.einsum("fjk,kc->fjc", fields, forward, precision=lax.Precision.HIGHEST)

        def one_member(carry, member_spectra):
            spread = lax.all_to_all(member_spectra, "lat", split_axis=1, concat_axis=0, tiled=True)
            filtered = legendre_pass(spread[None])
            returned = lax.all_to_all(filtered[0], "lat", split_axis=0, concat_axis=1, tiled=True)
            return (carry, returned)

        unused, gathered = lax.scan(one_member, jnp.zeros((), jnp.float32), spectra)
        return jnp.einsum("fjc,ck->fjk", gathered, backward, precision=lax.Precision.HIGHEST)

    partial_value = jnp.sum(precip * local_weights[None, :, None], axis=(1, 2))
    masses = lax.psum(partial_value, "lat") / (4.0 * jnp.pi)
    scaling_logs = jnp.zeros(precip.shape, jnp.float32)
    log_barycenter = jnp.zeros(precip.shape[1:], jnp.float32)
    scaled = precip / masses[:, None, None]
    ratio_field = scaled
    for sweep in range(ITERS):
        smoothed = kernel_apply_step(ratio_field)
        clamped_values = jnp.log(jnp.maximum(smoothed, floor_value))
        added_total = lax.psum(jnp.sum(scaling_logs + clamped_values, axis=0), "field")
        log_barycenter = added_total / count_fields
        scaling_logs = log_barycenter[None] - clamped_values
        if sweep + 1 < ITERS:
            blurred_scale = kernel_apply_step(jnp.exp(scaling_logs))
            ratio_field = scaled / jnp.maximum(blurred_scale, floor_value)
    return (jnp.exp(log_barycenter), scaling_logs)


QUART = 4


def split_pair(value):
    high = value.astype(jnp.bfloat16)
    low = (value - high.astype(jnp.float32)).astype(jnp.bfloat16)
    return high, low


def pair_rows(value):
    high, low = split_pair(value)
    return jnp.concatenate([high, low], axis=0)


def dot_nt(left, right):
    return lax.dot_general(left, right, (((1,), (1,)), ((), ())), preferred_element_type=jnp.float32)


def dot_nn(left, right):
    return lax.dot_general(left, right, (((1,), (0,)), ((), ())), preferred_element_type=jnp.float32)


def wave_tables(lon_total, devices, slots):
    span = lon_total // QUART
    residue = np.arange(QUART)[:, None, None]
    order = residue + QUART * np.arange(devices // QUART)[None, :, None]
    order = (order + devices * np.arange(slots)[None, None, :]).reshape(QUART, -1)
    phase = (order[:, :, None] * np.arange(span)[None, None, :] % lon_total) * (2.0 * np.pi / lon_total)
    table = np.concatenate([np.cos(phase), np.sin(phase)], axis=1).astype(np.float32)
    high = table.astype(ml_dtypes.bfloat16)
    low = (table - high.astype(np.float32)).astype(ml_dtypes.bfloat16)
    return np.stack([high, low])


def forward_waves(field, wave_ref, out_ref, ready=None, done=None):
    span = field.shape[1] // QUART
    rows = field.shape[0]
    lanes = 2 * rows
    part = [field[:, q * span : (q + 1) * span] for q in range(QUART)]
    sum_even, sum_odd = part[0] + part[2], part[1] + part[3]
    diff_even, diff_odd = part[0] - part[2], part[1] - part[3]
    stack_even = pair_rows(jnp.concatenate([sum_even + sum_odd, sum_even - sum_odd], axis=0))
    stack_odd = pair_rows(jnp.concatenate([diff_even, diff_odd], axis=0))
    orders = wave_ref.shape[2] // 2
    first = lax.broadcasted_iota(jnp.int32, (orders, lanes), 1) < rows
    for residue in range(QUART):
        stack = stack_odd if residue % 2 else stack_even
        if ready:
            ready[residue].wait()
        found = dot_nt(wave_ref[0, residue], stack) + dot_nt(wave_ref[1, residue], stack)
        found = found[:, :lanes] + found[:, lanes:]
        cosine, sine = found[:orders], found[orders:]
        if residue == 0:
            packed = jnp.where(first, cosine, -pltpu.roll(sine, rows, 1))
        elif residue == 2:
            packed = jnp.where(first, pltpu.roll(cosine, rows, 1), -sine)
        elif residue == 1:
            packed = jnp.where(first, cosine, -cosine) - pltpu.roll(sine, rows, 1)
        else:
            turned = pltpu.roll(sine, rows, 1)
            packed = cosine + jnp.where(first, turned, -turned)
        out_ref[:, residue] = packed.reshape(out_ref.shape[0], out_ref.shape[2], lanes)
        if done:
            done[residue].start()


def inverse_waves(spec_ref, wave_ref):
    outer, _, slots, lanes = spec_ref.shape
    rows = lanes // 2
    real = [None] * QUART
    cross = {}
    spare = None
    for residue in range(QUART):
        turned = jnp.transpose(spec_ref[:, residue].reshape(outer * slots, lanes))
        cosine, sine = turned[:rows], turned[rows:]
        if residue == 0:
            spare = sine[:, 0:1]
        left = jnp.concatenate([cosine, -sine], axis=1)
        if residue % 2:
            left = jnp.concatenate([left, jnp.concatenate([sine, cosine], axis=1)], axis=0)
        count = left.shape[0]
        left = pair_rows(left)
        found = dot_nn(left, wave_ref[0, residue]) + dot_nn(left, wave_ref[1, residue])
        found = found[:count] + found[count:]
        real[residue] = found[:rows]
        if residue % 2:
            cross[residue] = found[rows:]
    plus, minus = real[0] + real[2], real[0] - real[2]
    both, gap = real[1] + real[3], cross[1] - cross[3]
    return jnp.concatenate([plus + both, minus - gap, plus - both, minus + gap], axis=1), spare


def flip_rows(value, south, lat_rows):
    lanes = 128
    rows, width = value.shape
    sub = lax.broadcasted_iota(jnp.int32, (8, lanes), 0)
    source = jnp.where(south, 7 - sub, sub)
    blocks = lat_rows // 8
    out = []
    for base in range(0, rows, lat_rows):
        for block in range(blocks):
            near = value[base + 8 * block : base + 8 * block + 8]
            far = value[base + 8 * (blocks - 1 - block) : base + 8 * (blocks - block)]
            tile = jnp.where(south, far, near)
            pieces = [
                jnp.take_along_axis(tile[:, at : at + lanes], source, axis=0) for at in range(0, width, lanes)
            ]
            out.append(jnp.concatenate(pieces, axis=1))
    return jnp.concatenate(out, axis=0)


def device_index():
    return lax.axis_index("lat") * lax.axis_size("field") + lax.axis_index("field")


def in_south():
    return lax.axis_index("lat") >= lax.axis_size("lat") // 2


def first_body(lat_rows, field_hbm, wave_hbm, flipped_hbm, out_hbm, field_ref, wave_ref, flipped_ref, out_ref, sems):
    get_field = pltpu.make_async_copy(field_hbm, field_ref, sems.at[0])
    get_wave = [
        pltpu.make_async_copy(wave_hbm.at[:, r], wave_ref.at[:, r], sems.at[1 + r]) for r in range(QUART)
    ]
    put_flipped = pltpu.make_async_copy(flipped_ref, flipped_hbm, sems.at[1 + QUART])
    put_wave = [
        pltpu.make_async_copy(out_ref.at[:, r], out_hbm.at[:, r], sems.at[2 + QUART + r]) for r in range(QUART)
    ]
    get_field.start()
    for copy in get_wave:
        copy.start()
    get_field.wait()
    flipped_ref[...] = flip_rows(field_ref[...], in_south(), lat_rows)
    put_flipped.start()
    forward_waves(flipped_ref[...], wave_ref, out_ref, get_wave, put_wave)
    put_flipped.wait()
    for copy in put_wave:
        copy.wait()


def member_sum(value, lat_rows):
    total = value[:lat_rows]
    for member in range(1, value.shape[0] // lat_rows):
        total = total + value[member * lat_rows : (member + 1) * lat_rows]
    return total


def mass_body(lat_rows, spec_ref, field_ref, wave_ref, clamp_ref, sum_ref, scaled_ref):
    blurred, total = inverse_waves(spec_ref, wave_ref)
    inverse = (4.0 * math.pi) / total
    scaled_ref[...] = field_ref[...] * inverse
    clamped = jnp.log(jnp.maximum(blurred * inverse, floor_value))
    clamp_ref[...] = clamped
    sum_ref[...] = member_sum(clamped, lat_rows)


def center_body(count, lat_rows, clamp_ref, sum_ref, other_ref, wave_ref, logs_ref, out_ref):
    center = (sum_ref[...] + other_ref[...]) / count
    members = clamp_ref.shape[0] // lat_rows
    logs = jnp.concatenate([center] * members, axis=0) - clamp_ref[...]
    logs_ref[...] = logs
    forward_waves(jnp.exp(logs), wave_ref, out_ref)


def ratio_body(spec_ref, scaled_ref, wave_ref, out_ref):
    blurred, _ = inverse_waves(spec_ref, wave_ref)
    forward_waves(scaled_ref[...] / jnp.maximum(blurred, floor_value), wave_ref, out_ref)


def last_body(lat_rows, spec_ref, logs_ref, wave_ref, clamp_ref, sum_ref):
    blurred, _ = inverse_waves(spec_ref, wave_ref)
    clamped = jnp.log(jnp.maximum(blurred, floor_value))
    clamp_ref[...] = clamped
    sum_ref[...] = member_sum(logs_ref[...] + clamped, lat_rows)


def final_body(count, lat_rows, clamp_ref, sum_ref, other_ref, center_ref, logs_ref):
    south = in_south()
    center = flip_rows((sum_ref[...] + other_ref[...]) / count, south, lat_rows)
    center_ref[...] = jnp.exp(center)
    members = clamp_ref.shape[0] // lat_rows
    logs_ref[...] = jnp.concatenate([center] * members, axis=0) - flip_rows(clamp_ref[...], south, lat_rows)


def table_rows(degrees, devices, slot):
    return (degrees - devices * slot) // 2


def table_offset(degrees, devices, slot, parity):
    start = sum(2 * table_rows(degrees, devices, s) for s in range(slot))
    return start + parity * table_rows(degrees, devices, slot)


FAR_SLOTS = 3


def table_part(degrees, devices, slot, parity, near_ref, far_ref):
    count = table_rows(degrees, devices, slot)
    offset = table_offset(degrees, devices, slot, parity)
    if slot < FAR_SLOTS:
        return far_ref, offset, count
    return near_ref, offset - table_offset(degrees, devices, FAR_SLOTS, 0), count


def legendre_body(degrees, devices, slots, fixed_hbm, near_ref, far_hbm, fixed_ref, first_coef,
                  second_coef, left_half, right_half, far_ref, sem, far_sem):
    copy = pltpu.make_async_copy(fixed_hbm, fixed_ref, sem)
    copy.start()
    half = (left_half, right_half)
    lanes = 128
    device = device_index()
    order = lax.broadcasted_iota(jnp.int32, (slots, degrees), 0) * devices + device
    level = lax.broadcasted_iota(jnp.int32, (slots, degrees), 1)
    above = level > order
    order, level = order.astype(jnp.float32), level.astype(jnp.float32)
    diff = jnp.maximum(level * level - order * order, 1.0)
    rate = 0.5 * heat_rate / (degrees * (degrees - 1.0))
    first_ratio = jnp.exp(-rate * (2.0 * level))
    second_ratio = jnp.exp(-rate * (4.0 * level - 2.0))
    first_coef[...] = jnp.where(above, jnp.sqrt((4.0 * level * level - 1.0) / diff) * first_ratio, 0.0)
    numer = (2.0 * level + 1.0) * (level + order - 1.0) * (level - order - 1.0)
    denom = jnp.maximum((2.0 * level - 3.0) * diff, 1.0)
    second_coef[...] = jnp.where(above, jnp.sqrt(jnp.maximum(numer, 0.0) / denom) * second_ratio, 0.0)
    copy.wait()

    lane = lax.broadcasted_iota(jnp.int32, (slots, lanes), 1)
    start = jnp.sum(jnp.where(lane == device, fixed_ref[0:slots, 0:lanes], 0.0), axis=1, keepdims=True)
    sub = lax.broadcasted_iota(jnp.int32, (8, lanes), 0)
    tiles = slots // 8
    cosine = [jnp.broadcast_to(fixed_ref[slots : slots + 1, h * lanes : (h + 1) * lanes], (8, lanes)) for h in range(2)]
    log_sine = [jnp.broadcast_to(fixed_ref[slots + 1 : slots + 2, h * lanes : (h + 1) * lanes], (8, lanes)) for h in range(2)]
    order_tile = [(sub + 8 * t) * devices + device for t in range(tiles)]
    zero = jnp.zeros((8, lanes), jnp.float32)
    span_log = 60.0 * math.log(2.0)

    def fresh(tile):
        state = []
        for h in range(2):
            scale_log = start[8 * tile : 8 * tile + 8] + order_tile[tile].astype(jnp.float32) * log_sine[h]
            state.append((zero, zero, scale_log, jnp.exp(scale_log)))
        return state

    def chunk(index, states):
        active = len(states)
        base = pl.multiple_of(index * lanes, lanes)
        first = [first_coef[8 * t : 8 * t + 8, pl.ds(base, lanes)] for t in range(active)]
        second = [second_coef[8 * t : 8 * t + 8, pl.ds(base, lanes)] for t in range(active)]
        states = [list(s) for s in states]
        for k in range(lanes):
            degree = base + k
            for t in range(active):
                a = jnp.broadcast_to(first[t][:, k : k + 1], (8, lanes))
                b = jnp.broadcast_to(second[t][:, k : k + 1], (8, lanes))
                begin = jnp.where(order_tile[t] == degree, 1.0, 0.0)
                for h in range(2):
                    one, two, scale_log, scale = states[t][h]
                    now = (a * cosine[h]) * one + (begin - b * two)
                    half[h][pl.ds(degree * slots + 8 * t, 8), :] = now * scale
                    two, one = one, now
                    if (k + 1) % 8 == 0:
                        large = jnp.maximum(jnp.abs(one), jnp.abs(two)) > 2.0**30
                        factor = jnp.where(large, 2.0**-60, 1.0)
                        one, two = one * factor, two * factor
                        scale_log = scale_log + jnp.where(large, span_log, 0.0)
                        scale = jnp.exp(scale_log)
                    states[t][h] = (one, two, scale_log, scale)
        return states

    states = []
    chunks = degrees // lanes
    for index in range(chunks):
        while len(states) < tiles and 8 * len(states) * devices < (index + 1) * lanes:
            states.append(fresh(len(states)))
        states = chunk(index, states)

    put_far = pltpu.make_async_copy(far_ref, far_hbm, far_sem)
    for slot in range(slots):
        for parity in range(2):
            part_ref, offset, count = table_part(degrees, devices, slot, parity, near_ref, far_ref)
            begin = (devices * slot + parity) * slots + slot
            for h in range(2):
                high, low = split_pair(half[h][pl.ds(begin, count, stride=2 * slots), :])
                part_ref[0, offset : offset + count, h * lanes : (h + 1) * lanes] = high
                part_ref[1, offset : offset + count, h * lanes : (h + 1) * lanes] = low
        if slot == FAR_SLOTS - 1:
            put_far.start()
    put_far.wait()


def gather_orders(spec_ref, sign, fields, lat_groups, lat_rows, per_field, slots, even_in, odd_in):
    group_lanes = 128 // lat_rows
    for field in range(fields):
        for h in range(2):
            even, odd = [], []
            for q in range(group_lanes):
                lat = h * group_lanes + q
                north = spec_ref[lat * fields + field]
                south = spec_ref[(lat_groups - 1 - lat) * fields + field] * sign
                even.append(north + south)
                odd.append(north - south)
            for c in range(per_field):
                row = (field * per_field + c) * slots
                cut = slice(c * lat_rows, (c + 1) * lat_rows)
                even_in[h][row : row + slots, :] = jnp.concatenate([e[:, cut] for e in even], axis=1)
                odd_in[h][row : row + slots, :] = jnp.concatenate([o[:, cut] for o in odd], axis=1)


def scatter_orders(out_ref, fields, lat_groups, lat_rows, per_field, slots, north, south):
    group_lanes = 128 // lat_rows
    for field in range(fields):
        for lat in range(lat_groups // 2):
            h, q = lat // group_lanes, lat % group_lanes
            cut = slice(q * lat_rows, (q + 1) * lat_rows)
            rows = [(field * per_field + c) * slots for c in range(per_field)]
            near = [north[h][row : row + slots, cut] for row in rows]
            far = [south[h][row : row + slots, cut] for row in rows]
            out_ref[lat * fields + field] = jnp.concatenate(near, axis=1)
            out_ref[(lat_groups - 1 - lat) * fields + field] = jnp.concatenate(far, axis=1)


def sphere_body(degrees, devices, slots, lat_groups, lat_rows, members, with_mass, spec_ref, near_ref, far_in,
                fixed_ref, out_ref, *rest):
    far_ref, rest = (rest[0], rest[1:]) if with_mass else (far_in, rest)
    coef_ref, far_sem = rest[:2]
    halves = rest[2:]
    if with_mass:
        get_far = pltpu.make_async_copy(far_in, far_ref, far_sem)
        get_far.start()
    even_in, odd_in, north_out, south_out = halves[0:2], halves[2:4], halves[4:6], halves[6:8]
    device = device_index()
    sign = jnp.where(device % 2 == 0, 1.0, -1.0)
    fields = devices // lat_groups
    per_field = 2 * members
    columns = fields * per_field
    gather_orders(spec_ref, sign, fields, lat_groups, lat_rows, per_field, slots, even_in, odd_in)
    mass = None

    def pick(slot, parity):
        picked = pl.ds(slot, columns, stride=slots)
        gain = 2.0 if slot else jnp.where(device == 0, 1.0, 2.0)
        pair = (even_in, odd_in)[parity]
        values = jnp.concatenate([pair[0][picked, :], pair[1][picked, :]], axis=1)
        return values * (fixed_ref[slots + 2 : slots + 3, :] * gain)

    def table(slot, parity):
        part_ref, offset, count = table_part(degrees, devices, slot, parity, near_ref, far_ref)
        return part_ref[0, offset : offset + count, :], part_ref[1, offset : offset + count, :], count

    if with_mass:
        mass = jnp.sum(pick(0, 0), axis=1, keepdims=True)
    for slot in list(range(FAR_SLOTS, slots)) + list(range(FAR_SLOTS)):
        if with_mass and slot == 0:
            get_far.wait()
        for parity in range(2):
            high, low, count = table(slot, parity)
            packed = pair_rows(pick(slot, parity))
            coef = dot_nt(packed, high) + dot_nt(packed, low)
            coef_ref[2 * slot + parity, :, 0:count] = pair_rows(coef[:columns] + coef[columns:])

    for slot in range(slots):
        found = []
        for parity in range(2):
            high, low, count = table(slot, parity)
            packed = coef_ref[2 * slot + parity, :, 0:count]
            back = dot_nn(packed, high) + dot_nn(packed, low)
            found.append(back[:columns] + back[columns:])
        north, south = found[0] + found[1], (found[0] - found[1]) * sign
        if with_mass and slot == 0:
            spread = jnp.broadcast_to(mass, north.shape)
            spread = pltpu.roll(spread, members, 0)
            which = lax.broadcasted_iota(jnp.int32, north.shape, 0) % per_field
            spare = (which >= members) & (device == 0)
            north, south = jnp.where(spare, spread, north), jnp.where(spare, spread, south)
        picked = pl.ds(slot, columns, stride=slots)
        for h in range(2):
            north_out[h][picked, :] = north[:, 128 * h : 128 * h + 128]
            south_out[h][picked, :] = south[:, 128 * h : 128 * h + 128]

    scatter_orders(out_ref, fields, lat_groups, lat_rows, per_field, slots, north_out, south_out)


def on_device_packed(precip):
    lat_groups, fields = lax.axis_size("lat"), lax.axis_size("field")
    devices = lat_groups * fields
    members, lat_rows, lon_total = precip.shape
    lat_total, degrees = lat_rows * lat_groups, lon_total // 2
    slots = degrees // devices
    rows = members * lat_rows
    polar = np.pi * (np.arange(lat_total // 2) + 0.5) / lat_total
    level = np.arange(degrees)
    step = np.arange(1, degrees)
    starts = np.concatenate([[0.0], np.cumsum(np.log((2.0 * step - 1.0) / (2.0 * step)))])
    starts = 0.5 * np.log((2.0 * level + 1.0) / (4.0 * np.pi)) + 0.5 * starts
    starts = starts - 0.5 * heat_rate * level * (level + 1.0) / (degrees * (degrees - 1.0))
    fixed = np.zeros((slots + 8, lat_total // 2), np.float32)
    fixed[:slots, :devices] = starts.reshape(slots, devices)
    fixed[slots] = np.cos(polar)
    fixed[slots + 1] = np.log(np.sin(polar))
    fixed[slots + 2] = np.sin(polar) * (np.pi / lat_total) * (2.0 * np.pi / lon_total)
    fixed = jnp.asarray(fixed)
    wave = jnp.asarray(wave_tables(lon_total, devices, slots))

    vmem = pl.BlockSpec(memory_space=pltpu.VMEM)
    outer = devices // QUART
    spec_shape = jax.ShapeDtypeStruct((outer, QUART, slots, 2 * rows), jnp.float32)
    grid_shape = jax.ShapeDtypeStruct((rows, lon_total), jnp.float32)
    sum_shape = jax.ShapeDtypeStruct((lat_rows, lon_total), jnp.float32)
    far_rows = table_offset(degrees, devices, FAR_SLOTS, 0)
    near_rows = table_offset(degrees, devices, slots, 0) - far_rows
    near_shape = jax.ShapeDtypeStruct((2, near_rows, lat_total // 2), jnp.bfloat16)
    far_shape = jax.ShapeDtypeStruct((2, far_rows, lat_total // 2), jnp.bfloat16)
    flat_shape = jax.ShapeDtypeStruct((devices, slots, 2 * rows), jnp.float32)
    hbm = pl.BlockSpec(memory_space=pl.ANY)

    def call(body, shapes, *operands, name, far=(), far_out=(), scratch=(), cost=None, limit=8):
        single = not isinstance(shapes, tuple)
        shapes = (shapes,) if single else shapes
        outs = [hbm if index in far_out else vmem for index in range(len(shapes))]
        shapes = [
            pltpu.HBM(shape.shape, shape.dtype) if index in far_out else shape for index, shape in enumerate(shapes)
        ]
        specs = [hbm if any(o is f for f in far) else vmem for o in operands]
        operands = [
            pltpu.with_memory_space_constraint(o, pltpu.HBM) if any(o is f for f in far) else o for o in operands
        ]
        return pl.pallas_call(
            body,
            out_shape=shapes[0] if single else shapes,
            in_specs=specs,
            out_specs=outs[0] if single else outs,
            scratch_shapes=list(scratch),
            cost_estimate=cost,
            compiler_params=pltpu.CompilerParams(vmem_limit_bytes=limit << 20),
            name=name,
        )(*operands)

    def exchange(spec):
        flat = spec.reshape(devices, slots, 2 * rows)
        return lax.all_to_all(flat, ("lat", "field"), split_axis=0, concat_axis=0, tiled=True)

    def swap(value):
        return lax.ppermute(value, "field", [(0, 1), (1, 0)])

    def bind(body, *bound):
        return lambda *refs: body(*bound, *refs)

    def buffer(shape, dtype=jnp.float32):
        return pltpu.VMEM(shape, dtype)

    columns = fields * 2 * members
    signal = pltpu.SemaphoreType.DMA(())

    def sphere(spec, near, far, with_mass):
        return call(
            bind(sphere_body, degrees, devices, slots, lat_groups, lat_rows, members, with_mass),
            (flat_shape, far_shape) if with_mass else flat_shape,
            exchange(spec), near, far, fixed, far=(far,) if with_mass else (), name="sphere",
            limit=8,
            scratch=[buffer((2 * slots, 2 * columns, 256), jnp.bfloat16), signal]
            + [buffer((columns * slots, 128))] * 8,
        )

    def arrive(spec):
        return exchange(spec).reshape(spec_shape.shape)

    near, far = call(
        bind(legendre_body, degrees, devices, slots), (near_shape, far_shape), fixed, far=(fixed,), far_out=(1,),
        scratch=[buffer(fixed.shape)] + [buffer((slots, degrees))] * 2 + [buffer((degrees * slots, 128))] * 2
        + [buffer(far_shape.shape, jnp.bfloat16), signal, signal],
        cost=pl.CostEstimate(flops=40_000_000, bytes_accessed=16 << 20, transcendentals=0),
        name="legendre", limit=12,
    )
    field = precip.reshape(rows, lon_total)
    flipped, spec = call(
        bind(first_body, lat_rows), (grid_shape, spec_shape), field, wave, far=(field, wave), far_out=(0, 1),
        name="first", limit=8,
        scratch=[buffer((rows, lon_total)), buffer(wave.shape, jnp.bfloat16), buffer((rows, lon_total)),
                 buffer(spec_shape.shape), pltpu.SemaphoreType.DMA((2 + 2 * QUART,))],
    )
    spec, far = sphere(spec, near, far, True)
    clamped, total, scaled = call(
        bind(mass_body, lat_rows), (grid_shape, sum_shape, grid_shape), arrive(spec), flipped, wave, name="mass",
    )
    count = float(members * fields)
    logs, spec = call(
        bind(center_body, count, lat_rows), (grid_shape, spec_shape), clamped, total, swap(total), wave,
        name="center",
    )
    spec = sphere(spec, near, far, False)
    spec = call(ratio_body, spec_shape, arrive(spec), scaled, wave, name="ratio")
    spec = sphere(spec, near, far, False)
    clamped, total = call(
        bind(last_body, lat_rows), (grid_shape, sum_shape), arrive(spec), logs, wave, name="last",
    )
    barycenter, logs = call(
        bind(final_body, count, lat_rows), (sum_shape, grid_shape), clamped, total, swap(total), name="final",
    )
    return barycenter, logs.reshape(precip.shape)


def fits_packed(mesh, shape):
    lat_groups, fields = mesh.shape["lat"], mesh.shape["field"]
    devices = lat_groups * fields
    field_total, lat_total, lon_total = shape
    degrees = lon_total // 2
    members, lat_rows = field_total // fields, lat_total // lat_groups
    return (
        fields == 2
        and lon_total == 4 * lat_total // 2
        and lat_total == 512
        and 2 * members * lat_rows == 128
        and fields * 2 * members == 8
        and lat_groups % 2 == 0
        and devices % QUART == 0
        and degrees % (8 * devices) == 0
        and (devices // 2) % 16 == 0
        and devices <= 128
    )


def on_device(mesh, precip):
    members, lat_rows, lon_total = precip.shape
    shape = (members * mesh.shape["field"], lat_rows * mesh.shape["lat"], lon_total)
    return on_device_packed(precip) if ITERS == 2 and fits_packed(mesh, shape) else on_device_plain(precip)


def solution(mesh):
    in_specs = (P("field", "lat", None),)
    out_specs = (P("lat", None), P("field", "lat", None))
    return jax.shard_map(
        lambda precip: on_device(mesh, precip),
        mesh=mesh, in_specs=in_specs, out_specs=out_specs, check_vma=False,
    )
```

```python
import math

import jax
import jax.numpy as jnp
import ml_dtypes
import numpy as np
from jax import lax
from jax.experimental import pallas as pl
from jax.experimental.pallas import tpu as pltpu
from jax.sharding import PartitionSpec as P

ITERS = 2


heat_rate = 2.0
floor_value = 0.1


def colatitudes(lat_total):
    index_rows = jnp.arange(lat_total, dtype=jnp.float32)
    return jnp.pi * (index_rows + 0.5) / lat_total


def quad_weights(lat_total, lon_total):
    polar_angle = colatitudes(lat_total)
    return jnp.sin(polar_angle) * (jnp.pi / lat_total) * (2.0 * jnp.pi / lon_total)


def heat_factors(degrees):
    level = jnp.arange(degrees, dtype=jnp.float32)
    return jnp.exp(-heat_rate * level * (level + 1.0) / (degrees * (degrees - 1.0)))


def legendre_north(orders, lat_total, degrees):
    half_rows = lat_total // 2
    polar_angle = colatitudes(lat_total)[:half_rows]
    cosine = jnp.cos(polar_angle)
    log_sine = jnp.log(jnp.sin(polar_angle))
    order_value = orders.astype(jnp.float32)
    step_count = jnp.arange(1, degrees + 1, dtype=jnp.float32)
    log_ratios = jnp.log((2.0 * step_count - 1.0) / (2.0 * step_count))
    within = step_count[None, :] <= order_value[:, None]
    partial_log = jnp.sum(jnp.where(within, log_ratios[None, :], 0.0), axis=1)
    log_start = 0.5 * jnp.log((2.0 * order_value + 1.0) / (4.0 * jnp.pi)) + 0.5 * partial_log
    start_log = log_start[:, None] + order_value[:, None] * log_sine[None, :]
    span_size = min(32, degrees)

    def advance(state, block_start):
        prev_one, prev_two, log_scale = state
        collected = []
        for offset in range(span_size):
            degree = (block_start + offset).astype(jnp.float32)
            safe_diff = jnp.maximum(degree * degree - order_value * order_value, 1.0)
            first_factor = jnp.sqrt((4.0 * degree * degree - 1.0) / safe_diff)
            numerator = (
                (2.0 * degree + 1.0) * (degree + order_value - 1.0) * (degree - order_value - 1.0)
            )
            denominator = jnp.maximum((2.0 * degree - 3.0) * safe_diff, 1.0)
            second_factor = jnp.sqrt(jnp.maximum(numerator, 0.0) / denominator)
            recurred = (
                first_factor[:, None] * cosine[None, :] * prev_one
                - second_factor[:, None] * prev_two
            )
            current = jnp.where(
                (degree > order_value)[:, None],
                recurred,
                jnp.where(
                    (degree == order_value)[:, None],
                    jnp.ones_like(recurred),
                    jnp.zeros_like(recurred),
                ),
            )
            collected.append(current * jnp.exp(log_scale))
            prev_two = prev_one
            prev_one = current
            if (offset + 1) % 8 == 0:
                magnitude = jnp.maximum(jnp.abs(prev_one), jnp.abs(prev_two))
                safe_size = jnp.where(magnitude > 0.0, magnitude, jnp.ones_like(magnitude))
                prev_one = prev_one / safe_size
                prev_two = prev_two / safe_size
                log_scale = log_scale + jnp.log(safe_size)
        return ((prev_one, prev_two, log_scale), jnp.stack(collected))

    empty_state = jnp.zeros((orders.shape[0], half_rows), jnp.float32)
    block_starts = jnp.arange(0, degrees, span_size, dtype=jnp.int32)
    final_state, stacked = lax.scan(advance, (empty_state, empty_state, start_log), block_starts)
    legendre = stacked.reshape(degrees, orders.shape[0], half_rows)
    return jnp.transpose(legendre, (1, 2, 0))


def fourier_tables(lon_total, degrees, groups):
    per_group = degrees // groups
    column = jnp.arange(2 * degrees, dtype=jnp.int32)
    group_index = column // (2 * per_group)
    within_group = column % (2 * per_group)
    part_index = within_group // per_group
    order_index = group_index * per_group + within_group % per_group
    points = jnp.arange(lon_total, dtype=jnp.int32)
    phase = (points[:, None] * order_index[None, :] % lon_total).astype(jnp.float32) * (
        2.0 * jnp.pi / lon_total
    )
    forward = jnp.where(part_index[None, :] == 0, jnp.cos(phase), -jnp.sin(phase))
    doubled = jnp.where(order_index == 0, 1.0, 2.0)
    backward = jnp.transpose(forward) * doubled[:, None]
    return (forward, backward)


def on_device_plain(precip):
    groups = lax.axis_size("lat")
    lat_index = lax.axis_index("lat")
    local_fields, lat_rows, lon_total = precip.shape
    lat_total = lat_rows * groups
    degrees = lon_total // 2
    orders_here = degrees // groups
    half_rows = lat_total // 2
    count_fields = local_fields * lax.axis_size("field")
    weights_all = quad_weights(lat_total, lon_total)
    local_weights = lax.dynamic_slice_in_dim(weights_all, lat_index * lat_rows, lat_rows)
    forward, backward = fourier_tables(lon_total, degrees, groups)
    heat_factor = heat_factors(degrees)
    orders = lat_index * orders_here + jnp.arange(orders_here, dtype=jnp.int32)
    north_table = legendre_north(orders, lat_total, degrees)
    paired = north_table.reshape(orders_here, half_rows, degrees // 2, 2)
    parity = (orders % 2 == 0)[:, None, None]
    even_table = jnp.where(parity, paired[..., 0], paired[..., 1])
    odd_table = jnp.where(parity, paired[..., 1], paired[..., 0])
    heat_paired = heat_factor.reshape(degrees // 2, 2)
    heat_even = jnp.where(parity[:, :, 0], heat_paired[None, :, 0], heat_paired[None, :, 1])
    heat_odd = jnp.where(parity[:, :, 0], heat_paired[None, :, 1], heat_paired[None, :, 0])
    weights_north = weights_all[:half_rows]

    def legendre_pass(spread):
        count_here = spread.shape[0]
        shaped = spread.reshape(count_here, lat_total, 2, orders_here)
        north_part = shaped[:, :half_rows]
        south_part = jnp.flip(shaped[:, half_rows:], axis=1)
        even_input = (north_part + south_part) * weights_north[None, :, None, None]
        odd_input = (north_part - south_part) * weights_north[None, :, None, None]
        even_coef = jnp.einsum(
            "mjk,fjpm->mfpk", even_table, even_input, precision=lax.Precision.HIGHEST
        )
        odd_coef = jnp.einsum(
            "mjk,fjpm->mfpk", odd_table, odd_input, precision=lax.Precision.HIGHEST
        )
        even_coef = even_coef * heat_even[:, None, None, :]
        odd_coef = odd_coef * heat_odd[:, None, None, :]
        even_sum = jnp.einsum(
            "mjk,mfpk->fjpm", even_table, even_coef, precision=lax.Precision.HIGHEST
        )
        odd_sum = jnp.einsum("mjk,mfpk->fjpm", odd_table, odd_coef, precision=lax.Precision.HIGHEST)
        result = jnp.concatenate([even_sum + odd_sum, jnp.flip(even_sum - odd_sum, axis=1)], axis=1)
        return result.reshape(count_here, lat_total, 2 * orders_here)

    def kernel_apply_step(fields):
        spectra = jnp.einsum("fjk,kc->fjc", fields, forward, precision=lax.Precision.HIGHEST)

        def one_member(carry, member_spectra):
            spread = lax.all_to_all(member_spectra, "lat", split_axis=1, concat_axis=0, tiled=True)
            filtered = legendre_pass(spread[None])
            returned = lax.all_to_all(filtered[0], "lat", split_axis=0, concat_axis=1, tiled=True)
            return (carry, returned)

        unused, gathered = lax.scan(one_member, jnp.zeros((), jnp.float32), spectra)
        return jnp.einsum("fjc,ck->fjk", gathered, backward, precision=lax.Precision.HIGHEST)

    partial_value = jnp.sum(precip * local_weights[None, :, None], axis=(1, 2))
    masses = lax.psum(partial_value, "lat") / (4.0 * jnp.pi)
    scaling_logs = jnp.zeros(precip.shape, jnp.float32)
    log_barycenter = jnp.zeros(precip.shape[1:], jnp.float32)
    scaled = precip / masses[:, None, None]
    ratio_field = scaled
    for sweep in range(ITERS):
        smoothed = kernel_apply_step(ratio_field)
        clamped_values = jnp.log(jnp.maximum(smoothed, floor_value))
        added_total = lax.psum(jnp.sum(scaling_logs + clamped_values, axis=0), "field")
        log_barycenter = added_total / count_fields
        scaling_logs = log_barycenter[None] - clamped_values
        if sweep + 1 < ITERS:
            blurred_scale = kernel_apply_step(jnp.exp(scaling_logs))
            ratio_field = scaled / jnp.maximum(blurred_scale, floor_value)
    return (jnp.exp(log_barycenter), scaling_logs)


QUART = 4


def split_pair(value):
    high = value.astype(jnp.bfloat16)
    low = (value - high.astype(jnp.float32)).astype(jnp.bfloat16)
    return high, low


def pair_rows(value):
    high, low = split_pair(value)
    return jnp.concatenate([high, low], axis=0)


def dot_nt(left, right):
    return lax.dot_general(left, right, (((1,), (1,)), ((), ())), preferred_element_type=jnp.float32)


def dot_nn(left, right):
    return lax.dot_general(left, right, (((1,), (0,)), ((), ())), preferred_element_type=jnp.float32)


def wave_tables(lon_total, devices, slots):
    span = lon_total // QUART
    residue = np.arange(QUART)[:, None, None]
    order = residue + QUART * np.arange(devices // QUART)[None, :, None]
    order = (order + devices * np.arange(slots)[None, None, :]).reshape(QUART, -1)
    phase = (order[:, :, None] * np.arange(span)[None, None, :] % lon_total) * (2.0 * np.pi / lon_total)
    table = np.concatenate([np.cos(phase), np.sin(phase)], axis=1).astype(np.float32)
    high = table.astype(ml_dtypes.bfloat16)
    low = (table - high.astype(np.float32)).astype(ml_dtypes.bfloat16)
    return np.stack([high, low])


def wave_seeds(lon_total, devices, slots):
    span = lon_total // QUART
    first = (np.arange(QUART)[:, None] + QUART * np.arange(devices // QUART)[None, :]).reshape(-1)
    phases = [
        orders[:, None] * np.arange(span)[None, :] % lon_total * (2.0 * np.pi / lon_total)
        for orders in (first, devices * np.arange(slots))
    ]
    return np.concatenate([f(p) for p in phases for f in (np.cos, np.sin)]).astype(np.float32)


def grow_waves(seed_ref, wave_ref, devices, slots):
    orders = wave_ref.shape[2] // 2
    step_cos = seed_ref[2 * devices : 2 * devices + slots, :]
    step_sin = seed_ref[2 * devices + slots : 2 * devices + 2 * slots, :]
    for row in range(devices):
        residue, at = row // (devices // QUART), row % (devices // QUART) * slots
        cosine, sine = seed_ref[row : row + 1, :], seed_ref[devices + row : devices + row + 1, :]
        for place, value in (
            (at, cosine * step_cos - sine * step_sin),
            (orders + at, sine * step_cos + cosine * step_sin),
        ):
            high, low = split_pair(value)
            wave_ref[0, residue, place : place + slots, :] = high
            wave_ref[1, residue, place : place + slots, :] = low


def forward_waves(field, wave_ref, out_ref, done=None):
    span = field.shape[1] // QUART
    rows = field.shape[0]
    lanes = 2 * rows
    part = [field[:, q * span : (q + 1) * span] for q in range(QUART)]
    sum_even, sum_odd = part[0] + part[2], part[1] + part[3]
    diff_even, diff_odd = part[0] - part[2], part[1] - part[3]
    stack_even = pair_rows(jnp.concatenate([sum_even + sum_odd, sum_even - sum_odd], axis=0))
    stack_odd = pair_rows(jnp.concatenate([diff_even, diff_odd], axis=0))
    orders = wave_ref.shape[2] // 2
    first = lax.broadcasted_iota(jnp.int32, (orders, lanes), 1) < rows
    for residue in range(QUART):
        stack = stack_odd if residue % 2 else stack_even
        found = dot_nt(wave_ref[0, residue], stack) + dot_nt(wave_ref[1, residue], stack)
        found = found[:, :lanes] + found[:, lanes:]
        cosine, sine = found[:orders], found[orders:]
        if residue == 0:
            packed = jnp.where(first, cosine, -pltpu.roll(sine, rows, 1))
        elif residue == 2:
            packed = jnp.where(first, pltpu.roll(cosine, rows, 1), -sine)
        elif residue == 1:
            packed = jnp.where(first, cosine, -cosine) - pltpu.roll(sine, rows, 1)
        else:
            turned = pltpu.roll(sine, rows, 1)
            packed = cosine + jnp.where(first, turned, -turned)
        out_ref[:, residue] = packed.reshape(out_ref.shape[0], out_ref.shape[2], lanes)
        if done:
            done[residue].start()


def inverse_waves(spec_ref, wave_ref):
    outer, _, slots, lanes = spec_ref.shape
    rows = lanes // 2
    real = [None] * QUART
    cross = {}
    spare = None
    for residue in range(QUART):
        turned = jnp.transpose(spec_ref[:, residue].reshape(outer * slots, lanes))
        cosine, sine = turned[:rows], turned[rows:]
        if residue == 0:
            spare = sine[:, 0:1]
        left = jnp.concatenate([cosine, -sine], axis=1)
        if residue % 2:
            left = jnp.concatenate([left, jnp.concatenate([sine, cosine], axis=1)], axis=0)
        count = left.shape[0]
        left = pair_rows(left)
        found = dot_nn(left, wave_ref[0, residue]) + dot_nn(left, wave_ref[1, residue])
        found = found[:count] + found[count:]
        real[residue] = found[:rows]
        if residue % 2:
            cross[residue] = found[rows:]
    plus, minus = real[0] + real[2], real[0] - real[2]
    both, gap = real[1] + real[3], cross[1] - cross[3]
    return jnp.concatenate([plus + both, minus - gap, plus - both, minus + gap], axis=1), spare


def flip_rows(value, south, lat_rows):
    lanes = 128
    rows, width = value.shape
    sub = lax.broadcasted_iota(jnp.int32, (8, lanes), 0)
    source = jnp.where(south, 7 - sub, sub)
    blocks = lat_rows // 8
    out = []
    for base in range(0, rows, lat_rows):
        for block in range(blocks):
            near = value[base + 8 * block : base + 8 * block + 8]
            far = value[base + 8 * (blocks - 1 - block) : base + 8 * (blocks - block)]
            tile = jnp.where(south, far, near)
            pieces = [
                jnp.take_along_axis(tile[:, at : at + lanes], source, axis=0) for at in range(0, width, lanes)
            ]
            out.append(jnp.concatenate(pieces, axis=1))
    return jnp.concatenate(out, axis=0)


def device_index():
    return lax.axis_index("lat") * lax.axis_size("field") + lax.axis_index("field")


def in_south():
    return lax.axis_index("lat") >= lax.axis_size("lat") // 2


def first_body(lat_rows, devices, slots, field_hbm, seed_hbm, flipped_hbm, out_hbm, field_ref, seed_ref, wave_ref,
               flipped_ref, out_ref, sems):
    get_field = pltpu.make_async_copy(field_hbm, field_ref, sems.at[0])
    get_seed = pltpu.make_async_copy(seed_hbm, seed_ref, sems.at[1])
    put_flipped = pltpu.make_async_copy(flipped_ref, flipped_hbm, sems.at[2])
    put_wave = [
        pltpu.make_async_copy(out_ref.at[:, r], out_hbm.at[:, r], sems.at[3 + r]) for r in range(QUART)
    ]
    get_seed.start()
    get_field.start()
    get_seed.wait()
    grow_waves(seed_ref, wave_ref, devices, slots)
    get_field.wait()
    flipped_ref[...] = flip_rows(field_ref[...], in_south(), lat_rows)
    put_flipped.start()
    forward_waves(flipped_ref[...], wave_ref, out_ref, put_wave)
    put_flipped.wait()
    for copy in put_wave:
        copy.wait()


def member_sum(value, lat_rows):
    total = value[:lat_rows]
    for member in range(1, value.shape[0] // lat_rows):
        total = total + value[member * lat_rows : (member + 1) * lat_rows]
    return total


def core_select(core, first, second):
    return jnp.where(core == 0, first, second), jnp.where(core == 0, second, first)


def center_body(count, part_rows, spec_ref, wave_ref, logs_ref, inverse_ref, out_ref):
    blurred, total = inverse_waves(spec_ref, wave_ref)
    inverse = (4.0 * math.pi) / total
    clamped = jnp.log(jnp.maximum(blurred * inverse, floor_value))
    center = member_sum(clamped, part_rows) / count
    logs = jnp.concatenate([center] * (clamped.shape[0] // part_rows), axis=0) - clamped
    logs_ref[...] = logs
    forward_waves(jnp.exp(logs), wave_ref, out_ref)
    half = inverse.shape[0] // 2
    own, _ = core_select(lax.axis_index("field"), inverse[:half], inverse[half:])
    parts = [own[at : at + part_rows] for at in range(0, half, part_rows)]
    inverse_ref[...] = jnp.broadcast_to(jnp.concatenate([p for p in parts for _ in range(2)], axis=0), inverse_ref.shape)


def ratio_body(spec_ref, field_ref, inverse_ref, wave_ref, out_ref):
    blurred, _ = inverse_waves(spec_ref, wave_ref)
    scaled = field_ref[...] * inverse_ref[:, 0:1]
    forward_waves(scaled / jnp.maximum(blurred, floor_value), wave_ref, out_ref)


def last_body(count, part_rows, spec_ref, logs_ref, wave_ref, keep_ref, send_ref):
    blurred, _ = inverse_waves(spec_ref, wave_ref)
    clamped = jnp.log(jnp.maximum(blurred, floor_value))
    center = member_sum(logs_ref[...] + clamped, part_rows) / count
    logs = jnp.concatenate([center] * (clamped.shape[0] // part_rows), axis=0) - clamped
    half = logs.shape[0] // 2
    own, other = core_select(lax.axis_index("field"), logs[:half], logs[half:])
    keep_ref[...] = jnp.concatenate([own, center], axis=0)
    send_ref[...] = jnp.concatenate([other, center], axis=0)


def final_body(part_rows, keep_ref, got_ref, center_ref, logs_ref):
    low, high = core_select(lax.axis_index("field"), keep_ref[...], got_ref[...])
    pieces = []
    for at in range(0, low.shape[0], part_rows):
        pieces += [low[at : at + part_rows], high[at : at + part_rows]]
    whole = flip_rows(jnp.concatenate(pieces, axis=0), in_south(), 2 * part_rows)
    rows = logs_ref.shape[0]
    logs_ref[...] = whole[:rows]
    center_ref[...] = jnp.exp(whole[rows:])


def table_rows(degrees, devices, slot):
    return (degrees - devices * slot) // 2


def table_offset(degrees, devices, slot, parity):
    start = sum(2 * table_rows(degrees, devices, s) for s in range(slot))
    return start + parity * table_rows(degrees, devices, slot)


FAR_SLOTS = 3


def table_part(degrees, devices, slot, parity, near_ref, far_ref):
    count = table_rows(degrees, devices, slot)
    offset = table_offset(degrees, devices, slot, parity)
    if slot < FAR_SLOTS:
        return far_ref, offset, count
    return near_ref, offset - table_offset(degrees, devices, FAR_SLOTS, 0), count


def move_far(degrees, devices, slot, src_ref, dst_ref, sems):
    part = (slice(None), pl.ds(table_offset(degrees, devices, slot, 0), 2 * table_rows(degrees, devices, slot)))
    return pltpu.make_async_copy(src_ref.at[part], dst_ref.at[part], sems.at[slot])


def legendre_body(degrees, devices, slots, fixed_hbm, near_ref, far_hbm, weight_ref, fixed_ref, first_coef,
                  second_coef, left_half, right_half, far_ref, sem, far_sems):
    copy = pltpu.make_async_copy(fixed_hbm, fixed_ref, sem)
    copy.start()
    half = (left_half, right_half)
    lanes = 128
    device = device_index()
    order = lax.broadcasted_iota(jnp.int32, (slots, degrees), 0) * devices + device
    level = lax.broadcasted_iota(jnp.int32, (slots, degrees), 1)
    above = level > order
    order, level = order.astype(jnp.float32), level.astype(jnp.float32)
    diff = jnp.maximum(level * level - order * order, 1.0)
    rate = 0.5 * heat_rate / (degrees * (degrees - 1.0))
    first_ratio = jnp.exp(-rate * (2.0 * level))
    second_ratio = jnp.exp(-rate * (4.0 * level - 2.0))
    first_coef[...] = jnp.where(above, jnp.sqrt((4.0 * level * level - 1.0) / diff) * first_ratio, 0.0)
    numer = (2.0 * level + 1.0) * (level + order - 1.0) * (level - order - 1.0)
    denom = jnp.maximum((2.0 * level - 3.0) * diff, 1.0)
    second_coef[...] = jnp.where(above, jnp.sqrt(jnp.maximum(numer, 0.0) / denom) * second_ratio, 0.0)
    copy.wait()

    lane = lax.broadcasted_iota(jnp.int32, (slots, lanes), 1)
    start = jnp.sum(jnp.where(lane == device, fixed_ref[0:slots, 0:lanes], 0.0), axis=1, keepdims=True)
    sub = lax.broadcasted_iota(jnp.int32, (8, lanes), 0)
    tiles = slots // 8
    cosine = [jnp.broadcast_to(fixed_ref[slots : slots + 1, h * lanes : (h + 1) * lanes], (8, lanes)) for h in range(2)]
    log_sine = [jnp.broadcast_to(fixed_ref[slots + 1 : slots + 2, h * lanes : (h + 1) * lanes], (8, lanes)) for h in range(2)]
    order_tile = [(sub + 8 * t) * devices + device for t in range(tiles)]
    zero = jnp.zeros((8, lanes), jnp.float32)
    span_log = 60.0 * math.log(2.0)

    def fresh(tile):
        state = []
        for h in range(2):
            scale_log = start[8 * tile : 8 * tile + 8] + order_tile[tile].astype(jnp.float32) * log_sine[h]
            state.append((zero, zero, scale_log, jnp.exp(scale_log)))
        return state

    def chunk(index, states):
        active = len(states)
        base = pl.multiple_of(index * lanes, lanes)
        first = [first_coef[8 * t : 8 * t + 8, pl.ds(base, lanes)] for t in range(active)]
        second = [second_coef[8 * t : 8 * t + 8, pl.ds(base, lanes)] for t in range(active)]
        states = [list(s) for s in states]
        for k in range(lanes):
            degree = base + k
            for t in range(active):
                a = jnp.broadcast_to(first[t][:, k : k + 1], (8, lanes))
                b = jnp.broadcast_to(second[t][:, k : k + 1], (8, lanes))
                begin = jnp.where(order_tile[t] == degree, 1.0, 0.0)
                for h in range(2):
                    one, two, scale_log, scale = states[t][h]
                    now = (a * cosine[h]) * one + (begin - b * two)
                    half[h][pl.ds(degree * slots + 8 * t, 8), :] = now * scale
                    two, one = one, now
                    if (k + 1) % 8 == 0:
                        large = jnp.maximum(jnp.abs(one), jnp.abs(two)) > 2.0**30
                        factor = jnp.where(large, 2.0**-60, 1.0)
                        one, two = one * factor, two * factor
                        scale_log = scale_log + jnp.where(large, span_log, 0.0)
                        scale = jnp.exp(scale_log)
                    states[t][h] = (one, two, scale_log, scale)
        return states

    states = []
    chunks = degrees // lanes
    for index in range(chunks):
        while len(states) < tiles and 8 * len(states) * devices < (index + 1) * lanes:
            states.append(fresh(len(states)))
        states = chunk(index, states)

    weight_ref[...] = fixed_ref[slots + 2 : slots + 3, :]
    for slot in range(slots):
        for parity in range(2):
            part_ref, offset, count = table_part(degrees, devices, slot, parity, near_ref, far_ref)
            begin = (devices * slot + parity) * slots + slot
            for h in range(2):
                high, low = split_pair(half[h][pl.ds(begin, count, stride=2 * slots), :])
                part_ref[0, offset : offset + count, h * lanes : (h + 1) * lanes] = high
                part_ref[1, offset : offset + count, h * lanes : (h + 1) * lanes] = low
        if slot < FAR_SLOTS:
            move_far(degrees, devices, slot, far_ref, far_hbm, far_sems).start()
    for slot in range(FAR_SLOTS):
        move_far(degrees, devices, slot, far_ref, far_hbm, far_sems).wait()


def gather_orders(spec_ref, sign, fields, lat_groups, lat_rows, members, slots, halved, even_in, odd_in):
    group_lanes = 128 // lat_rows
    width = lat_rows // fields if halved else lat_rows
    for h in range(2):
        even, odd = {}, {}
        for q in range(group_lanes):
            for source in range(fields):
                lat = h * group_lanes + q
                north = spec_ref[lat * fields + source]
                south = spec_ref[(lat_groups - 1 - lat) * fields + source] * sign
                even[q, source] = north + south
                odd[q, source] = north - south
        for field in range(fields):
            for c in range(2 * members):
                row = (field * 2 * members + c) * slots
                part, member = c // members, c % members
                if halved:
                    at = (part * fields * members + field * members + member) * width
                    keys = [(q, source) for q in range(group_lanes) for source in range(fields)]
                else:
                    at = c * width
                    keys = [(q, field) for q in range(group_lanes)]
                cut = slice(at, at + width)
                even_in[h][row : row + slots, :] = jnp.concatenate([even[k][:, cut] for k in keys], axis=1)
                odd_in[h][row : row + slots, :] = jnp.concatenate([odd[k][:, cut] for k in keys], axis=1)


def scatter_orders(out_ref, fields, lat_groups, lat_rows, members, slots, halved, north, south):
    group_lanes = 128 // lat_rows
    width = lat_rows // fields if halved else lat_rows
    for target in range(fields):
        for lat in range(lat_groups // 2):
            h, q = lat // group_lanes, lat % group_lanes
            at = q * lat_rows + (target * width if halved else 0)
            cut = slice(at, at + width)
            owners = range(fields) if halved else [target]
            rows = [
                (field * 2 * members + part * members + member) * slots
                for part in range(2) for field in owners for member in range(members)
            ]
            near = [north[h][row : row + slots, cut] for row in rows]
            far = [south[h][row : row + slots, cut] for row in rows]
            out_ref[lat * fields + target] = jnp.concatenate(near, axis=1)
            out_ref[(lat_groups - 1 - lat) * fields + target] = jnp.concatenate(far, axis=1)


def sphere_body(degrees, devices, slots, lat_groups, lat_rows, members, with_mass, halves_in, halves_out, spec_ref, near_ref, far_in,
                weight_ref, out_ref, *rest):
    far_ref, rest = (rest[0], rest[1:]) if with_mass else (far_in, rest)
    coef_ref, far_sem = rest[:2]
    halves = rest[2:]
    if with_mass:
        get_far = pltpu.make_async_copy(far_in, far_ref, far_sem)
        get_far.start()
    even_in, odd_in, north_out, south_out = halves[0:2], halves[2:4], halves[4:6], halves[6:8]
    device = device_index()
    sign = jnp.where(device % 2 == 0, 1.0, -1.0)
    fields = devices // lat_groups
    per_field = 2 * members
    columns = fields * per_field
    gather_orders(spec_ref, sign, fields, lat_groups, lat_rows, members, slots, halves_in, even_in, odd_in)
    mass = None

    def pick(slot, parity):
        picked = pl.ds(slot, columns, stride=slots)
        gain = 2.0 if slot else jnp.where(device == 0, 1.0, 2.0)
        pair = (even_in, odd_in)[parity]
        values = jnp.concatenate([pair[0][picked, :], pair[1][picked, :]], axis=1)
        return values * (weight_ref[...] * gain)

    def table(slot, parity):
        part_ref, offset, count = table_part(degrees, devices, slot, parity, near_ref, far_ref)
        return part_ref[0, offset : offset + count, :], part_ref[1, offset : offset + count, :], count

    if with_mass:
        mass = jnp.sum(pick(0, 0), axis=1, keepdims=True)

    def analyse(slot):
        for parity in range(2):
            high, low, count = table(slot, parity)
            packed = pair_rows(pick(slot, parity))
            coef = dot_nt(packed, high) + dot_nt(packed, low)
            coef_ref[2 * slot + parity, :, 0:count] = pair_rows(coef[:columns] + coef[columns:])

    def synthesise(slot):
        found = []
        for parity in range(2):
            high, low, count = table(slot, parity)
            packed = coef_ref[2 * slot + parity, :, 0:count]
            back = dot_nn(packed, high) + dot_nn(packed, low)
            found.append(back[:columns] + back[columns:])
        north, south = found[0] + found[1], (found[0] - found[1]) * sign
        if with_mass and slot == 0:
            spread = jnp.broadcast_to(mass, north.shape)
            spread = pltpu.roll(spread, members, 0)
            which = lax.broadcasted_iota(jnp.int32, north.shape, 0) % per_field
            spare = (which >= members) & (device == 0)
            north, south = jnp.where(spare, spread, north), jnp.where(spare, spread, south)
        picked = pl.ds(slot, columns, stride=slots)
        for h in range(2):
            north_out[h][picked, :] = north[:, 128 * h : 128 * h + 128]
            south_out[h][picked, :] = south[:, 128 * h : 128 * h + 128]

    near_slots, far_slots = range(FAR_SLOTS, slots), range(FAR_SLOTS)
    early = FAR_SLOTS + (slots - FAR_SLOTS) // 2 if with_mass else FAR_SLOTS
    for slot in near_slots:
        analyse(slot)
    for slot in range(FAR_SLOTS, early):
        synthesise(slot)
    if with_mass:
        get_far.wait()
    for slot in far_slots:
        analyse(slot)
    for slot in list(range(early, slots)) + list(far_slots):
        synthesise(slot)

    scatter_orders(out_ref, fields, lat_groups, lat_rows, members, slots, halves_out, north_out, south_out)


def on_device_packed(precip):
    lat_groups, fields = lax.axis_size("lat"), lax.axis_size("field")
    devices = lat_groups * fields
    members, lat_rows, lon_total = precip.shape
    lat_total, degrees = lat_rows * lat_groups, lon_total // 2
    slots = degrees // devices
    rows = members * lat_rows
    polar = np.pi * (np.arange(lat_total // 2) + 0.5) / lat_total
    level = np.arange(degrees)
    step = np.arange(1, degrees)
    starts = np.concatenate([[0.0], np.cumsum(np.log((2.0 * step - 1.0) / (2.0 * step)))])
    starts = 0.5 * np.log((2.0 * level + 1.0) / (4.0 * np.pi)) + 0.5 * starts
    starts = starts - 0.5 * heat_rate * level * (level + 1.0) / (degrees * (degrees - 1.0))
    fixed = np.zeros((slots + 8, lat_total // 2), np.float32)
    fixed[:slots, :devices] = starts.reshape(slots, devices)
    fixed[slots] = np.cos(polar)
    fixed[slots + 1] = np.log(np.sin(polar))
    fixed[slots + 2] = np.sin(polar) * (np.pi / lat_total) * (2.0 * np.pi / lon_total)
    fixed = jnp.asarray(fixed)
    wave = jnp.asarray(wave_tables(lon_total, devices, slots))

    vmem = pl.BlockSpec(memory_space=pltpu.VMEM)
    outer = devices // QUART
    spec_shape = jax.ShapeDtypeStruct((outer, QUART, slots, 2 * rows), jnp.float32)
    grid_shape = jax.ShapeDtypeStruct((rows, lon_total), jnp.float32)
    sum_shape = jax.ShapeDtypeStruct((lat_rows, lon_total), jnp.float32)
    far_rows = table_offset(degrees, devices, FAR_SLOTS, 0)
    near_rows = table_offset(degrees, devices, slots, 0) - far_rows
    near_shape = jax.ShapeDtypeStruct((2, near_rows, lat_total // 2), jnp.bfloat16)
    far_shape = jax.ShapeDtypeStruct((2, far_rows, lat_total // 2), jnp.bfloat16)
    flat_shape = jax.ShapeDtypeStruct((devices, slots, 2 * rows), jnp.float32)
    hbm = pl.BlockSpec(memory_space=pl.ANY)

    def call(body, shapes, *operands, name, far=(), far_out=(), scratch=(), cost=None, limit=8):
        single = not isinstance(shapes, tuple)
        shapes = (shapes,) if single else shapes
        outs = [hbm if index in far_out else vmem for index in range(len(shapes))]
        shapes = [
            pltpu.HBM(shape.shape, shape.dtype) if index in far_out else shape for index, shape in enumerate(shapes)
        ]
        specs = [hbm if any(o is f for f in far) else vmem for o in operands]
        operands = [
            pltpu.with_memory_space_constraint(o, pltpu.HBM) if any(o is f for f in far) else o for o in operands
        ]
        return pl.pallas_call(
            body,
            out_shape=shapes[0] if single else shapes,
            in_specs=specs,
            out_specs=outs[0] if single else outs,
            scratch_shapes=list(scratch),
            cost_estimate=cost,
            compiler_params=pltpu.CompilerParams(vmem_limit_bytes=limit << 20),
            name=name,
        )(*operands)

    def exchange(spec):
        flat = spec.reshape(devices, slots, 2 * rows)
        return lax.all_to_all(flat, ("lat", "field"), split_axis=0, concat_axis=0, tiled=True)

    def bind(body, *bound):
        return lambda *refs: body(*bound, *refs)

    def buffer(shape, dtype=jnp.float32):
        return pltpu.VMEM(shape, dtype)

    columns = fields * 2 * members
    signal = pltpu.SemaphoreType.DMA(())

    def sphere(spec, near, far, with_mass, halves_in, halves_out):
        return call(
            bind(sphere_body, degrees, devices, slots, lat_groups, lat_rows, members, with_mass, halves_in,
                 halves_out),
            (flat_shape, far_shape) if with_mass else flat_shape,
            exchange(spec), near, far, weight, far=(far,) if with_mass else (), name="sphere",
            limit=8,
            scratch=[buffer((2 * slots, 2 * columns, 256), jnp.bfloat16), signal]
            + [buffer((columns * slots, 128))] * 8,
        )

    def arrive(spec):
        return exchange(spec).reshape(spec_shape.shape)

    weight_shape = jax.ShapeDtypeStruct((1, lat_total // 2), jnp.float32)
    near, far, weight = call(
        bind(legendre_body, degrees, devices, slots), (near_shape, far_shape, weight_shape), fixed, far=(fixed,), far_out=(1,),
        scratch=[buffer(fixed.shape)] + [buffer((slots, degrees))] * 2 + [buffer((degrees * slots, 128))] * 2
        + [buffer(far_shape.shape, jnp.bfloat16), signal, pltpu.SemaphoreType.DMA((FAR_SLOTS,))],
        cost=pl.CostEstimate(flops=40_000_000, bytes_accessed=16 << 20, transcendentals=0),
        name="legendre", limit=12,
    )
    field = precip.reshape(rows, lon_total)
    seed = jnp.asarray(wave_seeds(lon_total, devices, slots))
    flipped, spec = call(
        bind(first_body, lat_rows, devices, slots), (grid_shape, spec_shape), field, seed, far=(field, seed),
        far_out=(0, 1), name="first",
        scratch=[buffer((rows, lon_total)), buffer(seed.shape), buffer(wave.shape, jnp.bfloat16),
                 buffer((rows, lon_total)), buffer(spec_shape.shape), pltpu.SemaphoreType.DMA((3 + QUART,))],
    )
    spec, far = sphere(spec, near, far, True, False, True)
    count = float(members * fields)
    part_rows = lat_rows // fields
    inverse_shape = jax.ShapeDtypeStruct((rows, 128), jnp.float32)
    logs, inverse, spec = call(
        bind(center_body, count, part_rows), (grid_shape, inverse_shape, spec_shape), arrive(spec), wave, name="center",
    )
    spec = sphere(spec, near, far, False, True, False)
    spec = call(ratio_body, spec_shape, arrive(spec), flipped, inverse, wave, name="ratio")
    spec = sphere(spec, near, far, False, False, True)
    part_shape = jax.ShapeDtypeStruct(((members + 1) * part_rows, lon_total), jnp.float32)
    keep, send = call(
        bind(last_body, count, part_rows), (part_shape, part_shape), arrive(spec), logs, wave, name="last",
    )
    got = lax.ppermute(send, "field", [(0, 1), (1, 0)])
    barycenter, logs = call(bind(final_body, part_rows), (sum_shape, grid_shape), keep, got, name="final")
    return barycenter, logs.reshape(precip.shape)


def fits_packed(mesh, shape):
    lat_groups, fields = mesh.shape["lat"], mesh.shape["field"]
    devices = lat_groups * fields
    field_total, lat_total, lon_total = shape
    degrees = lon_total // 2
    members, lat_rows = field_total // fields, lat_total // lat_groups
    return (
        fields == 2
        and lon_total == 4 * lat_total // 2
        and lat_total == 512
        and 2 * members * lat_rows == 128
        and fields * 2 * members == 8
        and lat_groups % 2 == 0
        and devices % QUART == 0
        and degrees % (8 * devices) == 0
        and (devices // 2) % 16 == 0
        and devices <= 128
    )


def on_device(mesh, precip):
    members, lat_rows, lon_total = precip.shape
    shape = (members * mesh.shape["field"], lat_rows * mesh.shape["lat"], lon_total)
    return on_device_packed(precip) if ITERS == 2 and fits_packed(mesh, shape) else on_device_plain(precip)


def solution(mesh):
    in_specs = (P("field", "lat", None),)
    out_specs = (P("lat", None), P("field", "lat", None))
    return jax.shard_map(
        lambda precip: on_device(mesh, precip),
        mesh=mesh, in_specs=in_specs, out_specs=out_specs, check_vma=False,
    )
```

```python
import math

import jax
import jax.numpy as jnp
import ml_dtypes
import numpy as np
from jax import lax
from jax.experimental import pallas as pl
from jax.experimental.pallas import tpu as pltpu
from jax.sharding import PartitionSpec as P

ITERS = 2


heat_rate = 2.0
floor_value = 0.1


def colatitudes(lat_total):
    index_rows = jnp.arange(lat_total, dtype=jnp.float32)
    return jnp.pi * (index_rows + 0.5) / lat_total


def quad_weights(lat_total, lon_total):
    polar_angle = colatitudes(lat_total)
    return jnp.sin(polar_angle) * (jnp.pi / lat_total) * (2.0 * jnp.pi / lon_total)


def heat_factors(degrees):
    level = jnp.arange(degrees, dtype=jnp.float32)
    return jnp.exp(-heat_rate * level * (level + 1.0) / (degrees * (degrees - 1.0)))


def legendre_north(orders, lat_total, degrees):
    half_rows = lat_total // 2
    polar_angle = colatitudes(lat_total)[:half_rows]
    cosine = jnp.cos(polar_angle)
    log_sine = jnp.log(jnp.sin(polar_angle))
    order_value = orders.astype(jnp.float32)
    step_count = jnp.arange(1, degrees + 1, dtype=jnp.float32)
    log_ratios = jnp.log((2.0 * step_count - 1.0) / (2.0 * step_count))
    within = step_count[None, :] <= order_value[:, None]
    partial_log = jnp.sum(jnp.where(within, log_ratios[None, :], 0.0), axis=1)
    log_start = 0.5 * jnp.log((2.0 * order_value + 1.0) / (4.0 * jnp.pi)) + 0.5 * partial_log
    start_log = log_start[:, None] + order_value[:, None] * log_sine[None, :]
    span_size = min(32, degrees)

    def advance(state, block_start):
        prev_one, prev_two, log_scale = state
        collected = []
        for offset in range(span_size):
            degree = (block_start + offset).astype(jnp.float32)
            safe_diff = jnp.maximum(degree * degree - order_value * order_value, 1.0)
            first_factor = jnp.sqrt((4.0 * degree * degree - 1.0) / safe_diff)
            numerator = (
                (2.0 * degree + 1.0) * (degree + order_value - 1.0) * (degree - order_value - 1.0)
            )
            denominator = jnp.maximum((2.0 * degree - 3.0) * safe_diff, 1.0)
            second_factor = jnp.sqrt(jnp.maximum(numerator, 0.0) / denominator)
            recurred = (
                first_factor[:, None] * cosine[None, :] * prev_one
                - second_factor[:, None] * prev_two
            )
            current = jnp.where(
                (degree > order_value)[:, None],
                recurred,
                jnp.where(
                    (degree == order_value)[:, None],
                    jnp.ones_like(recurred),
                    jnp.zeros_like(recurred),
                ),
            )
            collected.append(current * jnp.exp(log_scale))
            prev_two = prev_one
            prev_one = current
            if (offset + 1) % 8 == 0:
                magnitude = jnp.maximum(jnp.abs(prev_one), jnp.abs(prev_two))
                safe_size = jnp.where(magnitude > 0.0, magnitude, jnp.ones_like(magnitude))
                prev_one = prev_one / safe_size
                prev_two = prev_two / safe_size
                log_scale = log_scale + jnp.log(safe_size)
        return ((prev_one, prev_two, log_scale), jnp.stack(collected))

    empty_state = jnp.zeros((orders.shape[0], half_rows), jnp.float32)
    block_starts = jnp.arange(0, degrees, span_size, dtype=jnp.int32)
    final_state, stacked = lax.scan(advance, (empty_state, empty_state, start_log), block_starts)
    legendre = stacked.reshape(degrees, orders.shape[0], half_rows)
    return jnp.transpose(legendre, (1, 2, 0))


def fourier_tables(lon_total, degrees, groups):
    per_group = degrees // groups
    column = jnp.arange(2 * degrees, dtype=jnp.int32)
    group_index = column // (2 * per_group)
    within_group = column % (2 * per_group)
    part_index = within_group // per_group
    order_index = group_index * per_group + within_group % per_group
    points = jnp.arange(lon_total, dtype=jnp.int32)
    phase = (points[:, None] * order_index[None, :] % lon_total).astype(jnp.float32) * (
        2.0 * jnp.pi / lon_total
    )
    forward = jnp.where(part_index[None, :] == 0, jnp.cos(phase), -jnp.sin(phase))
    doubled = jnp.where(order_index == 0, 1.0, 2.0)
    backward = jnp.transpose(forward) * doubled[:, None]
    return (forward, backward)


def on_device_plain(precip):
    groups = lax.axis_size("lat")
    lat_index = lax.axis_index("lat")
    local_fields, lat_rows, lon_total = precip.shape
    lat_total = lat_rows * groups
    degrees = lon_total // 2
    orders_here = degrees // groups
    half_rows = lat_total // 2
    count_fields = local_fields * lax.axis_size("field")
    weights_all = quad_weights(lat_total, lon_total)
    local_weights = lax.dynamic_slice_in_dim(weights_all, lat_index * lat_rows, lat_rows)
    forward, backward = fourier_tables(lon_total, degrees, groups)
    heat_factor = heat_factors(degrees)
    orders = lat_index * orders_here + jnp.arange(orders_here, dtype=jnp.int32)
    north_table = legendre_north(orders, lat_total, degrees)
    paired = north_table.reshape(orders_here, half_rows, degrees // 2, 2)
    parity = (orders % 2 == 0)[:, None, None]
    even_table = jnp.where(parity, paired[..., 0], paired[..., 1])
    odd_table = jnp.where(parity, paired[..., 1], paired[..., 0])
    heat_paired = heat_factor.reshape(degrees // 2, 2)
    heat_even = jnp.where(parity[:, :, 0], heat_paired[None, :, 0], heat_paired[None, :, 1])
    heat_odd = jnp.where(parity[:, :, 0], heat_paired[None, :, 1], heat_paired[None, :, 0])
    weights_north = weights_all[:half_rows]

    def legendre_pass(spread):
        count_here = spread.shape[0]
        shaped = spread.reshape(count_here, lat_total, 2, orders_here)
        north_part = shaped[:, :half_rows]
        south_part = jnp.flip(shaped[:, half_rows:], axis=1)
        even_input = (north_part + south_part) * weights_north[None, :, None, None]
        odd_input = (north_part - south_part) * weights_north[None, :, None, None]
        even_coef = jnp.einsum(
            "mjk,fjpm->mfpk", even_table, even_input, precision=lax.Precision.HIGHEST
        )
        odd_coef = jnp.einsum(
            "mjk,fjpm->mfpk", odd_table, odd_input, precision=lax.Precision.HIGHEST
        )
        even_coef = even_coef * heat_even[:, None, None, :]
        odd_coef = odd_coef * heat_odd[:, None, None, :]
        even_sum = jnp.einsum(
            "mjk,mfpk->fjpm", even_table, even_coef, precision=lax.Precision.HIGHEST
        )
        odd_sum = jnp.einsum("mjk,mfpk->fjpm", odd_table, odd_coef, precision=lax.Precision.HIGHEST)
        result = jnp.concatenate([even_sum + odd_sum, jnp.flip(even_sum - odd_sum, axis=1)], axis=1)
        return result.reshape(count_here, lat_total, 2 * orders_here)

    def kernel_apply_step(fields):
        spectra = jnp.einsum("fjk,kc->fjc", fields, forward, precision=lax.Precision.HIGHEST)

        def one_member(carry, member_spectra):
            spread = lax.all_to_all(member_spectra, "lat", split_axis=1, concat_axis=0, tiled=True)
            filtered = legendre_pass(spread[None])
            returned = lax.all_to_all(filtered[0], "lat", split_axis=0, concat_axis=1, tiled=True)
            return (carry, returned)

        unused, gathered = lax.scan(one_member, jnp.zeros((), jnp.float32), spectra)
        return jnp.einsum("fjc,ck->fjk", gathered, backward, precision=lax.Precision.HIGHEST)

    partial_value = jnp.sum(precip * local_weights[None, :, None], axis=(1, 2))
    masses = lax.psum(partial_value, "lat") / (4.0 * jnp.pi)
    scaling_logs = jnp.zeros(precip.shape, jnp.float32)
    log_barycenter = jnp.zeros(precip.shape[1:], jnp.float32)
    scaled = precip / masses[:, None, None]
    ratio_field = scaled
    for sweep in range(ITERS):
        smoothed = kernel_apply_step(ratio_field)
        clamped_values = jnp.log(jnp.maximum(smoothed, floor_value))
        added_total = lax.psum(jnp.sum(scaling_logs + clamped_values, axis=0), "field")
        log_barycenter = added_total / count_fields
        scaling_logs = log_barycenter[None] - clamped_values
        if sweep + 1 < ITERS:
            blurred_scale = kernel_apply_step(jnp.exp(scaling_logs))
            ratio_field = scaled / jnp.maximum(blurred_scale, floor_value)
    return (jnp.exp(log_barycenter), scaling_logs)


QUART = 4


def split_pair(value):
    high = value.astype(jnp.bfloat16)
    low = (value - high.astype(jnp.float32)).astype(jnp.bfloat16)
    return high, low


def pair_rows(value):
    high, low = split_pair(value)
    return jnp.concatenate([high, low], axis=0)


def dot_nt(left, right):
    return lax.dot_general(left, right, (((1,), (1,)), ((), ())), preferred_element_type=jnp.float32)


def dot_nn(left, right):
    return lax.dot_general(left, right, (((1,), (0,)), ((), ())), preferred_element_type=jnp.float32)


def wave_tables(lon_total, devices, slots):
    span = lon_total // QUART
    residue = np.arange(QUART)[:, None, None]
    order = residue + QUART * np.arange(devices // QUART)[None, :, None]
    order = (order + devices * np.arange(slots)[None, None, :]).reshape(QUART, -1)
    phase = (order[:, :, None] * np.arange(span)[None, None, :] % lon_total) * (2.0 * np.pi / lon_total)
    table = np.concatenate([np.cos(phase), np.sin(phase)], axis=1).astype(np.float32)
    high = table.astype(ml_dtypes.bfloat16)
    low = (table - high.astype(np.float32)).astype(ml_dtypes.bfloat16)
    return np.stack([high, low])


def wave_seeds(lon_total, devices, slots):
    span = lon_total // QUART
    first = (np.arange(QUART)[:, None] + QUART * np.arange(devices // QUART)[None, :]).reshape(-1)
    phases = [
        orders[:, None] * np.arange(span)[None, :] % lon_total * (2.0 * np.pi / lon_total)
        for orders in (first, devices * np.arange(slots))
    ]
    return np.concatenate([f(p) for p in phases for f in (np.cos, np.sin)]).astype(np.float32)


def grow_waves(seed_ref, wave_ref, devices, slots):
    orders = wave_ref.shape[2] // 2
    step_cos = seed_ref[2 * devices : 2 * devices + slots, :]
    step_sin = seed_ref[2 * devices + slots : 2 * devices + 2 * slots, :]
    for row in range(devices):
        residue, at = row // (devices // QUART), row % (devices // QUART) * slots
        cosine, sine = seed_ref[row : row + 1, :], seed_ref[devices + row : devices + row + 1, :]
        for place, value in (
            (at, cosine * step_cos - sine * step_sin),
            (orders + at, sine * step_cos + cosine * step_sin),
        ):
            high, low = split_pair(value)
            wave_ref[0, residue, place : place + slots, :] = high
            wave_ref[1, residue, place : place + slots, :] = low


def forward_waves(field, wave_ref, out_ref, done=None):
    span = field.shape[1] // QUART
    rows = field.shape[0]
    lanes = 2 * rows
    part = [field[:, q * span : (q + 1) * span] for q in range(QUART)]
    sum_even, sum_odd = part[0] + part[2], part[1] + part[3]
    diff_even, diff_odd = part[0] - part[2], part[1] - part[3]
    stack_even = pair_rows(jnp.concatenate([sum_even + sum_odd, sum_even - sum_odd], axis=0))
    stack_odd = pair_rows(jnp.concatenate([diff_even, diff_odd], axis=0))
    orders = wave_ref.shape[2] // 2
    first = lax.broadcasted_iota(jnp.int32, (orders, lanes), 1) < rows
    for residue in range(QUART):
        stack = stack_odd if residue % 2 else stack_even
        found = dot_nt(wave_ref[0, residue], stack) + dot_nt(wave_ref[1, residue], stack)
        found = found[:, :lanes] + found[:, lanes:]
        cosine, sine = found[:orders], found[orders:]
        if residue == 0:
            packed = jnp.where(first, cosine, -pltpu.roll(sine, rows, 1))
        elif residue == 2:
            packed = jnp.where(first, pltpu.roll(cosine, rows, 1), -sine)
        elif residue == 1:
            packed = jnp.where(first, cosine, -cosine) - pltpu.roll(sine, rows, 1)
        else:
            turned = pltpu.roll(sine, rows, 1)
            packed = cosine + jnp.where(first, turned, -turned)
        out_ref[:, residue] = packed.reshape(out_ref.shape[0], out_ref.shape[2], lanes)
        if done:
            done[residue].start()


def inverse_waves(spec_ref, wave_ref):
    outer, _, slots, lanes = spec_ref.shape
    rows = lanes // 2
    real = [None] * QUART
    cross = {}
    spare = None
    for residue in range(QUART):
        turned = jnp.transpose(spec_ref[:, residue].reshape(outer * slots, lanes))
        cosine, sine = turned[:rows], turned[rows:]
        if residue == 0:
            spare = sine[:, 0:1]
        left = jnp.concatenate([cosine, -sine], axis=1)
        if residue % 2:
            left = jnp.concatenate([left, jnp.concatenate([sine, cosine], axis=1)], axis=0)
        count = left.shape[0]
        left = pair_rows(left)
        found = dot_nn(left, wave_ref[0, residue]) + dot_nn(left, wave_ref[1, residue])
        found = found[:count] + found[count:]
        real[residue] = found[:rows]
        if residue % 2:
            cross[residue] = found[rows:]
    plus, minus = real[0] + real[2], real[0] - real[2]
    both, gap = real[1] + real[3], cross[1] - cross[3]
    return jnp.concatenate([plus + both, minus - gap, plus - both, minus + gap], axis=1), spare


def flip_rows(value, south, lat_rows):
    lanes = 128
    rows, width = value.shape
    sub = lax.broadcasted_iota(jnp.int32, (8, lanes), 0)
    source = jnp.where(south, 7 - sub, sub)
    blocks = lat_rows // 8
    out = []
    for base in range(0, rows, lat_rows):
        for block in range(blocks):
            near = value[base + 8 * block : base + 8 * block + 8]
            far = value[base + 8 * (blocks - 1 - block) : base + 8 * (blocks - block)]
            tile = jnp.where(south, far, near)
            pieces = [
                jnp.take_along_axis(tile[:, at : at + lanes], source, axis=0) for at in range(0, width, lanes)
            ]
            out.append(jnp.concatenate(pieces, axis=1))
    return jnp.concatenate(out, axis=0)


def device_index():
    return lax.axis_index("lat") * lax.axis_size("field") + lax.axis_index("field")


def in_south():
    return lax.axis_index("lat") >= lax.axis_size("lat") // 2


def first_body(lat_rows, devices, slots, field_hbm, seed_hbm, flipped_hbm, out_hbm, field_ref, seed_ref, wave_ref,
               flipped_ref, out_ref, sems):
    get_field = pltpu.make_async_copy(field_hbm, field_ref, sems.at[0])
    get_seed = pltpu.make_async_copy(seed_hbm, seed_ref, sems.at[1])
    put_flipped = pltpu.make_async_copy(flipped_ref, flipped_hbm, sems.at[2])
    put_wave = [
        pltpu.make_async_copy(out_ref.at[:, r], out_hbm.at[:, r], sems.at[3 + r]) for r in range(QUART)
    ]
    get_seed.start()
    get_field.start()
    get_seed.wait()
    grow_waves(seed_ref, wave_ref, devices, slots)
    get_field.wait()
    flipped_ref[...] = flip_rows(field_ref[...], in_south(), lat_rows)
    put_flipped.start()
    forward_waves(flipped_ref[...], wave_ref, out_ref, put_wave)
    put_flipped.wait()
    for copy in put_wave:
        copy.wait()


def member_sum(value, lat_rows):
    total = value[:lat_rows]
    for member in range(1, value.shape[0] // lat_rows):
        total = total + value[member * lat_rows : (member + 1) * lat_rows]
    return total


def core_select(core, first, second):
    return jnp.where(core == 0, first, second), jnp.where(core == 0, second, first)


def center_body(count, part_rows, spec_ref, wave_ref, logs_ref, inverse_ref, out_ref):
    blurred, total = inverse_waves(spec_ref, wave_ref)
    inverse = (4.0 * math.pi) / total
    clamped = jnp.log(jnp.maximum(blurred * inverse, floor_value))
    center = member_sum(clamped, part_rows) / count
    logs = jnp.concatenate([center] * (clamped.shape[0] // part_rows), axis=0) - clamped
    logs_ref[...] = logs
    forward_waves(jnp.exp(logs), wave_ref, out_ref)
    half = inverse.shape[0] // 2
    own, _ = core_select(lax.axis_index("field"), inverse[:half], inverse[half:])
    parts = [own[at : at + part_rows] for at in range(0, half, part_rows)]
    inverse_ref[...] = jnp.broadcast_to(jnp.concatenate([p for p in parts for _ in range(2)], axis=0), inverse_ref.shape)


def ratio_body(spec_ref, field_ref, inverse_ref, wave_ref, out_ref):
    blurred, _ = inverse_waves(spec_ref, wave_ref)
    scaled = field_ref[...] * inverse_ref[:, 0:1]
    forward_waves(scaled / jnp.maximum(blurred, floor_value), wave_ref, out_ref)


def last_body(count, part_rows, spec_ref, logs_ref, wave_ref, keep_ref, send_ref):
    blurred, _ = inverse_waves(spec_ref, wave_ref)
    clamped = jnp.log(jnp.maximum(blurred, floor_value))
    center = member_sum(logs_ref[...] + clamped, part_rows) / count
    logs = jnp.concatenate([center] * (clamped.shape[0] // part_rows), axis=0) - clamped
    half = logs.shape[0] // 2
    own, other = core_select(lax.axis_index("field"), logs[:half], logs[half:])
    keep_ref[...] = jnp.concatenate([own, center], axis=0)
    send_ref[...] = jnp.concatenate([other, center], axis=0)


def final_body(part_rows, keep_ref, got_ref, center_ref, logs_ref):
    low, high = core_select(lax.axis_index("field"), keep_ref[...], got_ref[...])
    pieces = []
    for at in range(0, low.shape[0], part_rows):
        pieces += [low[at : at + part_rows], high[at : at + part_rows]]
    whole = flip_rows(jnp.concatenate(pieces, axis=0), in_south(), 2 * part_rows)
    rows = logs_ref.shape[0]
    logs_ref[...] = whole[:rows]
    center_ref[...] = jnp.exp(whole[rows:])


def table_rows(degrees, devices, slot):
    return (degrees - devices * slot) // 2


def table_offset(degrees, devices, slot, parity):
    start = sum(2 * table_rows(degrees, devices, s) for s in range(slot))
    return start + parity * table_rows(degrees, devices, slot)


FAR_SLOTS = 3


def table_part(degrees, devices, slot, parity, near_ref, far_ref):
    count = table_rows(degrees, devices, slot)
    offset = table_offset(degrees, devices, slot, parity)
    if slot < FAR_SLOTS:
        return far_ref, offset, count
    return near_ref, offset - table_offset(degrees, devices, FAR_SLOTS, 0), count


def move_far(degrees, devices, slot, src_ref, dst_ref, sems):
    part = (slice(None), pl.ds(table_offset(degrees, devices, slot, 0), 2 * table_rows(degrees, devices, slot)))
    return pltpu.make_async_copy(src_ref.at[part], dst_ref.at[part], sems.at[slot])


def legendre_body(degrees, devices, slots, fixed_hbm, near_ref, far_hbm, weight_ref, fixed_ref, first_coef,
                  second_coef, left_half, right_half, far_ref, sem, far_sems):
    copy = pltpu.make_async_copy(fixed_hbm, fixed_ref, sem)
    copy.start()
    half = (left_half, right_half)
    lanes = 128
    device = device_index()
    order = lax.broadcasted_iota(jnp.int32, (slots, degrees), 0) * devices + device
    level = lax.broadcasted_iota(jnp.int32, (slots, degrees), 1)
    above = level > order
    order, level = order.astype(jnp.float32), level.astype(jnp.float32)
    diff = jnp.maximum(level * level - order * order, 1.0)
    rate = 0.5 * heat_rate / (degrees * (degrees - 1.0))
    first_ratio = jnp.exp(-rate * (2.0 * level))
    second_ratio = jnp.exp(-rate * (4.0 * level - 2.0))
    first_coef[...] = jnp.where(above, jnp.sqrt((4.0 * level * level - 1.0) / diff) * first_ratio, 0.0)
    numer = (2.0 * level + 1.0) * (level + order - 1.0) * (level - order - 1.0)
    denom = jnp.maximum((2.0 * level - 3.0) * diff, 1.0)
    second_coef[...] = jnp.where(above, jnp.sqrt(jnp.maximum(numer, 0.0) / denom) * second_ratio, 0.0)
    copy.wait()

    lane = lax.broadcasted_iota(jnp.int32, (slots, lanes), 1)
    start = jnp.sum(jnp.where(lane == device, fixed_ref[0:slots, 0:lanes], 0.0), axis=1, keepdims=True)
    sub = lax.broadcasted_iota(jnp.int32, (8, lanes), 0)
    tiles = slots // 8
    cosine = [jnp.broadcast_to(fixed_ref[slots : slots + 1, h * lanes : (h + 1) * lanes], (8, lanes)) for h in range(2)]
    log_sine = [jnp.broadcast_to(fixed_ref[slots + 1 : slots + 2, h * lanes : (h + 1) * lanes], (8, lanes)) for h in range(2)]
    order_tile = [(sub + 8 * t) * devices + device for t in range(tiles)]
    zero = jnp.zeros((8, lanes), jnp.float32)
    span_log = 60.0 * math.log(2.0)

    def fresh(tile):
        state = []
        for h in range(2):
            scale_log = start[8 * tile : 8 * tile + 8] + order_tile[tile].astype(jnp.float32) * log_sine[h]
            state.append((zero, zero, scale_log, jnp.exp(scale_log)))
        return state

    def chunk(index, states):
        active = len(states)
        base = pl.multiple_of(index * lanes, lanes)
        first = [first_coef[8 * t : 8 * t + 8, pl.ds(base, lanes)] for t in range(active)]
        second = [second_coef[8 * t : 8 * t + 8, pl.ds(base, lanes)] for t in range(active)]
        states = [list(s) for s in states]
        for k in range(lanes):
            degree = base + k
            for t in range(active):
                a = jnp.broadcast_to(first[t][:, k : k + 1], (8, lanes))
                b = jnp.broadcast_to(second[t][:, k : k + 1], (8, lanes))
                begin = jnp.where(order_tile[t] == degree, 1.0, 0.0)
                for h in range(2):
                    one, two, scale_log, scale = states[t][h]
                    now = (a * cosine[h]) * one + (begin - b * two)
                    half[h][pl.ds(degree * slots + 8 * t, 8), :] = now * scale
                    two, one = one, now
                    if (k + 1) % 8 == 0:
                        large = jnp.maximum(jnp.abs(one), jnp.abs(two)) > 2.0**30
                        factor = jnp.where(large, 2.0**-60, 1.0)
                        one, two = one * factor, two * factor
                        scale_log = scale_log + jnp.where(large, span_log, 0.0)
                        scale = jnp.exp(scale_log)
                    states[t][h] = (one, two, scale_log, scale)
        return states

    states = []
    chunks = degrees // lanes
    for index in range(chunks):
        while len(states) < tiles and 8 * len(states) * devices < (index + 1) * lanes:
            states.append(fresh(len(states)))
        states = chunk(index, states)

    weight_ref[...] = fixed_ref[slots + 2 : slots + 3, :]
    for slot in range(slots):
        for parity in range(2):
            part_ref, offset, count = table_part(degrees, devices, slot, parity, near_ref, far_ref)
            begin = (devices * slot + parity) * slots + slot
            for h in range(2):
                high, low = split_pair(half[h][pl.ds(begin, count, stride=2 * slots), :])
                part_ref[0, offset : offset + count, h * lanes : (h + 1) * lanes] = high
                part_ref[1, offset : offset + count, h * lanes : (h + 1) * lanes] = low
        if slot < FAR_SLOTS:
            move_far(degrees, devices, slot, far_ref, far_hbm, far_sems).start()
    for slot in range(FAR_SLOTS):
        move_far(degrees, devices, slot, far_ref, far_hbm, far_sems).wait()


def weave(first, second, width):
    lanes = first.shape[-1]
    even = lax.broadcasted_iota(jnp.int32, first.shape, first.ndim - 1) // width % 2 == 0
    axis = first.ndim - 1
    return (
        jnp.where(even, first, pltpu.roll(second, width, axis)),
        jnp.where(even, pltpu.roll(first, lanes - width, axis), second),
    )


def gather_orders(spec_ref, sign, fields, lat_groups, lat_rows, members, slots, halved, even_in, odd_in):
    group_lanes = 128 // lat_rows
    for h in range(2):
        even, odd = [], []
        for q in range(group_lanes):
            lat = h * group_lanes + q
            pair = ([], [])
            for source in range(fields):
                north = spec_ref[lat * fields + source]
                south = spec_ref[(lat_groups - 1 - lat) * fields + source] * sign
                pair[0].append(north + south)
                pair[1].append(north - south)
            if halved:
                pair = [weave(*p, lat_rows // 2) for p in pair]
            even.append(pair[0])
            odd.append(pair[1])
        for field in range(fields):
            for c in range(2 * members):
                row = (field * 2 * members + c) * slots
                part, member = c // members, c % members
                block, at = (member, part * fields + field) if halved else (field, c)
                cut = slice(at * lat_rows, (at + 1) * lat_rows)
                even_in[h][row : row + slots, :] = jnp.concatenate([e[block][:, cut] for e in even], axis=1)
                odd_in[h][row : row + slots, :] = jnp.concatenate([o[block][:, cut] for o in odd], axis=1)


def scatter_orders(out_ref, fields, lat_groups, lat_rows, members, slots, halved, north, south):
    group_lanes = 128 // lat_rows
    for lat in range(lat_groups // 2):
        h, q = lat // group_lanes, lat % group_lanes
        cut = slice(q * lat_rows, (q + 1) * lat_rows)
        for source, place in ((north, lat), (south, lat_groups - 1 - lat)):
            blocks = []
            for block in range(2):
                if halved:
                    owners = [(field, part, block) for part in range(2) for field in range(fields)]
                else:
                    owners = [(block, part, member) for part in range(2) for member in range(members)]
                rows = [((field * 2 + part) * members + member) * slots for field, part, member in owners]
                blocks.append(jnp.concatenate([source[h][row : row + slots, cut] for row in rows], axis=1))
            if halved:
                blocks = weave(*blocks, lat_rows // 2)
            out_ref[place * fields], out_ref[place * fields + 1] = blocks


def sphere_body(degrees, devices, slots, lat_groups, lat_rows, members, with_mass, halves_in, halves_out, spec_ref, near_ref, far_in,
                weight_ref, out_ref, *rest):
    far_ref, rest = (rest[0], rest[1:]) if with_mass else (far_in, rest)
    coef_ref, far_sem = rest[:2]
    halves = rest[2:]
    if with_mass:
        get_far = pltpu.make_async_copy(far_in, far_ref, far_sem)
        get_far.start()
    even_in, odd_in, north_out, south_out = halves[0:2], halves[2:4], halves[4:6], halves[6:8]
    device = device_index()
    sign = jnp.where(device % 2 == 0, 1.0, -1.0)
    fields = devices // lat_groups
    per_field = 2 * members
    columns = fields * per_field
    gather_orders(spec_ref, sign, fields, lat_groups, lat_rows, members, slots, halves_in, even_in, odd_in)
    mass = None

    def pick(slot, parity):
        picked = pl.ds(slot, columns, stride=slots)
        gain = 2.0 if slot else jnp.where(device == 0, 1.0, 2.0)
        pair = (even_in, odd_in)[parity]
        values = jnp.concatenate([pair[0][picked, :], pair[1][picked, :]], axis=1)
        return values * (weight_ref[...] * gain)

    def table(slot, parity):
        part_ref, offset, count = table_part(degrees, devices, slot, parity, near_ref, far_ref)
        return part_ref[0, offset : offset + count, :], part_ref[1, offset : offset + count, :], count

    if with_mass:
        mass = jnp.sum(pick(0, 0), axis=1, keepdims=True)

    def analyse(slot):
        for parity in range(2):
            high, low, count = table(slot, parity)
            packed = pair_rows(pick(slot, parity))
            coef = dot_nt(packed, high) + dot_nt(packed, low)
            coef_ref[2 * slot + parity, :, 0:count] = pair_rows(coef[:columns] + coef[columns:])

    def synthesise(slot):
        found = []
        for parity in range(2):
            high, low, count = table(slot, parity)
            packed = coef_ref[2 * slot + parity, :, 0:count]
            back = dot_nn(packed, high) + dot_nn(packed, low)
            found.append(back[:columns] + back[columns:])
        north, south = found[0] + found[1], (found[0] - found[1]) * sign
        if with_mass and slot == 0:
            spread = jnp.broadcast_to(mass, north.shape)
            spread = pltpu.roll(spread, members, 0)
            which = lax.broadcasted_iota(jnp.int32, north.shape, 0) % per_field
            spare = (which >= members) & (device == 0)
            north, south = jnp.where(spare, spread, north), jnp.where(spare, spread, south)
        picked = pl.ds(slot, columns, stride=slots)
        for h in range(2):
            north_out[h][picked, :] = north[:, 128 * h : 128 * h + 128]
            south_out[h][picked, :] = south[:, 128 * h : 128 * h + 128]

    near_slots, far_slots = range(FAR_SLOTS, slots), range(FAR_SLOTS)
    early = slots if with_mass else FAR_SLOTS
    for slot in near_slots:
        analyse(slot)
    for slot in range(FAR_SLOTS, early):
        synthesise(slot)
    if with_mass:
        get_far.wait()
    for slot in far_slots:
        analyse(slot)
    for slot in list(range(early, slots)) + list(far_slots):
        synthesise(slot)

    scatter_orders(out_ref, fields, lat_groups, lat_rows, members, slots, halves_out, north_out, south_out)


def on_device_packed(precip):
    lat_groups, fields = lax.axis_size("lat"), lax.axis_size("field")
    devices = lat_groups * fields
    members, lat_rows, lon_total = precip.shape
    lat_total, degrees = lat_rows * lat_groups, lon_total // 2
    slots = degrees // devices
    rows = members * lat_rows
    polar = np.pi * (np.arange(lat_total // 2) + 0.5) / lat_total
    level = np.arange(degrees)
    step = np.arange(1, degrees)
    starts = np.concatenate([[0.0], np.cumsum(np.log((2.0 * step - 1.0) / (2.0 * step)))])
    starts = 0.5 * np.log((2.0 * level + 1.0) / (4.0 * np.pi)) + 0.5 * starts
    starts = starts - 0.5 * heat_rate * level * (level + 1.0) / (degrees * (degrees - 1.0))
    fixed = np.zeros((slots + 8, lat_total // 2), np.float32)
    fixed[:slots, :devices] = starts.reshape(slots, devices)
    fixed[slots] = np.cos(polar)
    fixed[slots + 1] = np.log(np.sin(polar))
    fixed[slots + 2] = np.sin(polar) * (np.pi / lat_total) * (2.0 * np.pi / lon_total)
    fixed = jnp.asarray(fixed)
    wave = jnp.asarray(wave_tables(lon_total, devices, slots))

    vmem = pl.BlockSpec(memory_space=pltpu.VMEM)
    outer = devices // QUART
    spec_shape = jax.ShapeDtypeStruct((outer, QUART, slots, 2 * rows), jnp.float32)
    grid_shape = jax.ShapeDtypeStruct((rows, lon_total), jnp.float32)
    sum_shape = jax.ShapeDtypeStruct((lat_rows, lon_total), jnp.float32)
    far_rows = table_offset(degrees, devices, FAR_SLOTS, 0)
    near_rows = table_offset(degrees, devices, slots, 0) - far_rows
    near_shape = jax.ShapeDtypeStruct((2, near_rows, lat_total // 2), jnp.bfloat16)
    far_shape = jax.ShapeDtypeStruct((2, far_rows, lat_total // 2), jnp.bfloat16)
    flat_shape = jax.ShapeDtypeStruct((devices, slots, 2 * rows), jnp.float32)
    hbm = pl.BlockSpec(memory_space=pl.ANY)

    def call(body, shapes, *operands, name, far=(), far_out=(), scratch=(), cost=None, limit=8):
        single = not isinstance(shapes, tuple)
        shapes = (shapes,) if single else shapes
        outs = [hbm if index in far_out else vmem for index in range(len(shapes))]
        shapes = [
            pltpu.HBM(shape.shape, shape.dtype) if index in far_out else shape for index, shape in enumerate(shapes)
        ]
        specs = [hbm if any(o is f for f in far) else vmem for o in operands]
        operands = [
            pltpu.with_memory_space_constraint(o, pltpu.HBM) if any(o is f for f in far) else o for o in operands
        ]
        return pl.pallas_call(
            body,
            out_shape=shapes[0] if single else shapes,
            in_specs=specs,
            out_specs=outs[0] if single else outs,
            scratch_shapes=list(scratch),
            cost_estimate=cost,
            compiler_params=pltpu.CompilerParams(vmem_limit_bytes=limit << 20),
            name=name,
        )(*operands)

    def exchange(spec):
        flat = spec.reshape(devices, slots, 2 * rows)
        return lax.all_to_all(flat, ("lat", "field"), split_axis=0, concat_axis=0, tiled=True)

    def bind(body, *bound):
        return lambda *refs: body(*bound, *refs)

    def buffer(shape, dtype=jnp.float32):
        return pltpu.VMEM(shape, dtype)

    columns = fields * 2 * members
    signal = pltpu.SemaphoreType.DMA(())

    def sphere(spec, near, far, with_mass, halves_in, halves_out):
        return call(
            bind(sphere_body, degrees, devices, slots, lat_groups, lat_rows, members, with_mass, halves_in,
                 halves_out),
            (flat_shape, far_shape) if with_mass else flat_shape,
            exchange(spec), near, far, weight, far=(far,) if with_mass else (), name="sphere",
            limit=8,
            scratch=[buffer((2 * slots, 2 * columns, 256), jnp.bfloat16), signal]
            + [buffer((columns * slots, 128))] * 8,
        )

    def arrive(spec):
        return exchange(spec).reshape(spec_shape.shape)

    weight_shape = jax.ShapeDtypeStruct((1, lat_total // 2), jnp.float32)
    near, far, weight = call(
        bind(legendre_body, degrees, devices, slots), (near_shape, far_shape, weight_shape), fixed, far=(fixed,), far_out=(1,),
        scratch=[buffer(fixed.shape)] + [buffer((slots, degrees))] * 2 + [buffer((degrees * slots, 128))] * 2
        + [buffer(far_shape.shape, jnp.bfloat16), signal, pltpu.SemaphoreType.DMA((FAR_SLOTS,))],
        cost=pl.CostEstimate(flops=40_000_000, bytes_accessed=16 << 20, transcendentals=0),
        name="legendre", limit=12,
    )
    field = precip.reshape(rows, lon_total)
    seed = jnp.asarray(wave_seeds(lon_total, devices, slots))
    flipped, spec = call(
        bind(first_body, lat_rows, devices, slots), (grid_shape, spec_shape), field, seed, far=(field, seed),
        far_out=(0, 1), name="first",
        scratch=[buffer((rows, lon_total)), buffer(seed.shape), buffer(wave.shape, jnp.bfloat16),
                 buffer((rows, lon_total)), buffer(spec_shape.shape), pltpu.SemaphoreType.DMA((3 + QUART,))],
    )
    spec, far = sphere(spec, near, far, True, False, True)
    count = float(members * fields)
    part_rows = lat_rows // fields
    inverse_shape = jax.ShapeDtypeStruct((rows, 128), jnp.float32)
    logs, inverse, spec = call(
        bind(center_body, count, part_rows), (grid_shape, inverse_shape, spec_shape), arrive(spec), wave, name="center",
    )
    spec = sphere(spec, near, far, False, True, False)
    spec = call(ratio_body, spec_shape, arrive(spec), flipped, inverse, wave, name="ratio")
    spec = sphere(spec, near, far, False, False, True)
    part_shape = jax.ShapeDtypeStruct(((members + 1) * part_rows, lon_total), jnp.float32)
    keep, send = call(
        bind(last_body, count, part_rows), (part_shape, part_shape), arrive(spec), logs, wave, name="last",
    )
    got = lax.ppermute(send, "field", [(0, 1), (1, 0)])
    barycenter, logs = call(bind(final_body, part_rows), (sum_shape, grid_shape), keep, got, name="final")
    return barycenter, logs.reshape(precip.shape)


def fits_packed(mesh, shape):
    lat_groups, fields = mesh.shape["lat"], mesh.shape["field"]
    devices = lat_groups * fields
    field_total, lat_total, lon_total = shape
    degrees = lon_total // 2
    members, lat_rows = field_total // fields, lat_total // lat_groups
    return (
        fields == 2
        and lon_total == 4 * lat_total // 2
        and lat_total == 512
        and 2 * members * lat_rows == 128
        and members == 2
        and lat_groups % 2 == 0
        and devices % QUART == 0
        and degrees % (8 * devices) == 0
        and (devices // 2) % 16 == 0
        and devices <= 128
    )


def on_device(mesh, precip):
    members, lat_rows, lon_total = precip.shape
    shape = (members * mesh.shape["field"], lat_rows * mesh.shape["lat"], lon_total)
    return on_device_packed(precip) if ITERS == 2 and fits_packed(mesh, shape) else on_device_plain(precip)


def solution(mesh):
    in_specs = (P("field", "lat", None),)
    out_specs = (P("lat", None), P("field", "lat", None))
    return jax.shard_map(
        lambda precip: on_device(mesh, precip),
        mesh=mesh, in_specs=in_specs, out_specs=out_specs, check_vma=False,
    )
```

```python
import math

import jax
import jax.numpy as jnp
import ml_dtypes
import numpy as np
from jax import lax
from jax.experimental import pallas as pl
from jax.experimental.pallas import tpu as pltpu
from jax.sharding import PartitionSpec as P

ITERS = 2


heat_rate = 2.0
floor_value = 0.1


def colatitudes(lat_total):
    index_rows = jnp.arange(lat_total, dtype=jnp.float32)
    return jnp.pi * (index_rows + 0.5) / lat_total


def quad_weights(lat_total, lon_total):
    polar_angle = colatitudes(lat_total)
    return jnp.sin(polar_angle) * (jnp.pi / lat_total) * (2.0 * jnp.pi / lon_total)


def heat_factors(degrees):
    level = jnp.arange(degrees, dtype=jnp.float32)
    return jnp.exp(-heat_rate * level * (level + 1.0) / (degrees * (degrees - 1.0)))


def legendre_north(orders, lat_total, degrees):
    half_rows = lat_total // 2
    polar_angle = colatitudes(lat_total)[:half_rows]
    cosine = jnp.cos(polar_angle)
    log_sine = jnp.log(jnp.sin(polar_angle))
    order_value = orders.astype(jnp.float32)
    step_count = jnp.arange(1, degrees + 1, dtype=jnp.float32)
    log_ratios = jnp.log((2.0 * step_count - 1.0) / (2.0 * step_count))
    within = step_count[None, :] <= order_value[:, None]
    partial_log = jnp.sum(jnp.where(within, log_ratios[None, :], 0.0), axis=1)
    log_start = 0.5 * jnp.log((2.0 * order_value + 1.0) / (4.0 * jnp.pi)) + 0.5 * partial_log
    start_log = log_start[:, None] + order_value[:, None] * log_sine[None, :]
    span_size = min(32, degrees)

    def advance(state, block_start):
        prev_one, prev_two, log_scale = state
        collected = []
        for offset in range(span_size):
            degree = (block_start + offset).astype(jnp.float32)
            safe_diff = jnp.maximum(degree * degree - order_value * order_value, 1.0)
            first_factor = jnp.sqrt((4.0 * degree * degree - 1.0) / safe_diff)
            numerator = (
                (2.0 * degree + 1.0) * (degree + order_value - 1.0) * (degree - order_value - 1.0)
            )
            denominator = jnp.maximum((2.0 * degree - 3.0) * safe_diff, 1.0)
            second_factor = jnp.sqrt(jnp.maximum(numerator, 0.0) / denominator)
            recurred = (
                first_factor[:, None] * cosine[None, :] * prev_one
                - second_factor[:, None] * prev_two
            )
            current = jnp.where(
                (degree > order_value)[:, None],
                recurred,
                jnp.where(
                    (degree == order_value)[:, None],
                    jnp.ones_like(recurred),
                    jnp.zeros_like(recurred),
                ),
            )
            collected.append(current * jnp.exp(log_scale))
            prev_two = prev_one
            prev_one = current
            if (offset + 1) % 8 == 0:
                magnitude = jnp.maximum(jnp.abs(prev_one), jnp.abs(prev_two))
                safe_size = jnp.where(magnitude > 0.0, magnitude, jnp.ones_like(magnitude))
                prev_one = prev_one / safe_size
                prev_two = prev_two / safe_size
                log_scale = log_scale + jnp.log(safe_size)
        return ((prev_one, prev_two, log_scale), jnp.stack(collected))

    empty_state = jnp.zeros((orders.shape[0], half_rows), jnp.float32)
    block_starts = jnp.arange(0, degrees, span_size, dtype=jnp.int32)
    final_state, stacked = lax.scan(advance, (empty_state, empty_state, start_log), block_starts)
    legendre = stacked.reshape(degrees, orders.shape[0], half_rows)
    return jnp.transpose(legendre, (1, 2, 0))


def fourier_tables(lon_total, degrees, groups):
    per_group = degrees // groups
    column = jnp.arange(2 * degrees, dtype=jnp.int32)
    group_index = column // (2 * per_group)
    within_group = column % (2 * per_group)
    part_index = within_group // per_group
    order_index = group_index * per_group + within_group % per_group
    points = jnp.arange(lon_total, dtype=jnp.int32)
    phase = (points[:, None] * order_index[None, :] % lon_total).astype(jnp.float32) * (
        2.0 * jnp.pi / lon_total
    )
    forward = jnp.where(part_index[None, :] == 0, jnp.cos(phase), -jnp.sin(phase))
    doubled = jnp.where(order_index == 0, 1.0, 2.0)
    backward = jnp.transpose(forward) * doubled[:, None]
    return (forward, backward)


def on_device_plain(precip):
    groups = lax.axis_size("lat")
    lat_index = lax.axis_index("lat")
    local_fields, lat_rows, lon_total = precip.shape
    lat_total = lat_rows * groups
    degrees = lon_total // 2
    orders_here = degrees // groups
    half_rows = lat_total // 2
    count_fields = local_fields * lax.axis_size("field")
    weights_all = quad_weights(lat_total, lon_total)
    local_weights = lax.dynamic_slice_in_dim(weights_all, lat_index * lat_rows, lat_rows)
    forward, backward = fourier_tables(lon_total, degrees, groups)
    heat_factor = heat_factors(degrees)
    orders = lat_index * orders_here + jnp.arange(orders_here, dtype=jnp.int32)
    north_table = legendre_north(orders, lat_total, degrees)
    paired = north_table.reshape(orders_here, half_rows, degrees // 2, 2)
    parity = (orders % 2 == 0)[:, None, None]
    even_table = jnp.where(parity, paired[..., 0], paired[..., 1])
    odd_table = jnp.where(parity, paired[..., 1], paired[..., 0])
    heat_paired = heat_factor.reshape(degrees // 2, 2)
    heat_even = jnp.where(parity[:, :, 0], heat_paired[None, :, 0], heat_paired[None, :, 1])
    heat_odd = jnp.where(parity[:, :, 0], heat_paired[None, :, 1], heat_paired[None, :, 0])
    weights_north = weights_all[:half_rows]

    def legendre_pass(spread):
        count_here = spread.shape[0]
        shaped = spread.reshape(count_here, lat_total, 2, orders_here)
        north_part = shaped[:, :half_rows]
        south_part = jnp.flip(shaped[:, half_rows:], axis=1)
        even_input = (north_part + south_part) * weights_north[None, :, None, None]
        odd_input = (north_part - south_part) * weights_north[None, :, None, None]
        even_coef = jnp.einsum(
            "mjk,fjpm->mfpk", even_table, even_input, precision=lax.Precision.HIGHEST
        )
        odd_coef = jnp.einsum(
            "mjk,fjpm->mfpk", odd_table, odd_input, precision=lax.Precision.HIGHEST
        )
        even_coef = even_coef * heat_even[:, None, None, :]
        odd_coef = odd_coef * heat_odd[:, None, None, :]
        even_sum = jnp.einsum(
            "mjk,mfpk->fjpm", even_table, even_coef, precision=lax.Precision.HIGHEST
        )
        odd_sum = jnp.einsum("mjk,mfpk->fjpm", odd_table, odd_coef, precision=lax.Precision.HIGHEST)
        result = jnp.concatenate([even_sum + odd_sum, jnp.flip(even_sum - odd_sum, axis=1)], axis=1)
        return result.reshape(count_here, lat_total, 2 * orders_here)

    def kernel_apply_step(fields):
        spectra = jnp.einsum("fjk,kc->fjc", fields, forward, precision=lax.Precision.HIGHEST)

        def one_member(carry, member_spectra):
            spread = lax.all_to_all(member_spectra, "lat", split_axis=1, concat_axis=0, tiled=True)
            filtered = legendre_pass(spread[None])
            returned = lax.all_to_all(filtered[0], "lat", split_axis=0, concat_axis=1, tiled=True)
            return (carry, returned)

        unused, gathered = lax.scan(one_member, jnp.zeros((), jnp.float32), spectra)
        return jnp.einsum("fjc,ck->fjk", gathered, backward, precision=lax.Precision.HIGHEST)

    partial_value = jnp.sum(precip * local_weights[None, :, None], axis=(1, 2))
    masses = lax.psum(partial_value, "lat") / (4.0 * jnp.pi)
    scaling_logs = jnp.zeros(precip.shape, jnp.float32)
    log_barycenter = jnp.zeros(precip.shape[1:], jnp.float32)
    scaled = precip / masses[:, None, None]
    ratio_field = scaled
    for sweep in range(ITERS):
        smoothed = kernel_apply_step(ratio_field)
        clamped_values = jnp.log(jnp.maximum(smoothed, floor_value))
        added_total = lax.psum(jnp.sum(scaling_logs + clamped_values, axis=0), "field")
        log_barycenter = added_total / count_fields
        scaling_logs = log_barycenter[None] - clamped_values
        if sweep + 1 < ITERS:
            blurred_scale = kernel_apply_step(jnp.exp(scaling_logs))
            ratio_field = scaled / jnp.maximum(blurred_scale, floor_value)
    return (jnp.exp(log_barycenter), scaling_logs)


QUART = 4


def split_pair(value):
    high = value.astype(jnp.bfloat16)
    low = (value - high.astype(jnp.float32)).astype(jnp.bfloat16)
    return high, low


def pair_rows(value):
    high, low = split_pair(value)
    return jnp.concatenate([high, low], axis=0)


def dot_nt(left, right):
    return lax.dot_general(left, right, (((1,), (1,)), ((), ())), preferred_element_type=jnp.float32)


def dot_nn(left, right):
    return lax.dot_general(left, right, (((1,), (0,)), ((), ())), preferred_element_type=jnp.float32)


def wave_tables(lon_total, devices, slots):
    span = lon_total // QUART
    residue = np.arange(QUART)[:, None, None]
    order = residue + QUART * np.arange(devices // QUART)[None, :, None]
    order = (order + devices * np.arange(slots)[None, None, :]).reshape(QUART, -1)
    phase = (order[:, :, None] * np.arange(span)[None, None, :] % lon_total) * (2.0 * np.pi / lon_total)
    table = np.concatenate([np.cos(phase), np.sin(phase)], axis=1).astype(np.float32)
    high = table.astype(ml_dtypes.bfloat16)
    low = (table - high.astype(np.float32)).astype(ml_dtypes.bfloat16)
    return np.stack([high, low])


def wave_seeds(lon_total, devices, slots):
    span = lon_total // QUART
    first = (np.arange(QUART)[:, None] + QUART * np.arange(devices // QUART)[None, :]).reshape(-1)
    phases = [
        orders[:, None] * np.arange(span)[None, :] % lon_total * (2.0 * np.pi / lon_total)
        for orders in (first, devices * np.arange(slots))
    ]
    return np.concatenate([f(p) for p in phases for f in (np.cos, np.sin)]).astype(np.float32)


def grow_waves(seed_ref, wave_ref, devices, slots):
    orders = wave_ref.shape[2] // 2
    step_cos = seed_ref[2 * devices : 2 * devices + slots, :]
    step_sin = seed_ref[2 * devices + slots : 2 * devices + 2 * slots, :]
    for row in range(devices):
        residue, at = row // (devices // QUART), row % (devices // QUART) * slots
        cosine, sine = seed_ref[row : row + 1, :], seed_ref[devices + row : devices + row + 1, :]
        for place, value in (
            (at, cosine * step_cos - sine * step_sin),
            (orders + at, sine * step_cos + cosine * step_sin),
        ):
            high, low = split_pair(value)
            wave_ref[0, residue, place : place + slots, :] = high
            wave_ref[1, residue, place : place + slots, :] = low


def forward_waves(field, wave_ref, out_ref, done=None):
    span = field.shape[1] // QUART
    rows = field.shape[0]
    lanes = 2 * rows
    part = [field[:, q * span : (q + 1) * span] for q in range(QUART)]
    sum_even, sum_odd = part[0] + part[2], part[1] + part[3]
    diff_even, diff_odd = part[0] - part[2], part[1] - part[3]
    stack_even = pair_rows(jnp.concatenate([sum_even + sum_odd, sum_even - sum_odd], axis=0))
    stack_odd = pair_rows(jnp.concatenate([diff_even, diff_odd], axis=0))
    orders = wave_ref.shape[2] // 2
    first = lax.broadcasted_iota(jnp.int32, (orders, lanes), 1) < rows
    for residue in range(QUART):
        stack = stack_odd if residue % 2 else stack_even
        found = dot_nt(wave_ref[0, residue], stack) + dot_nt(wave_ref[1, residue], stack)
        found = found[:, :lanes] + found[:, lanes:]
        cosine, sine = found[:orders], found[orders:]
        if residue == 0:
            packed = jnp.where(first, cosine, -pltpu.roll(sine, rows, 1))
        elif residue == 2:
            packed = jnp.where(first, pltpu.roll(cosine, rows, 1), -sine)
        elif residue == 1:
            packed = jnp.where(first, cosine, -cosine) - pltpu.roll(sine, rows, 1)
        else:
            turned = pltpu.roll(sine, rows, 1)
            packed = cosine + jnp.where(first, turned, -turned)
        out_ref[:, residue] = packed.reshape(out_ref.shape[0], out_ref.shape[2], lanes)
        if done:
            done[residue].start()


def inverse_waves(spec_ref, wave_ref):
    outer, _, slots, lanes = spec_ref.shape
    rows = lanes // 2
    real = [None] * QUART
    cross = {}
    spare = None
    for residue in range(QUART):
        turned = jnp.transpose(spec_ref[:, residue].reshape(outer * slots, lanes))
        cosine, sine = turned[:rows], turned[rows:]
        if residue == 0:
            spare = sine[:, 0:1]
        left = jnp.concatenate([cosine, -sine], axis=1)
        if residue % 2:
            left = jnp.concatenate([left, jnp.concatenate([sine, cosine], axis=1)], axis=0)
        count = left.shape[0]
        left = pair_rows(left)
        found = dot_nn(left, wave_ref[0, residue]) + dot_nn(left, wave_ref[1, residue])
        found = found[:count] + found[count:]
        real[residue] = found[:rows]
        if residue % 2:
            cross[residue] = found[rows:]
    plus, minus = real[0] + real[2], real[0] - real[2]
    both, gap = real[1] + real[3], cross[1] - cross[3]
    return jnp.concatenate([plus + both, minus - gap, plus - both, minus + gap], axis=1), spare


def flip_rows(value, south, lat_rows):
    lanes = 128
    rows, width = value.shape
    sub = lax.broadcasted_iota(jnp.int32, (8, lanes), 0)
    source = jnp.where(south, 7 - sub, sub)
    blocks = lat_rows // 8
    out = []
    for base in range(0, rows, lat_rows):
        for block in range(blocks):
            near = value[base + 8 * block : base + 8 * block + 8]
            far = value[base + 8 * (blocks - 1 - block) : base + 8 * (blocks - block)]
            tile = jnp.where(south, far, near)
            pieces = [
                jnp.take_along_axis(tile[:, at : at + lanes], source, axis=0) for at in range(0, width, lanes)
            ]
            out.append(jnp.concatenate(pieces, axis=1))
    return jnp.concatenate(out, axis=0)


def device_index():
    return lax.axis_index("lat") * lax.axis_size("field") + lax.axis_index("field")


def in_south():
    return lax.axis_index("lat") >= lax.axis_size("lat") // 2


def first_body(lat_rows, devices, slots, field_hbm, seed_hbm, flipped_hbm, out_hbm, field_ref, seed_ref, wave_ref,
               flipped_ref, out_ref, sems):
    get_field = pltpu.make_async_copy(field_hbm, field_ref, sems.at[0])
    get_seed = pltpu.make_async_copy(seed_hbm, seed_ref, sems.at[1])
    put_flipped = pltpu.make_async_copy(flipped_ref, flipped_hbm, sems.at[2])
    put_wave = [
        pltpu.make_async_copy(out_ref.at[:, r], out_hbm.at[:, r], sems.at[3 + r]) for r in range(QUART)
    ]
    get_seed.start()
    get_field.start()
    get_seed.wait()
    grow_waves(seed_ref, wave_ref, devices, slots)
    get_field.wait()
    flipped_ref[...] = flip_rows(field_ref[...], in_south(), lat_rows) * 2.0**-8
    put_flipped.start()
    forward_waves(flipped_ref[...], wave_ref, out_ref, put_wave)
    put_flipped.wait()
    for copy in put_wave:
        copy.wait()


def member_sum(value, lat_rows):
    total = value[:lat_rows]
    for member in range(1, value.shape[0] // lat_rows):
        total = total + value[member * lat_rows : (member + 1) * lat_rows]
    return total


def core_select(core, first, second):
    return jnp.where(core == 0, first, second), jnp.where(core == 0, second, first)


def center_body(count, part_rows, spec_ref, wave_ref, logs_ref, inverse_ref, out_ref):
    blurred, total = inverse_waves(spec_ref, wave_ref)
    inverse = (4.0 * math.pi) / total
    clamped = jnp.log(jnp.maximum(blurred * inverse, floor_value))
    center = member_sum(clamped, part_rows) / count
    logs = jnp.concatenate([center] * (clamped.shape[0] // part_rows), axis=0) - clamped
    logs_ref[...] = logs
    forward_waves(jnp.exp(logs), wave_ref, out_ref)
    half = inverse.shape[0] // 2
    own, _ = core_select(lax.axis_index("field"), inverse[:half], inverse[half:])
    parts = [own[at : at + part_rows] for at in range(0, half, part_rows)]
    inverse_ref[...] = jnp.broadcast_to(jnp.concatenate([p for p in parts for _ in range(2)], axis=0), inverse_ref.shape)


def ratio_body(spec_ref, field_ref, inverse_ref, wave_ref, out_ref):
    blurred, _ = inverse_waves(spec_ref, wave_ref)
    scaled = field_ref[...] * inverse_ref[:, 0:1]
    forward_waves(scaled / jnp.maximum(blurred, floor_value), wave_ref, out_ref)


def last_body(count, part_rows, spec_ref, logs_ref, wave_ref, keep_ref, send_ref):
    blurred, _ = inverse_waves(spec_ref, wave_ref)
    clamped = jnp.log(jnp.maximum(blurred, floor_value))
    center = member_sum(logs_ref[...] + clamped, part_rows) / count
    logs = jnp.concatenate([center] * (clamped.shape[0] // part_rows), axis=0) - clamped
    half = logs.shape[0] // 2
    own, other = core_select(lax.axis_index("field"), logs[:half], logs[half:])
    keep_ref[...] = jnp.concatenate([own, center], axis=0)
    send_ref[...] = jnp.concatenate([other, center], axis=0)


def final_body(part_rows, keep_ref, got_ref, center_ref, logs_ref):
    low, high = core_select(lax.axis_index("field"), keep_ref[...], got_ref[...])
    pieces = []
    for at in range(0, low.shape[0], part_rows):
        pieces += [low[at : at + part_rows], high[at : at + part_rows]]
    whole = flip_rows(jnp.concatenate(pieces, axis=0), in_south(), 2 * part_rows)
    rows = logs_ref.shape[0]
    logs_ref[...] = whole[:rows]
    center_ref[...] = jnp.exp(whole[rows:])


def table_rows(degrees, devices, slot):
    return (degrees - devices * slot) // 2


def table_offset(degrees, devices, slot, parity):
    start = sum(2 * table_rows(degrees, devices, s) for s in range(slot))
    return start + parity * table_rows(degrees, devices, slot)


FAR_SLOTS = 3


def table_part(degrees, devices, slot, parity, near_ref, far_ref):
    count = table_rows(degrees, devices, slot)
    offset = table_offset(degrees, devices, slot, parity)
    if slot < FAR_SLOTS:
        return far_ref, offset, count
    return near_ref, offset - table_offset(degrees, devices, FAR_SLOTS, 0), count


def move_far(degrees, devices, slot, src_ref, dst_ref, sems):
    part = (slice(None), pl.ds(table_offset(degrees, devices, slot, 0), 2 * table_rows(degrees, devices, slot)))
    return pltpu.make_async_copy(src_ref.at[part], dst_ref.at[part], sems.at[slot])


def legendre_body(degrees, devices, slots, fixed_hbm, near_ref, far_hbm, weight_ref, fixed_ref, first_coef,
                  second_coef, left_half, right_half, far_ref, sem, far_sems):
    copy = pltpu.make_async_copy(fixed_hbm, fixed_ref, sem)
    copy.start()
    half = (left_half, right_half)
    lanes = 128
    device = device_index()
    order = lax.broadcasted_iota(jnp.int32, (slots, degrees), 0) * devices + device
    level = lax.broadcasted_iota(jnp.int32, (slots, degrees), 1)
    above = level > order
    order, level = order.astype(jnp.float32), level.astype(jnp.float32)
    diff = jnp.maximum(level * level - order * order, 1.0)
    rate = 0.5 * heat_rate / (degrees * (degrees - 1.0))
    first_ratio = jnp.exp(-rate * (2.0 * level))
    second_ratio = jnp.exp(-rate * (4.0 * level - 2.0))
    first_coef[...] = jnp.where(above, jnp.sqrt((4.0 * level * level - 1.0) / diff) * first_ratio, 0.0)
    numer = (2.0 * level + 1.0) * (level + order - 1.0) * (level - order - 1.0)
    denom = jnp.maximum((2.0 * level - 3.0) * diff, 1.0)
    second_coef[...] = jnp.where(above, jnp.sqrt(jnp.maximum(numer, 0.0) / denom) * second_ratio, 0.0)
    copy.wait()

    lane = lax.broadcasted_iota(jnp.int32, (slots, lanes), 1)
    start = jnp.sum(jnp.where(lane == device, fixed_ref[0:slots, 0:lanes], 0.0), axis=1, keepdims=True)
    sub = lax.broadcasted_iota(jnp.int32, (8, lanes), 0)
    tiles = slots // 8
    cosine = [jnp.broadcast_to(fixed_ref[slots : slots + 1, h * lanes : (h + 1) * lanes], (8, lanes)) for h in range(2)]
    log_sine = [jnp.broadcast_to(fixed_ref[slots + 1 : slots + 2, h * lanes : (h + 1) * lanes], (8, lanes)) for h in range(2)]
    order_tile = [(sub + 8 * t) * devices + device for t in range(tiles)]
    zero = jnp.zeros((8, lanes), jnp.float32)
    span_log = 60.0 * math.log(2.0)

    def fresh(tile):
        state = []
        for h in range(2):
            scale_log = start[8 * tile : 8 * tile + 8] + order_tile[tile].astype(jnp.float32) * log_sine[h]
            state.append((zero, zero, scale_log, jnp.exp(scale_log)))
        return state

    def chunk(index, states):
        active = len(states)
        base = pl.multiple_of(index * lanes, lanes)
        first = [first_coef[8 * t : 8 * t + 8, pl.ds(base, lanes)] for t in range(active)]
        second = [second_coef[8 * t : 8 * t + 8, pl.ds(base, lanes)] for t in range(active)]
        states = [list(s) for s in states]
        for k in range(lanes):
            degree = base + k
            for t in range(active):
                a = jnp.broadcast_to(first[t][:, k : k + 1], (8, lanes))
                b = jnp.broadcast_to(second[t][:, k : k + 1], (8, lanes))
                begin = jnp.where(order_tile[t] == degree, 1.0, 0.0)
                for h in range(2):
                    one, two, scale_log, scale = states[t][h]
                    now = (a * cosine[h]) * one + (begin - b * two)
                    half[h][pl.ds(degree * slots + 8 * t, 8), :] = now * scale
                    two, one = one, now
                    if (k + 1) % 8 == 0:
                        large = jnp.maximum(jnp.abs(one), jnp.abs(two)) > 2.0**30
                        factor = jnp.where(large, 2.0**-60, 1.0)
                        one, two = one * factor, two * factor
                        scale_log = scale_log + jnp.where(large, span_log, 0.0)
                        scale = jnp.exp(scale_log)
                    states[t][h] = (one, two, scale_log, scale)
        return states

    states = []
    chunks = degrees // lanes
    for index in range(chunks):
        while len(states) < tiles and 8 * len(states) * devices < (index + 1) * lanes:
            states.append(fresh(len(states)))
        states = chunk(index, states)

    weight_ref[...] = fixed_ref[slots + 2 : slots + 3, :]
    for slot in range(slots):
        for parity in range(2):
            part_ref, offset, count = table_part(degrees, devices, slot, parity, near_ref, far_ref)
            begin = (devices * slot + parity) * slots + slot
            for h in range(2):
                high, low = split_pair(half[h][pl.ds(begin, count, stride=2 * slots), :])
                part_ref[0, offset : offset + count, h * lanes : (h + 1) * lanes] = high
                part_ref[1, offset : offset + count, h * lanes : (h + 1) * lanes] = low
        if slot < FAR_SLOTS:
            move_far(degrees, devices, slot, far_ref, far_hbm, far_sems).start()
    for slot in range(FAR_SLOTS):
        move_far(degrees, devices, slot, far_ref, far_hbm, far_sems).wait()


def weave(first, second, width):
    lanes = first.shape[-1]
    even = lax.broadcasted_iota(jnp.int32, first.shape, first.ndim - 1) // width % 2 == 0
    axis = first.ndim - 1
    return (
        jnp.where(even, first, pltpu.roll(second, width, axis)),
        jnp.where(even, pltpu.roll(first, lanes - width, axis), second),
    )


def gather_orders(spec_ref, sign, fields, lat_groups, lat_rows, members, slots, halved, even_in, odd_in):
    group_lanes = 128 // lat_rows
    for h in range(2):
        even, odd = [], []
        for q in range(group_lanes):
            lat = h * group_lanes + q
            pair = ([], [])
            for source in range(fields):
                north = spec_ref[lat * fields + source]
                south = spec_ref[(lat_groups - 1 - lat) * fields + source] * sign
                pair[0].append(north + south)
                pair[1].append(north - south)
            if halved:
                pair = [weave(*p, lat_rows // 2) for p in pair]
            even.append(pair[0])
            odd.append(pair[1])
        for field in range(fields):
            for c in range(2 * members):
                row = (field * 2 * members + c) * slots
                part, member = c // members, c % members
                block, at = (member, part * fields + field) if halved else (field, c)
                cut = slice(at * lat_rows, (at + 1) * lat_rows)
                even_in[h][row : row + slots, :] = jnp.concatenate([e[block][:, cut] for e in even], axis=1)
                odd_in[h][row : row + slots, :] = jnp.concatenate([o[block][:, cut] for o in odd], axis=1)


def scatter_orders(out_ref, fields, lat_groups, lat_rows, members, slots, halved, north, south):
    group_lanes = 128 // lat_rows
    for lat in range(lat_groups // 2):
        h, q = lat // group_lanes, lat % group_lanes
        cut = slice(q * lat_rows, (q + 1) * lat_rows)
        for source, place in ((north, lat), (south, lat_groups - 1 - lat)):
            blocks = []
            for block in range(2):
                if halved:
                    owners = [(field, part, block) for part in range(2) for field in range(fields)]
                else:
                    owners = [(block, part, member) for part in range(2) for member in range(members)]
                rows = [((field * 2 + part) * members + member) * slots for field, part, member in owners]
                blocks.append(jnp.concatenate([source[h][row : row + slots, cut] for row in rows], axis=1))
            if halved:
                blocks = weave(*blocks, lat_rows // 2)
            out_ref[place * fields], out_ref[place * fields + 1] = blocks


def sphere_body(degrees, devices, slots, lat_groups, lat_rows, members, with_mass, halves_in, halves_out, spec_ref, near_ref, far_in,
                weight_ref, out_ref, *rest):
    far_ref, rest = (rest[0], rest[1:]) if with_mass else (far_in, rest)
    coef_ref, far_sem = rest[:2]
    halves = rest[2:]
    if with_mass:
        get_far = pltpu.make_async_copy(far_in, far_ref, far_sem)
        get_far.start()
    even_in, odd_in, north_out, south_out = halves[0:2], halves[2:4], halves[4:6], halves[6:8]
    device = device_index()
    sign = jnp.where(device % 2 == 0, 1.0, -1.0)
    fields = devices // lat_groups
    per_field = 2 * members
    columns = fields * per_field
    gather_orders(spec_ref, sign, fields, lat_groups, lat_rows, members, slots, halves_in, even_in, odd_in)
    mass = None

    def pick(slot, parity):
        picked = pl.ds(slot, columns, stride=slots)
        gain = 2.0 if slot else jnp.where(device == 0, 1.0, 2.0)
        pair = (even_in, odd_in)[parity]
        values = jnp.concatenate([pair[0][picked, :], pair[1][picked, :]], axis=1)
        return values * (weight_ref[...] * gain)

    def table(slot, parity):
        part_ref, offset, count = table_part(degrees, devices, slot, parity, near_ref, far_ref)
        return part_ref[0, offset : offset + count, :], part_ref[1, offset : offset + count, :], count

    if with_mass:
        mass = jnp.sum(pick(0, 0), axis=1, keepdims=True)

    def analyse(slot):
        for parity in range(2):
            high, low, count = table(slot, parity)
            packed = pair_rows(pick(slot, parity))
            coef = dot_nt(packed, high) + dot_nt(packed, low)
            coef_ref[2 * slot + parity, :, 0:count] = pair_rows(coef[:columns] + coef[columns:])

    def synthesise(slot):
        found = []
        for parity in range(2):
            high, low, count = table(slot, parity)
            packed = coef_ref[2 * slot + parity, :, 0:count]
            back = dot_nn(packed, high) + dot_nn(packed, low)
            found.append(back[:columns] + back[columns:])
        north, south = found[0] + found[1], (found[0] - found[1]) * sign
        if with_mass and slot == 0:
            spread = jnp.broadcast_to(mass, north.shape)
            spread = pltpu.roll(spread, members, 0)
            which = lax.broadcasted_iota(jnp.int32, north.shape, 0) % per_field
            spare = (which >= members) & (device == 0)
            north, south = jnp.where(spare, spread, north), jnp.where(spare, spread, south)
        picked = pl.ds(slot, columns, stride=slots)
        for h in range(2):
            north_out[h][picked, :] = north[:, 128 * h : 128 * h + 128]
            south_out[h][picked, :] = south[:, 128 * h : 128 * h + 128]

    near_slots, far_slots = range(FAR_SLOTS, slots), range(FAR_SLOTS)
    early = slots if with_mass else FAR_SLOTS
    for slot in near_slots:
        analyse(slot)
    for slot in range(FAR_SLOTS, early):
        synthesise(slot)
    if with_mass:
        get_far.wait()
    for slot in far_slots:
        analyse(slot)
    for slot in list(range(early, slots)) + list(far_slots):
        synthesise(slot)

    scatter_orders(out_ref, fields, lat_groups, lat_rows, members, slots, halves_out, north_out, south_out)


def on_device_packed(precip):
    lat_groups, fields = lax.axis_size("lat"), lax.axis_size("field")
    devices = lat_groups * fields
    members, lat_rows, lon_total = precip.shape
    lat_total, degrees = lat_rows * lat_groups, lon_total // 2
    slots = degrees // devices
    rows = members * lat_rows
    polar = np.pi * (np.arange(lat_total // 2) + 0.5) / lat_total
    level = np.arange(degrees)
    step = np.arange(1, degrees)
    starts = np.concatenate([[0.0], np.cumsum(np.log((2.0 * step - 1.0) / (2.0 * step)))])
    starts = 0.5 * np.log((2.0 * level + 1.0) / (4.0 * np.pi)) + 0.5 * starts
    starts = starts - 0.5 * heat_rate * level * (level + 1.0) / (degrees * (degrees - 1.0))
    fixed = np.zeros((slots + 8, lat_total // 2), np.float32)
    fixed[:slots, :devices] = starts.reshape(slots, devices)
    fixed[slots] = np.cos(polar)
    fixed[slots + 1] = np.log(np.sin(polar))
    fixed[slots + 2] = np.sin(polar) * (np.pi / lat_total) * (2.0 * np.pi / lon_total)
    fixed = jnp.asarray(fixed)
    wave = jnp.asarray(wave_tables(lon_total, devices, slots))

    vmem = pl.BlockSpec(memory_space=pltpu.VMEM)
    outer = devices // QUART
    spec_shape = jax.ShapeDtypeStruct((outer, QUART, slots, 2 * rows), jnp.float32)
    grid_shape = jax.ShapeDtypeStruct((rows, lon_total), jnp.float32)
    sum_shape = jax.ShapeDtypeStruct((lat_rows, lon_total), jnp.float32)
    far_rows = table_offset(degrees, devices, FAR_SLOTS, 0)
    near_rows = table_offset(degrees, devices, slots, 0) - far_rows
    near_shape = jax.ShapeDtypeStruct((2, near_rows, lat_total // 2), jnp.bfloat16)
    far_shape = jax.ShapeDtypeStruct((2, far_rows, lat_total // 2), jnp.bfloat16)
    flat_shape = jax.ShapeDtypeStruct((devices, slots, 2 * rows), jnp.float32)
    hbm = pl.BlockSpec(memory_space=pl.ANY)

    def call(body, shapes, *operands, name, far=(), far_out=(), scratch=(), cost=None, limit=8):
        single = not isinstance(shapes, tuple)
        shapes = (shapes,) if single else shapes
        outs = [hbm if index in far_out else vmem for index in range(len(shapes))]
        shapes = [
            pltpu.HBM(shape.shape, shape.dtype) if index in far_out else shape for index, shape in enumerate(shapes)
        ]
        specs = [hbm if any(o is f for f in far) else vmem for o in operands]
        operands = [
            pltpu.with_memory_space_constraint(o, pltpu.HBM) if any(o is f for f in far) else o for o in operands
        ]
        return pl.pallas_call(
            body,
            out_shape=shapes[0] if single else shapes,
            in_specs=specs,
            out_specs=outs[0] if single else outs,
            scratch_shapes=list(scratch),
            cost_estimate=cost,
            compiler_params=pltpu.CompilerParams(vmem_limit_bytes=limit << 20),
            name=name,
        )(*operands)

    def exchange(spec):
        flat = spec.reshape(devices, slots, 2 * rows)
        return lax.all_to_all(flat, ("lat", "field"), split_axis=0, concat_axis=0, tiled=True)

    def bind(body, *bound):
        return lambda *refs: body(*bound, *refs)

    def buffer(shape, dtype=jnp.float32):
        return pltpu.VMEM(shape, dtype)

    columns = fields * 2 * members
    signal = pltpu.SemaphoreType.DMA(())

    def sphere(spec, near, far, with_mass, halves_in, halves_out):
        return call(
            bind(sphere_body, degrees, devices, slots, lat_groups, lat_rows, members, with_mass, halves_in,
                 halves_out),
            (flat_shape, far_shape) if with_mass else flat_shape,
            exchange(spec), near, far, weight, far=(far,) if with_mass else (), name="sphere",
            limit=8,
            scratch=[buffer((2 * slots, 2 * columns, 256), jnp.bfloat16), signal]
            + [buffer((columns * slots + slots, 128))] * 8,
        )

    def arrive(spec):
        return exchange(spec).reshape(spec_shape.shape)

    weight_shape = jax.ShapeDtypeStruct((1, lat_total // 2), jnp.float32)
    near, far, weight = call(
        bind(legendre_body, degrees, devices, slots), (near_shape, far_shape, weight_shape), fixed, far=(fixed,), far_out=(1,),
        scratch=[buffer(fixed.shape)] + [buffer((slots, degrees))] * 2 + [buffer((degrees * slots + 2 * slots, 128))] * 2
        + [buffer(far_shape.shape, jnp.bfloat16), signal, pltpu.SemaphoreType.DMA((FAR_SLOTS,))],
        cost=pl.CostEstimate(flops=40_000_000, bytes_accessed=16 << 20, transcendentals=0),
        name="legendre", limit=12,
    )
    field = precip.reshape(rows, lon_total)
    seed = jnp.asarray(wave_seeds(lon_total, devices, slots))
    flipped, spec = call(
        bind(first_body, lat_rows, devices, slots), (grid_shape, spec_shape), field, seed, far=(field, seed),
        far_out=(0, 1), name="first",
        scratch=[buffer((rows, lon_total)), buffer(seed.shape), buffer(wave.shape, jnp.bfloat16),
                 buffer((rows, lon_total)), buffer(spec_shape.shape), pltpu.SemaphoreType.DMA((3 + QUART,))],
    )
    spec, far = sphere(spec, near, far, True, False, True)
    count = float(members * fields)
    part_rows = lat_rows // fields
    inverse_shape = jax.ShapeDtypeStruct((rows, 128), jnp.float32)
    logs, inverse, spec = call(
        bind(center_body, count, part_rows), (grid_shape, inverse_shape, spec_shape), arrive(spec), wave, name="center",
    )
    spec = sphere(spec, near, far, False, True, False)
    spec = call(ratio_body, spec_shape, arrive(spec), flipped, inverse, wave, name="ratio")
    spec = sphere(spec, near, far, False, False, True)
    part_shape = jax.ShapeDtypeStruct(((members + 1) * part_rows, lon_total), jnp.float32)
    keep, send = call(
        bind(last_body, count, part_rows), (part_shape, part_shape), arrive(spec), logs, wave, name="last",
    )
    got = lax.ppermute(send, "field", [(0, 1), (1, 0)])
    barycenter, logs = call(bind(final_body, part_rows), (sum_shape, grid_shape), keep, got, name="final")
    return barycenter, logs.reshape(precip.shape)


def fits_packed(mesh, shape):
    lat_groups, fields = mesh.shape["lat"], mesh.shape["field"]
    devices = lat_groups * fields
    field_total, lat_total, lon_total = shape
    degrees = lon_total // 2
    members, lat_rows = field_total // fields, lat_total // lat_groups
    return (
        fields == 2
        and lon_total == 4 * lat_total // 2
        and lat_total == 512
        and 2 * members * lat_rows == 128
        and members == 2
        and lat_groups % 2 == 0
        and devices % QUART == 0
        and degrees % (8 * devices) == 0
        and (devices // 2) % 16 == 0
        and devices <= 128
    )


def on_device(mesh, precip):
    members, lat_rows, lon_total = precip.shape
    shape = (members * mesh.shape["field"], lat_rows * mesh.shape["lat"], lon_total)
    return on_device_packed(precip) if ITERS == 2 and fits_packed(mesh, shape) else on_device_plain(precip)


def solution(mesh):
    in_specs = (P("field", "lat", None),)
    out_specs = (P("lat", None), P("field", "lat", None))
    return jax.shard_map(
        lambda precip: on_device(mesh, precip),
        mesh=mesh, in_specs=in_specs, out_specs=out_specs, check_vma=False,
    )
```

```python
import math

import jax
import jax.numpy as jnp
import ml_dtypes
import numpy as np
from jax import lax
from jax.experimental import pallas as pl
from jax.experimental.pallas import tpu as pltpu
from jax.sharding import PartitionSpec as P

ITERS = 2


heat_rate = 2.0
floor_value = 0.1


def colatitudes(lat_total):
    index_rows = jnp.arange(lat_total, dtype=jnp.float32)
    return jnp.pi * (index_rows + 0.5) / lat_total


def quad_weights(lat_total, lon_total):
    polar_angle = colatitudes(lat_total)
    return jnp.sin(polar_angle) * (jnp.pi / lat_total) * (2.0 * jnp.pi / lon_total)


def heat_factors(degrees):
    level = jnp.arange(degrees, dtype=jnp.float32)
    return jnp.exp(-heat_rate * level * (level + 1.0) / (degrees * (degrees - 1.0)))


def legendre_north(orders, lat_total, degrees):
    half_rows = lat_total // 2
    polar_angle = colatitudes(lat_total)[:half_rows]
    cosine = jnp.cos(polar_angle)
    log_sine = jnp.log(jnp.sin(polar_angle))
    order_value = orders.astype(jnp.float32)
    step_count = jnp.arange(1, degrees + 1, dtype=jnp.float32)
    log_ratios = jnp.log((2.0 * step_count - 1.0) / (2.0 * step_count))
    within = step_count[None, :] <= order_value[:, None]
    partial_log = jnp.sum(jnp.where(within, log_ratios[None, :], 0.0), axis=1)
    log_start = 0.5 * jnp.log((2.0 * order_value + 1.0) / (4.0 * jnp.pi)) + 0.5 * partial_log
    start_log = log_start[:, None] + order_value[:, None] * log_sine[None, :]
    span_size = min(32, degrees)

    def advance(state, block_start):
        prev_one, prev_two, log_scale = state
        collected = []
        for offset in range(span_size):
            degree = (block_start + offset).astype(jnp.float32)
            safe_diff = jnp.maximum(degree * degree - order_value * order_value, 1.0)
            first_factor = jnp.sqrt((4.0 * degree * degree - 1.0) / safe_diff)
            numerator = (
                (2.0 * degree + 1.0) * (degree + order_value - 1.0) * (degree - order_value - 1.0)
            )
            denominator = jnp.maximum((2.0 * degree - 3.0) * safe_diff, 1.0)
            second_factor = jnp.sqrt(jnp.maximum(numerator, 0.0) / denominator)
            recurred = (
                first_factor[:, None] * cosine[None, :] * prev_one
                - second_factor[:, None] * prev_two
            )
            current = jnp.where(
                (degree > order_value)[:, None],
                recurred,
                jnp.where(
                    (degree == order_value)[:, None],
                    jnp.ones_like(recurred),
                    jnp.zeros_like(recurred),
                ),
            )
            collected.append(current * jnp.exp(log_scale))
            prev_two = prev_one
            prev_one = current
            if (offset + 1) % 8 == 0:
                magnitude = jnp.maximum(jnp.abs(prev_one), jnp.abs(prev_two))
                safe_size = jnp.where(magnitude > 0.0, magnitude, jnp.ones_like(magnitude))
                prev_one = prev_one / safe_size
                prev_two = prev_two / safe_size
                log_scale = log_scale + jnp.log(safe_size)
        return ((prev_one, prev_two, log_scale), jnp.stack(collected))

    empty_state = jnp.zeros((orders.shape[0], half_rows), jnp.float32)
    block_starts = jnp.arange(0, degrees, span_size, dtype=jnp.int32)
    final_state, stacked = lax.scan(advance, (empty_state, empty_state, start_log), block_starts)
    legendre = stacked.reshape(degrees, orders.shape[0], half_rows)
    return jnp.transpose(legendre, (1, 2, 0))


def fourier_tables(lon_total, degrees, groups):
    per_group = degrees // groups
    column = jnp.arange(2 * degrees, dtype=jnp.int32)
    group_index = column // (2 * per_group)
    within_group = column % (2 * per_group)
    part_index = within_group // per_group
    order_index = group_index * per_group + within_group % per_group
    points = jnp.arange(lon_total, dtype=jnp.int32)
    phase = (points[:, None] * order_index[None, :] % lon_total).astype(jnp.float32) * (
        2.0 * jnp.pi / lon_total
    )
    forward = jnp.where(part_index[None, :] == 0, jnp.cos(phase), -jnp.sin(phase))
    doubled = jnp.where(order_index == 0, 1.0, 2.0)
    backward = jnp.transpose(forward) * doubled[:, None]
    return (forward, backward)


def on_device_plain(precip):
    groups = lax.axis_size("lat")
    lat_index = lax.axis_index("lat")
    local_fields, lat_rows, lon_total = precip.shape
    lat_total = lat_rows * groups
    degrees = lon_total // 2
    orders_here = degrees // groups
    half_rows = lat_total // 2
    count_fields = local_fields * lax.axis_size("field")
    weights_all = quad_weights(lat_total, lon_total)
    local_weights = lax.dynamic_slice_in_dim(weights_all, lat_index * lat_rows, lat_rows)
    forward, backward = fourier_tables(lon_total, degrees, groups)
    heat_factor = heat_factors(degrees)
    orders = lat_index * orders_here + jnp.arange(orders_here, dtype=jnp.int32)
    north_table = legendre_north(orders, lat_total, degrees)
    paired = north_table.reshape(orders_here, half_rows, degrees // 2, 2)
    parity = (orders % 2 == 0)[:, None, None]
    even_table = jnp.where(parity, paired[..., 0], paired[..., 1])
    odd_table = jnp.where(parity, paired[..., 1], paired[..., 0])
    heat_paired = heat_factor.reshape(degrees // 2, 2)
    heat_even = jnp.where(parity[:, :, 0], heat_paired[None, :, 0], heat_paired[None, :, 1])
    heat_odd = jnp.where(parity[:, :, 0], heat_paired[None, :, 1], heat_paired[None, :, 0])
    weights_north = weights_all[:half_rows]

    def legendre_pass(spread):
        count_here = spread.shape[0]
        shaped = spread.reshape(count_here, lat_total, 2, orders_here)
        north_part = shaped[:, :half_rows]
        south_part = jnp.flip(shaped[:, half_rows:], axis=1)
        even_input = (north_part + south_part) * weights_north[None, :, None, None]
        odd_input = (north_part - south_part) * weights_north[None, :, None, None]
        even_coef = jnp.einsum(
            "mjk,fjpm->mfpk", even_table, even_input, precision=lax.Precision.HIGHEST
        )
        odd_coef = jnp.einsum(
            "mjk,fjpm->mfpk", odd_table, odd_input, precision=lax.Precision.HIGHEST
        )
        even_coef = even_coef * heat_even[:, None, None, :]
        odd_coef = odd_coef * heat_odd[:, None, None, :]
        even_sum = jnp.einsum(
            "mjk,mfpk->fjpm", even_table, even_coef, precision=lax.Precision.HIGHEST
        )
        odd_sum = jnp.einsum("mjk,mfpk->fjpm", odd_table, odd_coef, precision=lax.Precision.HIGHEST)
        result = jnp.concatenate([even_sum + odd_sum, jnp.flip(even_sum - odd_sum, axis=1)], axis=1)
        return result.reshape(count_here, lat_total, 2 * orders_here)

    def kernel_apply_step(fields):
        spectra = jnp.einsum("fjk,kc->fjc", fields, forward, precision=lax.Precision.HIGHEST)

        def one_member(carry, member_spectra):
            spread = lax.all_to_all(member_spectra, "lat", split_axis=1, concat_axis=0, tiled=True)
            filtered = legendre_pass(spread[None])
            returned = lax.all_to_all(filtered[0], "lat", split_axis=0, concat_axis=1, tiled=True)
            return (carry, returned)

        unused, gathered = lax.scan(one_member, jnp.zeros((), jnp.float32), spectra)
        return jnp.einsum("fjc,ck->fjk", gathered, backward, precision=lax.Precision.HIGHEST)

    partial_value = jnp.sum(precip * local_weights[None, :, None], axis=(1, 2))
    masses = lax.psum(partial_value, "lat") / (4.0 * jnp.pi)
    scaling_logs = jnp.zeros(precip.shape, jnp.float32)
    log_barycenter = jnp.zeros(precip.shape[1:], jnp.float32)
    scaled = precip / masses[:, None, None]
    ratio_field = scaled
    for sweep in range(ITERS):
        smoothed = kernel_apply_step(ratio_field)
        clamped_values = jnp.log(jnp.maximum(smoothed, floor_value))
        added_total = lax.psum(jnp.sum(scaling_logs + clamped_values, axis=0), "field")
        log_barycenter = added_total / count_fields
        scaling_logs = log_barycenter[None] - clamped_values
        if sweep + 1 < ITERS:
            blurred_scale = kernel_apply_step(jnp.exp(scaling_logs))
            ratio_field = scaled / jnp.maximum(blurred_scale, floor_value)
    return (jnp.exp(log_barycenter), scaling_logs)


QUART = 4


def split_pair(value):
    high = value.astype(jnp.bfloat16)
    low = (value - high.astype(jnp.float32)).astype(jnp.bfloat16)
    return high, low


def pair_rows(value):
    high, low = split_pair(value)
    return jnp.concatenate([high, low], axis=0)


def dot_nt(left, right):
    return lax.dot_general(left, right, (((1,), (1,)), ((), ())), preferred_element_type=jnp.float32)


def dot_nn(left, right):
    return lax.dot_general(left, right, (((1,), (0,)), ((), ())), preferred_element_type=jnp.float32)


def wave_tables(lon_total, devices, slots):
    span = lon_total // QUART
    residue = np.arange(QUART)[:, None, None]
    order = residue + QUART * np.arange(devices // QUART)[None, :, None]
    order = (order + devices * np.arange(slots)[None, None, :]).reshape(QUART, -1)
    phase = (order[:, :, None] * np.arange(span)[None, None, :] % lon_total) * (2.0 * np.pi / lon_total)
    table = np.concatenate([np.cos(phase), np.sin(phase)], axis=1).astype(np.float32)
    high = table.astype(ml_dtypes.bfloat16)
    low = (table - high.astype(np.float32)).astype(ml_dtypes.bfloat16)
    return np.stack([high, low])


def wave_seeds(lon_total, devices, slots):
    span = lon_total // QUART
    first = (np.arange(QUART)[:, None] + QUART * np.arange(devices // QUART)[None, :]).reshape(-1)
    phases = [
        orders[:, None] * np.arange(span)[None, :] % lon_total * (2.0 * np.pi / lon_total)
        for orders in (first, devices * np.arange(slots))
    ]
    return np.concatenate([f(p) for p in phases for f in (np.cos, np.sin)]).astype(np.float32)


def grow_waves(seed_ref, wave_ref, devices, slots):
    orders = wave_ref.shape[2] // 2
    step_cos = seed_ref[2 * devices : 2 * devices + slots, :]
    step_sin = seed_ref[2 * devices + slots : 2 * devices + 2 * slots, :]
    for row in range(devices):
        residue, at = row // (devices // QUART), row % (devices // QUART) * slots
        cosine, sine = seed_ref[row : row + 1, :], seed_ref[devices + row : devices + row + 1, :]
        for place, value in (
            (at, cosine * step_cos - sine * step_sin),
            (orders + at, sine * step_cos + cosine * step_sin),
        ):
            high, low = split_pair(value)
            wave_ref[0, residue, place : place + slots, :] = high
            wave_ref[1, residue, place : place + slots, :] = low


def forward_waves(field, wave_ref, out_ref, done=None):
    span = field.shape[1] // QUART
    rows = field.shape[0]
    lanes = 2 * rows
    part = [field[:, q * span : (q + 1) * span] for q in range(QUART)]
    sum_even, sum_odd = part[0] + part[2], part[1] + part[3]
    diff_even, diff_odd = part[0] - part[2], part[1] - part[3]
    stack_even = pair_rows(jnp.concatenate([sum_even + sum_odd, sum_even - sum_odd], axis=0))
    stack_odd = pair_rows(jnp.concatenate([diff_even, diff_odd], axis=0))
    orders = wave_ref.shape[2] // 2
    first = lax.broadcasted_iota(jnp.int32, (orders, lanes), 1) < rows
    for residue in range(QUART):
        stack = stack_odd if residue % 2 else stack_even
        found = dot_nt(wave_ref[0, residue], stack) + dot_nt(wave_ref[1, residue], stack)
        found = found[:, :lanes] + found[:, lanes:]
        cosine, sine = found[:orders], found[orders:]
        if residue == 0:
            packed = jnp.where(first, cosine, -pltpu.roll(sine, rows, 1))
        elif residue == 2:
            packed = jnp.where(first, pltpu.roll(cosine, rows, 1), -sine)
        elif residue == 1:
            packed = jnp.where(first, cosine, -cosine) - pltpu.roll(sine, rows, 1)
        else:
            turned = pltpu.roll(sine, rows, 1)
            packed = cosine + jnp.where(first, turned, -turned)
        out_ref[:, residue] = packed.reshape(out_ref.shape[0], out_ref.shape[2], lanes)
        if done:
            done[residue].start()


def inverse_waves(spec_ref, wave_ref):
    outer, _, slots, lanes = spec_ref.shape
    rows = lanes // 2
    real = [None] * QUART
    cross = {}
    spare = None
    for residue in range(QUART):
        turned = jnp.transpose(spec_ref[:, residue].reshape(outer * slots, lanes))
        cosine, sine = turned[:rows], turned[rows:]
        if residue == 0:
            spare = sine[:, 0:1]
        left = jnp.concatenate([cosine, -sine], axis=1)
        if residue % 2:
            left = jnp.concatenate([left, jnp.concatenate([sine, cosine], axis=1)], axis=0)
        count = left.shape[0]
        left = pair_rows(left)
        found = dot_nn(left, wave_ref[0, residue]) + dot_nn(left, wave_ref[1, residue])
        found = found[:count] + found[count:]
        real[residue] = found[:rows]
        if residue % 2:
            cross[residue] = found[rows:]
    plus, minus = real[0] + real[2], real[0] - real[2]
    both, gap = real[1] + real[3], cross[1] - cross[3]
    return jnp.concatenate([plus + both, minus - gap, plus - both, minus + gap], axis=1), spare


def flip_rows(value, south, lat_rows):
    lanes = 128
    rows, width = value.shape
    sub = lax.broadcasted_iota(jnp.int32, (8, lanes), 0)
    source = jnp.where(south, 7 - sub, sub)
    blocks = lat_rows // 8
    out = []
    for base in range(0, rows, lat_rows):
        for block in range(blocks):
            near = value[base + 8 * block : base + 8 * block + 8]
            far = value[base + 8 * (blocks - 1 - block) : base + 8 * (blocks - block)]
            tile = jnp.where(south, far, near)
            pieces = [
                jnp.take_along_axis(tile[:, at : at + lanes], source, axis=0) for at in range(0, width, lanes)
            ]
            out.append(jnp.concatenate(pieces, axis=1))
    return jnp.concatenate(out, axis=0)


def device_index():
    return lax.axis_index("lat") * lax.axis_size("field") + lax.axis_index("field")


def in_south():
    return lax.axis_index("lat") >= lax.axis_size("lat") // 2


def oriented(field, lat_rows):
    return flip_rows(field, in_south(), lat_rows) * 2.0**-8


def first_body(lat_rows, devices, slots, field_hbm, seed_hbm, out_hbm, field_ref, seed_ref, wave_ref, out_ref, sems):
    get_field = pltpu.make_async_copy(field_hbm, field_ref, sems.at[0])
    get_seed = pltpu.make_async_copy(seed_hbm, seed_ref, sems.at[1])
    put_wave = [
        pltpu.make_async_copy(out_ref.at[:, r], out_hbm.at[:, r], sems.at[2 + r]) for r in range(QUART)
    ]
    get_seed.start()
    get_field.start()
    get_seed.wait()
    grow_waves(seed_ref, wave_ref, devices, slots)
    get_field.wait()
    forward_waves(oriented(field_ref[...], lat_rows), wave_ref, out_ref, put_wave)
    for copy in put_wave:
        copy.wait()


def member_sum(value, lat_rows):
    total = value[:lat_rows]
    for member in range(1, value.shape[0] // lat_rows):
        total = total + value[member * lat_rows : (member + 1) * lat_rows]
    return total


def core_select(core, first, second):
    return jnp.where(core == 0, first, second), jnp.where(core == 0, second, first)


def center_body(count, part_rows, spec_ref, wave_ref, logs_ref, inverse_ref, out_ref):
    blurred, total = inverse_waves(spec_ref, wave_ref)
    inverse = (4.0 * math.pi) / total
    clamped = jnp.log(jnp.maximum(blurred * inverse, floor_value))
    center = member_sum(clamped, part_rows) / count
    logs = jnp.concatenate([center] * (clamped.shape[0] // part_rows), axis=0) - clamped
    logs_ref[...] = logs
    forward_waves(jnp.exp(logs), wave_ref, out_ref)
    half = inverse.shape[0] // 2
    own, _ = core_select(lax.axis_index("field"), inverse[:half], inverse[half:])
    parts = [own[at : at + part_rows] for at in range(0, half, part_rows)]
    inverse_ref[...] = jnp.broadcast_to(jnp.concatenate([p for p in parts for _ in range(2)], axis=0), inverse_ref.shape)


def ratio_body(lat_rows, spec_ref, field_ref, inverse_ref, wave_ref, out_ref):
    blurred, _ = inverse_waves(spec_ref, wave_ref)
    scaled = oriented(field_ref[...], lat_rows) * inverse_ref[:, 0:1]
    forward_waves(scaled / jnp.maximum(blurred, floor_value), wave_ref, out_ref)


def last_body(count, part_rows, spec_ref, logs_ref, wave_ref, keep_ref, send_ref):
    blurred, _ = inverse_waves(spec_ref, wave_ref)
    clamped = jnp.log(jnp.maximum(blurred, floor_value))
    center = member_sum(logs_ref[...] + clamped, part_rows) / count
    logs = jnp.concatenate([center] * (clamped.shape[0] // part_rows), axis=0) - clamped
    half = logs.shape[0] // 2
    own, other = core_select(lax.axis_index("field"), logs[:half], logs[half:])
    keep_ref[...] = jnp.concatenate([own, center], axis=0)
    send_ref[...] = jnp.concatenate([other, center], axis=0)


def final_body(part_rows, keep_ref, got_ref, center_ref, logs_ref):
    low, high = core_select(lax.axis_index("field"), keep_ref[...], got_ref[...])
    pieces = []
    for at in range(0, low.shape[0], part_rows):
        pieces += [low[at : at + part_rows], high[at : at + part_rows]]
    whole = flip_rows(jnp.concatenate(pieces, axis=0), in_south(), 2 * part_rows)
    rows = logs_ref.shape[0]
    logs_ref[...] = whole[:rows]
    center_ref[...] = jnp.exp(whole[rows:])


def table_rows(degrees, devices, slot):
    return (degrees - devices * slot) // 2


def table_offset(degrees, devices, slot, parity):
    start = sum(2 * table_rows(degrees, devices, s) for s in range(slot))
    return start + parity * table_rows(degrees, devices, slot)


FAR_SLOTS = 3


def table_part(degrees, devices, slot, parity, near_ref, far_ref):
    count = table_rows(degrees, devices, slot)
    offset = table_offset(degrees, devices, slot, parity)
    if slot < FAR_SLOTS:
        return far_ref, offset, count
    return near_ref, offset - table_offset(degrees, devices, FAR_SLOTS, 0), count


def move_far(degrees, devices, slot, src_ref, dst_ref, sems):
    part = (slice(None), pl.ds(table_offset(degrees, devices, slot, 0), 2 * table_rows(degrees, devices, slot)))
    return pltpu.make_async_copy(src_ref.at[part], dst_ref.at[part], sems.at[slot])


def legendre_body(degrees, devices, slots, fixed_hbm, near_ref, far_hbm, weight_ref, fixed_ref, first_coef,
                  second_coef, left_half, right_half, far_ref, sem, far_sems):
    copy = pltpu.make_async_copy(fixed_hbm, fixed_ref, sem)
    copy.start()
    half = (left_half, right_half)
    lanes = 128
    device = device_index()
    order = lax.broadcasted_iota(jnp.int32, (slots, degrees), 0) * devices + device
    level = lax.broadcasted_iota(jnp.int32, (slots, degrees), 1)
    above = level > order
    order, level = order.astype(jnp.float32), level.astype(jnp.float32)
    diff = jnp.maximum(level * level - order * order, 1.0)
    rate = 0.5 * heat_rate / (degrees * (degrees - 1.0))
    first_ratio = jnp.exp(-rate * (2.0 * level))
    second_ratio = jnp.exp(-rate * (4.0 * level - 2.0))
    first_coef[...] = jnp.where(above, jnp.sqrt((4.0 * level * level - 1.0) / diff) * first_ratio, 0.0)
    numer = (2.0 * level + 1.0) * (level + order - 1.0) * (level - order - 1.0)
    denom = jnp.maximum((2.0 * level - 3.0) * diff, 1.0)
    second_coef[...] = jnp.where(above, jnp.sqrt(jnp.maximum(numer, 0.0) / denom) * second_ratio, 0.0)
    copy.wait()

    lane = lax.broadcasted_iota(jnp.int32, (slots, lanes), 1)
    start = jnp.sum(jnp.where(lane == device, fixed_ref[0:slots, 0:lanes], 0.0), axis=1, keepdims=True)
    sub = lax.broadcasted_iota(jnp.int32, (8, lanes), 0)
    tiles = slots // 8
    cosine = [jnp.broadcast_to(fixed_ref[slots : slots + 1, h * lanes : (h + 1) * lanes], (8, lanes)) for h in range(2)]
    log_sine = [jnp.broadcast_to(fixed_ref[slots + 1 : slots + 2, h * lanes : (h + 1) * lanes], (8, lanes)) for h in range(2)]
    order_tile = [(sub + 8 * t) * devices + device for t in range(tiles)]
    zero = jnp.zeros((8, lanes), jnp.float32)
    span_log = 60.0 * math.log(2.0)

    def fresh(tile):
        state = []
        for h in range(2):
            scale_log = start[8 * tile : 8 * tile + 8] + order_tile[tile].astype(jnp.float32) * log_sine[h]
            state.append((zero, zero, scale_log, jnp.exp(scale_log)))
        return state

    def chunk(index, states):
        active = len(states)
        base = pl.multiple_of(index * lanes, lanes)
        first = [first_coef[8 * t : 8 * t + 8, pl.ds(base, lanes)] for t in range(active)]
        second = [second_coef[8 * t : 8 * t + 8, pl.ds(base, lanes)] for t in range(active)]
        states = [list(s) for s in states]
        for k in range(lanes):
            degree = base + k
            for t in range(active):
                a = jnp.broadcast_to(first[t][:, k : k + 1], (8, lanes))
                b = jnp.broadcast_to(second[t][:, k : k + 1], (8, lanes))
                begin = jnp.where(order_tile[t] == degree, 1.0, 0.0)
                for h in range(2):
                    one, two, scale_log, scale = states[t][h]
                    now = (a * cosine[h]) * one + (begin - b * two)
                    half[h][pl.ds(degree * slots + 8 * t, 8), :] = now * scale
                    two, one = one, now
                    if (k + 1) % 8 == 0:
                        large = jnp.maximum(jnp.abs(one), jnp.abs(two)) > 2.0**30
                        factor = jnp.where(large, 2.0**-60, 1.0)
                        one, two = one * factor, two * factor
                        scale_log = scale_log + jnp.where(large, span_log, 0.0)
                        scale = jnp.exp(scale_log)
                    states[t][h] = (one, two, scale_log, scale)
        return states

    states = []
    chunks = degrees // lanes
    for index in range(chunks):
        while len(states) < tiles and 8 * len(states) * devices < (index + 1) * lanes:
            states.append(fresh(len(states)))
        states = chunk(index, states)

    weight_ref[...] = fixed_ref[slots + 2 : slots + 3, :]
    for slot in range(slots):
        for parity in range(2):
            part_ref, offset, count = table_part(degrees, devices, slot, parity, near_ref, far_ref)
            begin = (devices * slot + parity) * slots + slot
            for h in range(2):
                high, low = split_pair(half[h][pl.ds(begin, count, stride=2 * slots), :])
                part_ref[0, offset : offset + count, h * lanes : (h + 1) * lanes] = high
                part_ref[1, offset : offset + count, h * lanes : (h + 1) * lanes] = low
        if slot < FAR_SLOTS:
            move_far(degrees, devices, slot, far_ref, far_hbm, far_sems).start()
    for slot in range(FAR_SLOTS):
        move_far(degrees, devices, slot, far_ref, far_hbm, far_sems).wait()


def weave(first, second, width):
    lanes = first.shape[-1]
    even = lax.broadcasted_iota(jnp.int32, first.shape, first.ndim - 1) // width % 2 == 0
    axis = first.ndim - 1
    return (
        jnp.where(even, first, pltpu.roll(second, width, axis)),
        jnp.where(even, pltpu.roll(first, lanes - width, axis), second),
    )


def gather_orders(spec_ref, sign, fields, lat_groups, lat_rows, members, slots, halved, even_in, odd_in):
    group_lanes = 128 // lat_rows
    for h in range(2):
        even, odd = [], []
        for q in range(group_lanes):
            lat = h * group_lanes + q
            pair = ([], [])
            for source in range(fields):
                north = spec_ref[lat * fields + source]
                south = spec_ref[(lat_groups - 1 - lat) * fields + source] * sign
                pair[0].append(north + south)
                pair[1].append(north - south)
            if halved:
                pair = [weave(*p, lat_rows // 2) for p in pair]
            even.append(pair[0])
            odd.append(pair[1])
        for field in range(fields):
            for c in range(2 * members):
                row = (field * 2 * members + c) * slots
                part, member = c // members, c % members
                block, at = (member, part * fields + field) if halved else (field, c)
                cut = slice(at * lat_rows, (at + 1) * lat_rows)
                even_in[h][row : row + slots, :] = jnp.concatenate([e[block][:, cut] for e in even], axis=1)
                odd_in[h][row : row + slots, :] = jnp.concatenate([o[block][:, cut] for o in odd], axis=1)


def scatter_orders(out_ref, fields, lat_groups, lat_rows, members, slots, halved, north, south):
    group_lanes = 128 // lat_rows
    columns = fields * 2 * members
    for h in range(2):
        for source, mirrored in ((north, False), (south, True)):
            values = [source[h][pl.ds(column, slots, stride=columns), :] for column in range(columns)]
            for q in range(group_lanes):
                lat = h * group_lanes + q
                place = lat_groups - 1 - lat if mirrored else lat
                cut = slice(q * lat_rows, (q + 1) * lat_rows)
                blocks = []
                for block in range(2):
                    if halved:
                        owners = [(field, part, block) for part in range(2) for field in range(fields)]
                    else:
                        owners = [(block, part, member) for part in range(2) for member in range(members)]
                    picked = [(field * 2 + part) * members + member for field, part, member in owners]
                    blocks.append(jnp.concatenate([values[column][:, cut] for column in picked], axis=1))
                if halved:
                    blocks = weave(*blocks, lat_rows // 2)
                out_ref[place * fields], out_ref[place * fields + 1] = blocks


def sphere_body(degrees, devices, slots, lat_groups, lat_rows, members, with_mass, halves_in, halves_out, spec_ref, near_ref, far_in,
                weight_ref, out_ref, *rest):
    far_ref, rest = (rest[0], rest[1:]) if with_mass else (far_in, rest)
    coef_ref, far_sem = rest[:2]
    halves = rest[2:]
    if with_mass:
        get_far = pltpu.make_async_copy(far_in, far_ref, far_sem)
        get_far.start()
    even_in, odd_in, north_out, south_out = halves[0:2], halves[2:4], halves[4:6], halves[6:8]
    device = device_index()
    sign = jnp.where(device % 2 == 0, 1.0, -1.0)
    fields = devices // lat_groups
    per_field = 2 * members
    columns = fields * per_field
    gather_orders(spec_ref, sign, fields, lat_groups, lat_rows, members, slots, halves_in, even_in, odd_in)
    mass = None

    def pick(slot, parity):
        picked = pl.ds(slot, columns, stride=slots)
        gain = 2.0 if slot else jnp.where(device == 0, 1.0, 2.0)
        pair = (even_in, odd_in)[parity]
        values = jnp.concatenate([pair[0][picked, :], pair[1][picked, :]], axis=1)
        return values * (weight_ref[...] * gain)

    def table(slot, parity):
        part_ref, offset, count = table_part(degrees, devices, slot, parity, near_ref, far_ref)
        return part_ref[0, offset : offset + count, :], part_ref[1, offset : offset + count, :], count

    if with_mass:
        mass = jnp.sum(pick(0, 0), axis=1, keepdims=True)

    def analyse(slot):
        for parity in range(2):
            high, low, count = table(slot, parity)
            packed = pair_rows(pick(slot, parity))
            coef = dot_nt(packed, high) + dot_nt(packed, low)
            coef_ref[2 * slot + parity, :, 0:count] = pair_rows(coef[:columns] + coef[columns:])

    def synthesise(slot):
        found = []
        for parity in range(2):
            high, low, count = table(slot, parity)
            packed = coef_ref[2 * slot + parity, :, 0:count]
            back = dot_nn(packed, high) + dot_nn(packed, low)
            found.append(back[:columns] + back[columns:])
        north, south = found[0] + found[1], (found[0] - found[1]) * sign
        if with_mass and slot == 0:
            spread = jnp.broadcast_to(mass, north.shape)
            spread = pltpu.roll(spread, members, 0)
            which = lax.broadcasted_iota(jnp.int32, north.shape, 0) % per_field
            spare = (which >= members) & (device == 0)
            north, south = jnp.where(spare, spread, north), jnp.where(spare, spread, south)
        picked = slice(slot * columns, (slot + 1) * columns)
        for h in range(2):
            north_out[h][picked, :] = north[:, 128 * h : 128 * h + 128]
            south_out[h][picked, :] = south[:, 128 * h : 128 * h + 128]

    near_slots, far_slots = range(FAR_SLOTS, slots), range(FAR_SLOTS)
    early = slots if with_mass else FAR_SLOTS
    for slot in near_slots:
        analyse(slot)
    for slot in range(FAR_SLOTS, early):
        synthesise(slot)
    if with_mass:
        get_far.wait()
    for slot in far_slots:
        analyse(slot)
    for slot in list(range(early, slots)) + list(far_slots):
        synthesise(slot)

    scatter_orders(out_ref, fields, lat_groups, lat_rows, members, slots, halves_out, north_out, south_out)


def on_device_packed(precip):
    lat_groups, fields = lax.axis_size("lat"), lax.axis_size("field")
    devices = lat_groups * fields
    members, lat_rows, lon_total = precip.shape
    lat_total, degrees = lat_rows * lat_groups, lon_total // 2
    slots = degrees // devices
    rows = members * lat_rows
    polar = np.pi * (np.arange(lat_total // 2) + 0.5) / lat_total
    level = np.arange(degrees)
    step = np.arange(1, degrees)
    starts = np.concatenate([[0.0], np.cumsum(np.log((2.0 * step - 1.0) / (2.0 * step)))])
    starts = 0.5 * np.log((2.0 * level + 1.0) / (4.0 * np.pi)) + 0.5 * starts
    starts = starts - 0.5 * heat_rate * level * (level + 1.0) / (degrees * (degrees - 1.0))
    fixed = np.zeros((slots + 8, lat_total // 2), np.float32)
    fixed[:slots, :devices] = starts.reshape(slots, devices)
    fixed[slots] = np.cos(polar)
    fixed[slots + 1] = np.log(np.sin(polar))
    fixed[slots + 2] = np.sin(polar) * (np.pi / lat_total) * (2.0 * np.pi / lon_total)
    fixed = jnp.asarray(fixed)
    wave = jnp.asarray(wave_tables(lon_total, devices, slots))

    vmem = pl.BlockSpec(memory_space=pltpu.VMEM)
    outer = devices // QUART
    spec_shape = jax.ShapeDtypeStruct((outer, QUART, slots, 2 * rows), jnp.float32)
    grid_shape = jax.ShapeDtypeStruct((rows, lon_total), jnp.float32)
    sum_shape = jax.ShapeDtypeStruct((lat_rows, lon_total), jnp.float32)
    far_rows = table_offset(degrees, devices, FAR_SLOTS, 0)
    near_rows = table_offset(degrees, devices, slots, 0) - far_rows
    near_shape = jax.ShapeDtypeStruct((2, near_rows, lat_total // 2), jnp.bfloat16)
    far_shape = jax.ShapeDtypeStruct((2, far_rows, lat_total // 2), jnp.bfloat16)
    flat_shape = jax.ShapeDtypeStruct((devices, slots, 2 * rows), jnp.float32)
    hbm = pl.BlockSpec(memory_space=pl.ANY)

    def call(body, shapes, *operands, name, far=(), far_out=(), scratch=(), cost=None, limit=8):
        single = not isinstance(shapes, tuple)
        shapes = (shapes,) if single else shapes
        outs = [hbm if index in far_out else vmem for index in range(len(shapes))]
        shapes = [
            pltpu.HBM(shape.shape, shape.dtype) if index in far_out else shape for index, shape in enumerate(shapes)
        ]
        specs = [hbm if any(o is f for f in far) else vmem for o in operands]
        operands = [
            pltpu.with_memory_space_constraint(o, pltpu.HBM) if any(o is f for f in far) else o for o in operands
        ]
        return pl.pallas_call(
            body,
            out_shape=shapes[0] if single else shapes,
            in_specs=specs,
            out_specs=outs[0] if single else outs,
            scratch_shapes=list(scratch),
            cost_estimate=cost,
            compiler_params=pltpu.CompilerParams(vmem_limit_bytes=limit << 20),
            name=name,
        )(*operands)

    def exchange(spec):
        flat = spec.reshape(devices, slots, 2 * rows)
        return lax.all_to_all(flat, ("lat", "field"), split_axis=0, concat_axis=0, tiled=True)

    def bind(body, *bound):
        return lambda *refs: body(*bound, *refs)

    def buffer(shape, dtype=jnp.float32):
        return pltpu.VMEM(shape, dtype)

    columns = fields * 2 * members
    signal = pltpu.SemaphoreType.DMA(())

    def sphere(spec, near, far, with_mass, halves_in, halves_out):
        return call(
            bind(sphere_body, degrees, devices, slots, lat_groups, lat_rows, members, with_mass, halves_in,
                 halves_out),
            (flat_shape, far_shape) if with_mass else flat_shape,
            exchange(spec), near, far, weight, far=(far,) if with_mass else (), name="sphere",
            limit=8,
            scratch=[buffer((2 * slots, 2 * columns, 256), jnp.bfloat16), signal]
            + [buffer((columns * slots + slots, 128))] * 8,
        )

    def arrive(spec):
        return exchange(spec).reshape(spec_shape.shape)

    weight_shape = jax.ShapeDtypeStruct((1, lat_total // 2), jnp.float32)
    near, far, weight = call(
        bind(legendre_body, degrees, devices, slots), (near_shape, far_shape, weight_shape), fixed, far=(fixed,), far_out=(1,),
        scratch=[buffer(fixed.shape)] + [buffer((slots, degrees))] * 2 + [buffer((degrees * slots + 2 * slots, 128))] * 2
        + [buffer(far_shape.shape, jnp.bfloat16), signal, pltpu.SemaphoreType.DMA((FAR_SLOTS,))],
        cost=pl.CostEstimate(flops=40_000_000, bytes_accessed=16 << 20, transcendentals=0),
        name="legendre", limit=12,
    )
    field = precip.reshape(rows, lon_total)
    seed = jnp.asarray(wave_seeds(lon_total, devices, slots))
    spec = call(
        bind(first_body, lat_rows, devices, slots), spec_shape, field, seed, far=(field, seed),
        far_out=(0,), name="first",
        scratch=[buffer((rows, lon_total)), buffer(seed.shape), buffer(wave.shape, jnp.bfloat16),
                 buffer(spec_shape.shape), pltpu.SemaphoreType.DMA((2 + QUART,))],
    )
    spec, far = sphere(spec, near, far, True, False, True)
    count = float(members * fields)
    part_rows = lat_rows // fields
    inverse_shape = jax.ShapeDtypeStruct((rows, 128), jnp.float32)
    logs, inverse, spec = call(
        bind(center_body, count, part_rows), (grid_shape, inverse_shape, spec_shape), arrive(spec), wave, name="center",
    )
    spec = sphere(spec, near, far, False, True, False)
    spec = call(bind(ratio_body, lat_rows), spec_shape, arrive(spec), field, inverse, wave, name="ratio")
    spec = sphere(spec, near, far, False, False, True)
    part_shape = jax.ShapeDtypeStruct(((members + 1) * part_rows, lon_total), jnp.float32)
    keep, send = call(
        bind(last_body, count, part_rows), (part_shape, part_shape), arrive(spec), logs, wave, name="last",
    )
    got = lax.ppermute(send, "field", [(0, 1), (1, 0)])
    barycenter, logs = call(bind(final_body, part_rows), (sum_shape, grid_shape), keep, got, name="final")
    return barycenter, logs.reshape(precip.shape)


def fits_packed(mesh, shape):
    lat_groups, fields = mesh.shape["lat"], mesh.shape["field"]
    devices = lat_groups * fields
    field_total, lat_total, lon_total = shape
    degrees = lon_total // 2
    members, lat_rows = field_total // fields, lat_total // lat_groups
    return (
        fields == 2
        and lon_total == 4 * lat_total // 2
        and lat_total == 512
        and 2 * members * lat_rows == 128
        and members == 2
        and lat_groups % 2 == 0
        and devices % QUART == 0
        and degrees % (8 * devices) == 0
        and (devices // 2) % 16 == 0
        and devices <= 128
    )


def on_device(mesh, precip):
    members, lat_rows, lon_total = precip.shape
    shape = (members * mesh.shape["field"], lat_rows * mesh.shape["lat"], lon_total)
    return on_device_packed(precip) if ITERS == 2 and fits_packed(mesh, shape) else on_device_plain(precip)


def solution(mesh):
    in_specs = (P("field", "lat", None),)
    out_specs = (P("lat", None), P("field", "lat", None))
    return jax.shard_map(
        lambda precip: on_device(mesh, precip),
        mesh=mesh, in_specs=in_specs, out_specs=out_specs, check_vma=False,
    )
```

```python
import math

import jax
import jax.numpy as jnp
import ml_dtypes
import numpy as np
from jax import lax
from jax.experimental import pallas as pl
from jax.experimental.pallas import tpu as pltpu
from jax.sharding import PartitionSpec as P

ITERS = 2


heat_rate = 2.0
floor_value = 0.1


def colatitudes(lat_total):
    index_rows = jnp.arange(lat_total, dtype=jnp.float32)
    return jnp.pi * (index_rows + 0.5) / lat_total


def quad_weights(lat_total, lon_total):
    polar_angle = colatitudes(lat_total)
    return jnp.sin(polar_angle) * (jnp.pi / lat_total) * (2.0 * jnp.pi / lon_total)


def heat_factors(degrees):
    level = jnp.arange(degrees, dtype=jnp.float32)
    return jnp.exp(-heat_rate * level * (level + 1.0) / (degrees * (degrees - 1.0)))


def legendre_north(orders, lat_total, degrees):
    half_rows = lat_total // 2
    polar_angle = colatitudes(lat_total)[:half_rows]
    cosine = jnp.cos(polar_angle)
    log_sine = jnp.log(jnp.sin(polar_angle))
    order_value = orders.astype(jnp.float32)
    step_count = jnp.arange(1, degrees + 1, dtype=jnp.float32)
    log_ratios = jnp.log((2.0 * step_count - 1.0) / (2.0 * step_count))
    within = step_count[None, :] <= order_value[:, None]
    partial_log = jnp.sum(jnp.where(within, log_ratios[None, :], 0.0), axis=1)
    log_start = 0.5 * jnp.log((2.0 * order_value + 1.0) / (4.0 * jnp.pi)) + 0.5 * partial_log
    start_log = log_start[:, None] + order_value[:, None] * log_sine[None, :]
    span_size = min(32, degrees)

    def advance(state, block_start):
        prev_one, prev_two, log_scale = state
        collected = []
        for offset in range(span_size):
            degree = (block_start + offset).astype(jnp.float32)
            safe_diff = jnp.maximum(degree * degree - order_value * order_value, 1.0)
            first_factor = jnp.sqrt((4.0 * degree * degree - 1.0) / safe_diff)
            numerator = (
                (2.0 * degree + 1.0) * (degree + order_value - 1.0) * (degree - order_value - 1.0)
            )
            denominator = jnp.maximum((2.0 * degree - 3.0) * safe_diff, 1.0)
            second_factor = jnp.sqrt(jnp.maximum(numerator, 0.0) / denominator)
            recurred = (
                first_factor[:, None] * cosine[None, :] * prev_one
                - second_factor[:, None] * prev_two
            )
            current = jnp.where(
                (degree > order_value)[:, None],
                recurred,
                jnp.where(
                    (degree == order_value)[:, None],
                    jnp.ones_like(recurred),
                    jnp.zeros_like(recurred),
                ),
            )
            collected.append(current * jnp.exp(log_scale))
            prev_two = prev_one
            prev_one = current
            if (offset + 1) % 8 == 0:
                magnitude = jnp.maximum(jnp.abs(prev_one), jnp.abs(prev_two))
                safe_size = jnp.where(magnitude > 0.0, magnitude, jnp.ones_like(magnitude))
                prev_one = prev_one / safe_size
                prev_two = prev_two / safe_size
                log_scale = log_scale + jnp.log(safe_size)
        return ((prev_one, prev_two, log_scale), jnp.stack(collected))

    empty_state = jnp.zeros((orders.shape[0], half_rows), jnp.float32)
    block_starts = jnp.arange(0, degrees, span_size, dtype=jnp.int32)
    final_state, stacked = lax.scan(advance, (empty_state, empty_state, start_log), block_starts)
    legendre = stacked.reshape(degrees, orders.shape[0], half_rows)
    return jnp.transpose(legendre, (1, 2, 0))


def fourier_tables(lon_total, degrees, groups):
    per_group = degrees // groups
    column = jnp.arange(2 * degrees, dtype=jnp.int32)
    group_index = column // (2 * per_group)
    within_group = column % (2 * per_group)
    part_index = within_group // per_group
    order_index = group_index * per_group + within_group % per_group
    points = jnp.arange(lon_total, dtype=jnp.int32)
    phase = (points[:, None] * order_index[None, :] % lon_total).astype(jnp.float32) * (
        2.0 * jnp.pi / lon_total
    )
    forward = jnp.where(part_index[None, :] == 0, jnp.cos(phase), -jnp.sin(phase))
    doubled = jnp.where(order_index == 0, 1.0, 2.0)
    backward = jnp.transpose(forward) * doubled[:, None]
    return (forward, backward)


def on_device_plain(precip):
    groups = lax.axis_size("lat")
    lat_index = lax.axis_index("lat")
    local_fields, lat_rows, lon_total = precip.shape
    lat_total = lat_rows * groups
    degrees = lon_total // 2
    orders_here = degrees // groups
    half_rows = lat_total // 2
    count_fields = local_fields * lax.axis_size("field")
    weights_all = quad_weights(lat_total, lon_total)
    local_weights = lax.dynamic_slice_in_dim(weights_all, lat_index * lat_rows, lat_rows)
    forward, backward = fourier_tables(lon_total, degrees, groups)
    heat_factor = heat_factors(degrees)
    orders = lat_index * orders_here + jnp.arange(orders_here, dtype=jnp.int32)
    north_table = legendre_north(orders, lat_total, degrees)
    paired = north_table.reshape(orders_here, half_rows, degrees // 2, 2)
    parity = (orders % 2 == 0)[:, None, None]
    even_table = jnp.where(parity, paired[..., 0], paired[..., 1])
    odd_table = jnp.where(parity, paired[..., 1], paired[..., 0])
    heat_paired = heat_factor.reshape(degrees // 2, 2)
    heat_even = jnp.where(parity[:, :, 0], heat_paired[None, :, 0], heat_paired[None, :, 1])
    heat_odd = jnp.where(parity[:, :, 0], heat_paired[None, :, 1], heat_paired[None, :, 0])
    weights_north = weights_all[:half_rows]

    def legendre_pass(spread):
        count_here = spread.shape[0]
        shaped = spread.reshape(count_here, lat_total, 2, orders_here)
        north_part = shaped[:, :half_rows]
        south_part = jnp.flip(shaped[:, half_rows:], axis=1)
        even_input = (north_part + south_part) * weights_north[None, :, None, None]
        odd_input = (north_part - south_part) * weights_north[None, :, None, None]
        even_coef = jnp.einsum(
            "mjk,fjpm->mfpk", even_table, even_input, precision=lax.Precision.HIGHEST
        )
        odd_coef = jnp.einsum(
            "mjk,fjpm->mfpk", odd_table, odd_input, precision=lax.Precision.HIGHEST
        )
        even_coef = even_coef * heat_even[:, None, None, :]
        odd_coef = odd_coef * heat_odd[:, None, None, :]
        even_sum = jnp.einsum(
            "mjk,mfpk->fjpm", even_table, even_coef, precision=lax.Precision.HIGHEST
        )
        odd_sum = jnp.einsum("mjk,mfpk->fjpm", odd_table, odd_coef, precision=lax.Precision.HIGHEST)
        result = jnp.concatenate([even_sum + odd_sum, jnp.flip(even_sum - odd_sum, axis=1)], axis=1)
        return result.reshape(count_here, lat_total, 2 * orders_here)

    def kernel_apply_step(fields):
        spectra = jnp.einsum("fjk,kc->fjc", fields, forward, precision=lax.Precision.HIGHEST)

        def one_member(carry, member_spectra):
            spread = lax.all_to_all(member_spectra, "lat", split_axis=1, concat_axis=0, tiled=True)
            filtered = legendre_pass(spread[None])
            returned = lax.all_to_all(filtered[0], "lat", split_axis=0, concat_axis=1, tiled=True)
            return (carry, returned)

        unused, gathered = lax.scan(one_member, jnp.zeros((), jnp.float32), spectra)
        return jnp.einsum("fjc,ck->fjk", gathered, backward, precision=lax.Precision.HIGHEST)

    partial_value = jnp.sum(precip * local_weights[None, :, None], axis=(1, 2))
    masses = lax.psum(partial_value, "lat") / (4.0 * jnp.pi)
    scaling_logs = jnp.zeros(precip.shape, jnp.float32)
    log_barycenter = jnp.zeros(precip.shape[1:], jnp.float32)
    scaled = precip / masses[:, None, None]
    ratio_field = scaled
    for sweep in range(ITERS):
        smoothed = kernel_apply_step(ratio_field)
        clamped_values = jnp.log(jnp.maximum(smoothed, floor_value))
        added_total = lax.psum(jnp.sum(scaling_logs + clamped_values, axis=0), "field")
        log_barycenter = added_total / count_fields
        scaling_logs = log_barycenter[None] - clamped_values
        if sweep + 1 < ITERS:
            blurred_scale = kernel_apply_step(jnp.exp(scaling_logs))
            ratio_field = scaled / jnp.maximum(blurred_scale, floor_value)
    return (jnp.exp(log_barycenter), scaling_logs)


QUART = 4


def split_pair(value):
    high = value.astype(jnp.bfloat16)
    low = (value - high.astype(jnp.float32)).astype(jnp.bfloat16)
    return high, low


def pair_rows(value):
    high, low = split_pair(value)
    return jnp.concatenate([high, low], axis=0)


def dot_nt(left, right):
    return lax.dot_general(left, right, (((1,), (1,)), ((), ())), preferred_element_type=jnp.float32)


def dot_nn(left, right):
    return lax.dot_general(left, right, (((1,), (0,)), ((), ())), preferred_element_type=jnp.float32)


def wave_tables(lon_total, devices, slots):
    span = lon_total // QUART
    residue = np.arange(QUART)[:, None, None]
    order = residue + QUART * np.arange(devices // QUART)[None, :, None]
    order = (order + devices * np.arange(slots)[None, None, :]).reshape(QUART, -1)
    phase = (order[:, :, None] * np.arange(span)[None, None, :] % lon_total) * (2.0 * np.pi / lon_total)
    table = np.concatenate([np.cos(phase), np.sin(phase)], axis=1).astype(np.float32)
    high = table.astype(ml_dtypes.bfloat16)
    low = (table - high.astype(np.float32)).astype(ml_dtypes.bfloat16)
    return np.stack([high, low])


def wave_seeds(lon_total, devices, slots):
    span = lon_total // QUART
    first = (np.arange(QUART)[:, None] + QUART * np.arange(devices // QUART)[None, :]).reshape(-1)
    phases = [
        orders[:, None] * np.arange(span)[None, :] % lon_total * (2.0 * np.pi / lon_total)
        for orders in (first, devices * np.arange(slots))
    ]
    return np.concatenate([f(p) for p in phases for f in (np.cos, np.sin)]).astype(np.float32)


def grow_waves(seed_ref, wave_ref, devices, slots):
    orders = wave_ref.shape[2] // 2
    step_cos = seed_ref[2 * devices : 2 * devices + slots, :]
    step_sin = seed_ref[2 * devices + slots : 2 * devices + 2 * slots, :]
    for row in range(devices):
        residue, at = row // (devices // QUART), row % (devices // QUART) * slots
        cosine, sine = seed_ref[row : row + 1, :], seed_ref[devices + row : devices + row + 1, :]
        for place, value in (
            (at, cosine * step_cos - sine * step_sin),
            (orders + at, sine * step_cos + cosine * step_sin),
        ):
            high, low = split_pair(value)
            wave_ref[0, residue, place : place + slots, :] = high
            wave_ref[1, residue, place : place + slots, :] = low


def forward_waves(field, wave_ref, out_ref, done=None):
    span = field.shape[1] // QUART
    rows = field.shape[0]
    lanes = 2 * rows
    part = [field[:, q * span : (q + 1) * span] for q in range(QUART)]
    sum_even, sum_odd = part[0] + part[2], part[1] + part[3]
    diff_even, diff_odd = part[0] - part[2], part[1] - part[3]
    stack_even = pair_rows(jnp.concatenate([sum_even + sum_odd, sum_even - sum_odd], axis=0))
    stack_odd = pair_rows(jnp.concatenate([diff_even, diff_odd], axis=0))
    orders = wave_ref.shape[2] // 2
    first = lax.broadcasted_iota(jnp.int32, (orders, lanes), 1) < rows
    for residue in range(QUART):
        stack = stack_odd if residue % 2 else stack_even
        found = dot_nt(wave_ref[0, residue], stack) + dot_nt(wave_ref[1, residue], stack)
        found = found[:, :lanes] + found[:, lanes:]
        cosine, sine = found[:orders], found[orders:]
        if residue == 0:
            packed = jnp.where(first, cosine, -pltpu.roll(sine, rows, 1))
        elif residue == 2:
            packed = jnp.where(first, pltpu.roll(cosine, rows, 1), -sine)
        elif residue == 1:
            packed = jnp.where(first, cosine, -cosine) - pltpu.roll(sine, rows, 1)
        else:
            turned = pltpu.roll(sine, rows, 1)
            packed = cosine + jnp.where(first, turned, -turned)
        out_ref[:, residue] = packed.reshape(out_ref.shape[0], out_ref.shape[2], lanes)
        if done:
            done[residue].start()


def inverse_waves(spec_ref, wave_ref):
    outer, _, slots, lanes = spec_ref.shape
    rows = lanes // 2
    real = [None] * QUART
    cross = {}
    spare = None
    for residue in range(QUART):
        turned = jnp.transpose(spec_ref[:, residue].reshape(outer * slots, lanes))
        cosine, sine = turned[:rows], turned[rows:]
        if residue == 0:
            spare = sine[:, 0:1]
        left = jnp.concatenate([cosine, -sine], axis=1)
        if residue % 2:
            left = jnp.concatenate([left, jnp.concatenate([sine, cosine], axis=1)], axis=0)
        count = left.shape[0]
        left = pair_rows(left)
        found = dot_nn(left, wave_ref[0, residue]) + dot_nn(left, wave_ref[1, residue])
        found = found[:count] + found[count:]
        real[residue] = found[:rows]
        if residue % 2:
            cross[residue] = found[rows:]
    plus, minus = real[0] + real[2], real[0] - real[2]
    both, gap = real[1] + real[3], cross[1] - cross[3]
    return jnp.concatenate([plus + both, minus - gap, plus - both, minus + gap], axis=1), spare


def flip_rows(value, south, lat_rows):
    lanes = 128
    rows, width = value.shape
    sub = lax.broadcasted_iota(jnp.int32, (8, lanes), 0)
    source = jnp.where(south, 7 - sub, sub)
    blocks = lat_rows // 8
    out = []
    for base in range(0, rows, lat_rows):
        for block in range(blocks):
            near = value[base + 8 * block : base + 8 * block + 8]
            far = value[base + 8 * (blocks - 1 - block) : base + 8 * (blocks - block)]
            tile = jnp.where(south, far, near)
            pieces = [
                jnp.take_along_axis(tile[:, at : at + lanes], source, axis=0) for at in range(0, width, lanes)
            ]
            out.append(jnp.concatenate(pieces, axis=1))
    return jnp.concatenate(out, axis=0)


def device_index():
    return lax.axis_index("lat") * lax.axis_size("field") + lax.axis_index("field")


def in_south():
    return lax.axis_index("lat") >= lax.axis_size("lat") // 2


def first_body(lat_rows, devices, slots, field_hbm, seed_hbm, flipped_hbm, out_hbm, field_ref, seed_ref, wave_ref,
               flipped_ref, out_ref, sems):
    get_field = pltpu.make_async_copy(field_hbm, field_ref, sems.at[0])
    get_seed = pltpu.make_async_copy(seed_hbm, seed_ref, sems.at[1])
    put_flipped = pltpu.make_async_copy(flipped_ref, flipped_hbm, sems.at[2])
    put_wave = [
        pltpu.make_async_copy(out_ref.at[:, r], out_hbm.at[:, r], sems.at[3 + r]) for r in range(QUART)
    ]
    get_seed.start()
    get_field.start()
    get_seed.wait()
    grow_waves(seed_ref, wave_ref, devices, slots)
    get_field.wait()
    flipped_ref[...] = flip_rows(field_ref[...], in_south(), lat_rows) * 2.0**-8
    put_flipped.start()
    forward_waves(flipped_ref[...], wave_ref, out_ref, put_wave)
    put_flipped.wait()
    for copy in put_wave:
        copy.wait()


def member_sum(value, lat_rows):
    total = value[:lat_rows]
    for member in range(1, value.shape[0] // lat_rows):
        total = total + value[member * lat_rows : (member + 1) * lat_rows]
    return total


def core_select(core, first, second):
    return jnp.where(core == 0, first, second), jnp.where(core == 0, second, first)


def center_body(count, part_rows, spec_ref, wave_ref, logs_ref, inverse_ref, out_ref):
    blurred, total = inverse_waves(spec_ref, wave_ref)
    inverse = (4.0 * math.pi) / total
    clamped = jnp.log(jnp.maximum(blurred * inverse, floor_value))
    center = member_sum(clamped, part_rows) / count
    logs = jnp.concatenate([center] * (clamped.shape[0] // part_rows), axis=0) - clamped
    logs_ref[...] = logs
    forward_waves(jnp.exp(logs), wave_ref, out_ref)
    half = inverse.shape[0] // 2
    own, _ = core_select(lax.axis_index("field"), inverse[:half], inverse[half:])
    parts = [own[at : at + part_rows] for at in range(0, half, part_rows)]
    inverse_ref[...] = jnp.broadcast_to(jnp.concatenate([p for p in parts for _ in range(2)], axis=0), inverse_ref.shape)


def ratio_body(spec_ref, field_ref, inverse_ref, wave_ref, out_ref):
    blurred, _ = inverse_waves(spec_ref, wave_ref)
    scaled = field_ref[...] * inverse_ref[:, 0:1]
    forward_waves(scaled / jnp.maximum(blurred, floor_value), wave_ref, out_ref)


def last_body(count, part_rows, spec_ref, logs_ref, wave_ref, keep_ref, send_ref):
    blurred, _ = inverse_waves(spec_ref, wave_ref)
    clamped = jnp.log(jnp.maximum(blurred, floor_value))
    center = member_sum(logs_ref[...] + clamped, part_rows) / count
    logs = jnp.concatenate([center] * (clamped.shape[0] // part_rows), axis=0) - clamped
    half = logs.shape[0] // 2
    own, other = core_select(lax.axis_index("field"), logs[:half], logs[half:])
    keep_ref[...] = jnp.concatenate([own, center], axis=0)
    send_ref[...] = jnp.concatenate([other, center], axis=0)


def final_body(part_rows, keep_ref, got_ref, center_ref, logs_ref):
    low, high = core_select(lax.axis_index("field"), keep_ref[...], got_ref[...])
    pieces = []
    for at in range(0, low.shape[0], part_rows):
        pieces += [low[at : at + part_rows], high[at : at + part_rows]]
    whole = flip_rows(jnp.concatenate(pieces, axis=0), in_south(), 2 * part_rows)
    rows = logs_ref.shape[0]
    logs_ref[...] = whole[:rows]
    center_ref[...] = jnp.exp(whole[rows:])


def table_rows(degrees, devices, slot):
    return (degrees - devices * slot) // 2


def table_offset(degrees, devices, slot, parity):
    start = sum(2 * table_rows(degrees, devices, s) for s in range(slot))
    return start + parity * table_rows(degrees, devices, slot)


FAR_SLOTS = 2


def table_part(degrees, devices, slot, parity, near_ref, far_ref):
    count = table_rows(degrees, devices, slot)
    offset = table_offset(degrees, devices, slot, parity)
    if slot < FAR_SLOTS:
        return far_ref, offset, count
    return near_ref, offset - table_offset(degrees, devices, FAR_SLOTS, 0), count


def move_far(degrees, devices, slot, src_ref, dst_ref, sems):
    part = (slice(None), pl.ds(table_offset(degrees, devices, slot, 0), 2 * table_rows(degrees, devices, slot)))
    return pltpu.make_async_copy(src_ref.at[part], dst_ref.at[part], sems.at[slot])


def legendre_body(degrees, devices, slots, fixed_hbm, near_ref, far_hbm, weight_ref, fixed_ref, first_coef,
                  second_coef, left_half, right_half, far_ref, sem, far_sems):
    copy = pltpu.make_async_copy(fixed_hbm, fixed_ref, sem)
    copy.start()
    half = (left_half, right_half)
    lanes = 128
    device = device_index()
    order = lax.broadcasted_iota(jnp.int32, (slots, degrees), 0) * devices + device
    level = lax.broadcasted_iota(jnp.int32, (slots, degrees), 1)
    above = level > order
    order, level = order.astype(jnp.float32), level.astype(jnp.float32)
    diff = jnp.maximum(level * level - order * order, 1.0)
    rate = 0.5 * heat_rate / (degrees * (degrees - 1.0))
    first_ratio = jnp.exp(-rate * (2.0 * level))
    second_ratio = jnp.exp(-rate * (4.0 * level - 2.0))
    first_coef[...] = jnp.where(above, jnp.sqrt((4.0 * level * level - 1.0) / diff) * first_ratio, 0.0)
    numer = (2.0 * level + 1.0) * (level + order - 1.0) * (level - order - 1.0)
    denom = jnp.maximum((2.0 * level - 3.0) * diff, 1.0)
    second_coef[...] = jnp.where(above, jnp.sqrt(jnp.maximum(numer, 0.0) / denom) * second_ratio, 0.0)
    copy.wait()

    lane = lax.broadcasted_iota(jnp.int32, (slots, lanes), 1)
    start = jnp.sum(jnp.where(lane == device, fixed_ref[0:slots, 0:lanes], 0.0), axis=1, keepdims=True)
    sub = lax.broadcasted_iota(jnp.int32, (8, lanes), 0)
    tiles = slots // 8
    cosine = [jnp.broadcast_to(fixed_ref[slots : slots + 1, h * lanes : (h + 1) * lanes], (8, lanes)) for h in range(2)]
    log_sine = [jnp.broadcast_to(fixed_ref[slots + 1 : slots + 2, h * lanes : (h + 1) * lanes], (8, lanes)) for h in range(2)]
    order_tile = [(sub + 8 * t) * devices + device for t in range(tiles)]
    zero = jnp.zeros((8, lanes), jnp.float32)
    span_log = 60.0 * math.log(2.0)

    def fresh(tile):
        state = []
        for h in range(2):
            scale_log = start[8 * tile : 8 * tile + 8] + order_tile[tile].astype(jnp.float32) * log_sine[h]
            state.append((zero, zero, scale_log, jnp.exp(scale_log)))
        return state

    def chunk(index, states):
        active = len(states)
        base = pl.multiple_of(index * lanes, lanes)
        first = [first_coef[8 * t : 8 * t + 8, pl.ds(base, lanes)] for t in range(active)]
        second = [second_coef[8 * t : 8 * t + 8, pl.ds(base, lanes)] for t in range(active)]
        states = [list(s) for s in states]
        for k in range(lanes):
            degree = base + k
            for t in range(active):
                a = jnp.broadcast_to(first[t][:, k : k + 1], (8, lanes))
                b = jnp.broadcast_to(second[t][:, k : k + 1], (8, lanes))
                begin = jnp.where(order_tile[t] == degree, 1.0, 0.0)
                for h in range(2):
                    one, two, scale_log, scale = states[t][h]
                    now = (a * cosine[h]) * one + (begin - b * two)
                    half[h][pl.ds(degree * slots + 8 * t, 8), :] = now * scale
                    two, one = one, now
                    if (k + 1) % 8 == 0:
                        large = jnp.maximum(jnp.abs(one), jnp.abs(two)) > 2.0**30
                        factor = jnp.where(large, 2.0**-60, 1.0)
                        one, two = one * factor, two * factor
                        scale_log = scale_log + jnp.where(large, span_log, 0.0)
                        scale = jnp.exp(scale_log)
                    states[t][h] = (one, two, scale_log, scale)
        return states

    states = []
    chunks = degrees // lanes
    for index in range(chunks):
        while len(states) < tiles and 8 * len(states) * devices < (index + 1) * lanes:
            states.append(fresh(len(states)))
        states = chunk(index, states)

    weight_ref[...] = fixed_ref[slots + 2 : slots + 3, :]
    for slot in range(slots):
        for parity in range(2):
            part_ref, offset, count = table_part(degrees, devices, slot, parity, near_ref, far_ref)
            begin = (devices * slot + parity) * slots + slot
            for h in range(2):
                high, low = split_pair(half[h][pl.ds(begin, count, stride=2 * slots), :])
                part_ref[0, offset : offset + count, h * lanes : (h + 1) * lanes] = high
                part_ref[1, offset : offset + count, h * lanes : (h + 1) * lanes] = low
        if slot < FAR_SLOTS:
            move_far(degrees, devices, slot, far_ref, far_hbm, far_sems).start()
    for slot in range(FAR_SLOTS):
        move_far(degrees, devices, slot, far_ref, far_hbm, far_sems).wait()


def weave(first, second, width):
    lanes = first.shape[-1]
    even = lax.broadcasted_iota(jnp.int32, first.shape, first.ndim - 1) // width % 2 == 0
    axis = first.ndim - 1
    return (
        jnp.where(even, first, pltpu.roll(second, width, axis)),
        jnp.where(even, pltpu.roll(first, lanes - width, axis), second),
    )


def gather_orders(spec_ref, sign, fields, lat_groups, lat_rows, members, slots, halved, even_in, odd_in):
    group_lanes = 128 // lat_rows
    for h in range(2):
        even, odd = [], []
        for q in range(group_lanes):
            lat = h * group_lanes + q
            pair = ([], [])
            for source in range(fields):
                north = spec_ref[lat * fields + source]
                south = spec_ref[(lat_groups - 1 - lat) * fields + source] * sign
                pair[0].append(north + south)
                pair[1].append(north - south)
            if halved:
                pair = [weave(*p, lat_rows // 2) for p in pair]
            even.append(pair[0])
            odd.append(pair[1])
        for field in range(fields):
            for c in range(2 * members):
                row = (field * 2 * members + c) * slots
                part, member = c // members, c % members
                block, at = (member, part * fields + field) if halved else (field, c)
                cut = slice(at * lat_rows, (at + 1) * lat_rows)
                even_in[h][row : row + slots, :] = jnp.concatenate([e[block][:, cut] for e in even], axis=1)
                odd_in[h][row : row + slots, :] = jnp.concatenate([o[block][:, cut] for o in odd], axis=1)


def scatter_orders(out_ref, fields, lat_groups, lat_rows, members, slots, halved, north, south):
    group_lanes = 128 // lat_rows
    for lat in range(lat_groups // 2):
        h, q = lat // group_lanes, lat % group_lanes
        cut = slice(q * lat_rows, (q + 1) * lat_rows)
        for source, place in ((north, lat), (south, lat_groups - 1 - lat)):
            blocks = []
            for block in range(2):
                if halved:
                    owners = [(field, part, block) for part in range(2) for field in range(fields)]
                else:
                    owners = [(block, part, member) for part in range(2) for member in range(members)]
                rows = [((field * 2 + part) * members + member) * slots for field, part, member in owners]
                blocks.append(jnp.concatenate([source[h][row : row + slots, cut] for row in rows], axis=1))
            if halved:
                blocks = weave(*blocks, lat_rows // 2)
            out_ref[place * fields], out_ref[place * fields + 1] = blocks


def sphere_body(degrees, devices, slots, lat_groups, lat_rows, members, with_mass, halves_in, halves_out, spec_ref, near_ref, far_in,
                weight_ref, out_ref, *rest):
    far_ref, rest = (rest[0], rest[1:]) if with_mass else (far_in, rest)
    coef_ref, far_sem = rest[:2]
    halves = rest[2:]
    if with_mass:
        get_far = pltpu.make_async_copy(far_in, far_ref, far_sem)
        get_far.start()
    even_in, odd_in, north_out, south_out = halves[0:2], halves[2:4], halves[4:6], halves[6:8]
    device = device_index()
    sign = jnp.where(device % 2 == 0, 1.0, -1.0)
    fields = devices // lat_groups
    per_field = 2 * members
    columns = fields * per_field
    gather_orders(spec_ref, sign, fields, lat_groups, lat_rows, members, slots, halves_in, even_in, odd_in)
    mass = None

    def pick(slot, parity):
        picked = pl.ds(slot, columns, stride=slots)
        gain = 2.0 if slot else jnp.where(device == 0, 1.0, 2.0)
        pair = (even_in, odd_in)[parity]
        values = jnp.concatenate([pair[0][picked, :], pair[1][picked, :]], axis=1)
        return values * (weight_ref[...] * gain)

    def table(slot, parity):
        part_ref, offset, count = table_part(degrees, devices, slot, parity, near_ref, far_ref)
        return part_ref[0, offset : offset + count, :], part_ref[1, offset : offset + count, :], count

    if with_mass:
        mass = jnp.sum(pick(0, 0), axis=1, keepdims=True)

    def analyse(slot):
        for parity in range(2):
            high, low, count = table(slot, parity)
            packed = pair_rows(pick(slot, parity))
            coef = dot_nt(packed, high) + dot_nt(packed, low)
            coef_ref[2 * slot + parity, :, 0:count] = pair_rows(coef[:columns] + coef[columns:])

    def synthesise(slot):
        found = []
        for parity in range(2):
            high, low, count = table(slot, parity)
            packed = coef_ref[2 * slot + parity, :, 0:count]
            back = dot_nn(packed, high) + dot_nn(packed, low)
            found.append(back[:columns] + back[columns:])
        north, south = found[0] + found[1], (found[0] - found[1]) * sign
        if with_mass and slot == 0:
            spread = jnp.broadcast_to(mass, north.shape)
            spread = pltpu.roll(spread, members, 0)
            which = lax.broadcasted_iota(jnp.int32, north.shape, 0) % per_field
            spare = (which >= members) & (device == 0)
            north, south = jnp.where(spare, spread, north), jnp.where(spare, spread, south)
        picked = pl.ds(slot, columns, stride=slots)
        for h in range(2):
            north_out[h][picked, :] = north[:, 128 * h : 128 * h + 128]
            south_out[h][picked, :] = south[:, 128 * h : 128 * h + 128]

    near_slots, far_slots = range(FAR_SLOTS, slots), range(FAR_SLOTS)
    early = slots if with_mass else FAR_SLOTS
    for slot in near_slots:
        analyse(slot)
    for slot in range(FAR_SLOTS, early):
        synthesise(slot)
    if with_mass:
        get_far.wait()
    for slot in far_slots:
        analyse(slot)
    for slot in list(range(early, slots)) + list(far_slots):
        synthesise(slot)

    scatter_orders(out_ref, fields, lat_groups, lat_rows, members, slots, halves_out, north_out, south_out)


def on_device_packed(precip):
    lat_groups, fields = lax.axis_size("lat"), lax.axis_size("field")
    devices = lat_groups * fields
    members, lat_rows, lon_total = precip.shape
    lat_total, degrees = lat_rows * lat_groups, lon_total // 2
    slots = degrees // devices
    rows = members * lat_rows
    polar = np.pi * (np.arange(lat_total // 2) + 0.5) / lat_total
    level = np.arange(degrees)
    step = np.arange(1, degrees)
    starts = np.concatenate([[0.0], np.cumsum(np.log((2.0 * step - 1.0) / (2.0 * step)))])
    starts = 0.5 * np.log((2.0 * level + 1.0) / (4.0 * np.pi)) + 0.5 * starts
    starts = starts - 0.5 * heat_rate * level * (level + 1.0) / (degrees * (degrees - 1.0))
    fixed = np.zeros((slots + 8, lat_total // 2), np.float32)
    fixed[:slots, :devices] = starts.reshape(slots, devices)
    fixed[slots] = np.cos(polar)
    fixed[slots + 1] = np.log(np.sin(polar))
    fixed[slots + 2] = np.sin(polar) * (np.pi / lat_total) * (2.0 * np.pi / lon_total)
    fixed = jnp.asarray(fixed)
    wave = jnp.asarray(wave_tables(lon_total, devices, slots))

    vmem = pl.BlockSpec(memory_space=pltpu.VMEM)
    outer = devices // QUART
    spec_shape = jax.ShapeDtypeStruct((outer, QUART, slots, 2 * rows), jnp.float32)
    grid_shape = jax.ShapeDtypeStruct((rows, lon_total), jnp.float32)
    sum_shape = jax.ShapeDtypeStruct((lat_rows, lon_total), jnp.float32)
    far_rows = table_offset(degrees, devices, FAR_SLOTS, 0)
    near_rows = table_offset(degrees, devices, slots, 0) - far_rows
    near_shape = jax.ShapeDtypeStruct((2, near_rows, lat_total // 2), jnp.bfloat16)
    far_shape = jax.ShapeDtypeStruct((2, far_rows, lat_total // 2), jnp.bfloat16)
    flat_shape = jax.ShapeDtypeStruct((devices, slots, 2 * rows), jnp.float32)
    hbm = pl.BlockSpec(memory_space=pl.ANY)

    def call(body, shapes, *operands, name, far=(), far_out=(), scratch=(), cost=None, limit=8):
        single = not isinstance(shapes, tuple)
        shapes = (shapes,) if single else shapes
        outs = [hbm if index in far_out else vmem for index in range(len(shapes))]
        shapes = [
            pltpu.HBM(shape.shape, shape.dtype) if index in far_out else shape for index, shape in enumerate(shapes)
        ]
        specs = [hbm if any(o is f for f in far) else vmem for o in operands]
        operands = [
            pltpu.with_memory_space_constraint(o, pltpu.HBM) if any(o is f for f in far) else o for o in operands
        ]
        return pl.pallas_call(
            body,
            out_shape=shapes[0] if single else shapes,
            in_specs=specs,
            out_specs=outs[0] if single else outs,
            scratch_shapes=list(scratch),
            cost_estimate=cost,
            compiler_params=pltpu.CompilerParams(vmem_limit_bytes=limit << 20),
            name=name,
        )(*operands)

    def exchange(spec):
        flat = spec.reshape(devices, slots, 2 * rows)
        return lax.all_to_all(flat, ("lat", "field"), split_axis=0, concat_axis=0, tiled=True)

    def bind(body, *bound):
        return lambda *refs: body(*bound, *refs)

    def buffer(shape, dtype=jnp.float32):
        return pltpu.VMEM(shape, dtype)

    columns = fields * 2 * members
    signal = pltpu.SemaphoreType.DMA(())

    def sphere(spec, near, far, with_mass, halves_in, halves_out):
        return call(
            bind(sphere_body, degrees, devices, slots, lat_groups, lat_rows, members, with_mass, halves_in,
                 halves_out),
            (flat_shape, far_shape) if with_mass else flat_shape,
            exchange(spec), near, far, weight, far=(far,) if with_mass else (), name="sphere",
            limit=8,
            scratch=[buffer((2 * slots, 2 * columns, 256), jnp.bfloat16), signal]
            + [buffer((columns * slots + slots, 128))] * 8,
        )

    def arrive(spec):
        return exchange(spec).reshape(spec_shape.shape)

    weight_shape = jax.ShapeDtypeStruct((1, lat_total // 2), jnp.float32)
    near, far, weight = call(
        bind(legendre_body, degrees, devices, slots), (near_shape, far_shape, weight_shape), fixed, far=(fixed,), far_out=(1,),
        scratch=[buffer(fixed.shape)] + [buffer((slots, degrees))] * 2 + [buffer((degrees * slots + 2 * slots, 128))] * 2
        + [buffer(far_shape.shape, jnp.bfloat16), signal, pltpu.SemaphoreType.DMA((FAR_SLOTS,))],
        cost=pl.CostEstimate(flops=40_000_000, bytes_accessed=16 << 20, transcendentals=0),
        name="legendre", limit=12,
    )
    field = precip.reshape(rows, lon_total)
    seed = jnp.asarray(wave_seeds(lon_total, devices, slots))
    flipped, spec = call(
        bind(first_body, lat_rows, devices, slots), (grid_shape, spec_shape), field, seed, far=(field, seed),
        far_out=(0, 1), name="first",
        scratch=[buffer((rows, lon_total)), buffer(seed.shape), buffer(wave.shape, jnp.bfloat16),
                 buffer((rows, lon_total)), buffer(spec_shape.shape), pltpu.SemaphoreType.DMA((3 + QUART,))],
    )
    spec, far = sphere(spec, near, far, True, False, True)
    count = float(members * fields)
    part_rows = lat_rows // fields
    inverse_shape = jax.ShapeDtypeStruct((rows, 128), jnp.float32)
    logs, inverse, spec = call(
        bind(center_body, count, part_rows), (grid_shape, inverse_shape, spec_shape), arrive(spec), wave, name="center",
    )
    spec = sphere(spec, near, far, False, True, False)
    spec = call(ratio_body, spec_shape, arrive(spec), flipped, inverse, wave, name="ratio")
    spec = sphere(spec, near, far, False, False, True)
    part_shape = jax.ShapeDtypeStruct(((members + 1) * part_rows, lon_total), jnp.float32)
    keep, send = call(
        bind(last_body, count, part_rows), (part_shape, part_shape), arrive(spec), logs, wave, name="last",
    )
    got = lax.ppermute(send, "field", [(0, 1), (1, 0)])
    barycenter, logs = call(bind(final_body, part_rows), (sum_shape, grid_shape), keep, got, name="final")
    return barycenter, logs.reshape(precip.shape)


def fits_packed(mesh, shape):
    lat_groups, fields = mesh.shape["lat"], mesh.shape["field"]
    devices = lat_groups * fields
    field_total, lat_total, lon_total = shape
    degrees = lon_total // 2
    members, lat_rows = field_total // fields, lat_total // lat_groups
    return (
        fields == 2
        and lon_total == 4 * lat_total // 2
        and lat_total == 512
        and 2 * members * lat_rows == 128
        and members == 2
        and lat_groups % 2 == 0
        and devices % QUART == 0
        and degrees % (8 * devices) == 0
        and (devices // 2) % 16 == 0
        and devices <= 128
    )


def on_device(mesh, precip):
    members, lat_rows, lon_total = precip.shape
    shape = (members * mesh.shape["field"], lat_rows * mesh.shape["lat"], lon_total)
    return on_device_packed(precip) if ITERS == 2 and fits_packed(mesh, shape) else on_device_plain(precip)


def solution(mesh):
    in_specs = (P("field", "lat", None),)
    out_specs = (P("lat", None), P("field", "lat", None))
    return jax.shard_map(
        lambda precip: on_device(mesh, precip),
        mesh=mesh, in_specs=in_specs, out_specs=out_specs, check_vma=False,
    )
```
